32 devices in a mesh: groups: 2 (over y), stripe: 8 (over z, x), exp: 2 (over core).
Axes of the slice: x: 2, y: 2, z: 4, core: 2. Of those that a mesh axis runs over, the one named last changes fastest.
Arguments:
- template: float32 [256, 2048], P(('groups', 'stripe'), 'exp'), parts along dimension 0, may hold values from -6 to 6
- exposure: float32 [4, 128, 2048], P(('groups', 'exp'), 'stripe'), parts along dimension 0, may hold values from -30 to 30
- cosmic_mask: int32 [4, 128, 2048], P(('groups', 'exp'), 'stripe'), parts along dimension 0, may hold values 0 or 1
- stamp_blocks: int32 [16, 16], P(('groups', 'stripe')), parts along dimension 0, may hold values from 0 to 31, as said below
- row_filters: float32 [19, 19], replicated, may hold values from -1 to 2.5
- col_filters: float32 [19, 19], replicated, may hold values from -1 to 2.5
Outputs:
- filtered: float32 [4, 128, 2048], P(('groups', 'exp'), 'stripe'), parts along dimension 0
- coefficients: float32 [4, 64], P(('groups', 'exp')), parts along dimension 0
The draws below stay inside these ranges and needn't reach their ends.
There are 2 independent parts, one for each index of `groups`. The reference program is written for one: setup_inputs(seed, part) draws one part's arguments, and reference() takes and returns one part's arrays. A program takes and returns all parts, laid end to end along the dimension named above; an argument that names none is the same for every part. Nothing has to cross between parts.
Inputs may be any that keep to these rules, and one draw needn't show every extreme that they name: `stamp_blocks`: each row lists the stamps of one stripe; stamp j lies in column block 2 j or 2 j + 1.
All inputs are finite; a program needn't handle non-finite values. No bound on the sum of `cosmic_mask` on one device may be relied on, other than what follows from the above.
Results may differ from the reference program's by a relative error of at most 0.0003.
Values sent between devices are 32-bit elements; how exact they have to be, the bound alone decides.
A program may use at most 64 MiB of HBM per device.

```python
import math
import jax
import jax.numpy as jnp
from jax import lax

ROWS_DEV = 16
COLS = 2048
HALF = 9
BASES = 19
STAMP_W = 64
TAPS = 19
NCOL = 64
NSTAMP = 16
STRIPES = 8
NR = 128
NEXP = 2


def sky_field(key):
    return jnp.clip(jax.random.normal(jax.random.fold_in(key, 101), (NR, COLS), jnp.float32), -5.0, 5.0)


def draw_template(key, part):
    sky = sky_field(key)
    extra = jnp.clip(jax.random.normal(jax.random.fold_in(key, 103), (NR, COLS), jnp.float32), -5.0, 5.0)
    return sky + 0.1 * extra


def blur_axis(field, near, far, axis_id):
    centre = 1.0 - 2.0 * near - 2.0 * far
    result = centre * field + near * (jnp.roll(field, 1, axis_id) + jnp.roll(field, -1, axis_id))
    return result + far * (jnp.roll(field, 2, axis_id) + jnp.roll(field, -2, axis_id))


def draw_exposure(key, part):
    sky = sky_field(key)
    row_pos = (2.0 * jnp.arange(NR, dtype=jnp.float32) + 1.0) / NR - 1.0
    col_pos = (2.0 * jnp.arange(COLS, dtype=jnp.float32) + 1.0) / COLS - 1.0
    amplitude = (1.3 + row_pos + 0.8 * row_pos * row_pos)[:, None] * (1.0 + 0.4 * jnp.cos(3.0 * math.pi * col_pos))[None, :]
    frames = []
    for frame in range(NEXP):
        frame_key = jax.random.fold_in(key, 200 + frame)
        params = jax.random.uniform(frame_key, (5,), jnp.float32)
        blurred = blur_axis(sky, 0.15 + 0.15 * params[0], 0.02 + 0.08 * params[1], 0)
        blurred = blur_axis(blurred, 0.15 + 0.15 * params[2], 0.02 + 0.08 * params[3], 1)
        jitter = 0.3 * jnp.clip(jax.random.normal(jax.random.fold_in(frame_key, 7), (NR, COLS), jnp.float32), -5.0, 5.0)
        offset_level = 0.5 * params[4] + 0.4 * col_pos[None, :] + 0.3 * row_pos[:, None] * col_pos[None, :]
        frames.append(amplitude * blurred + offset_level + jitter)
    return jnp.stack(frames)


def filter_bank(key, salt):
    taps_pos = jnp.arange(TAPS, dtype=jnp.float32) - HALF
    sigma = jnp.exp(jax.random.uniform(jax.random.fold_in(key, salt), (BASES, 1), jnp.float32, math.log(0.6), math.log(3.5)))
    profile = jnp.exp(-taps_pos[None, :] ** 2 / (2.0 * sigma * sigma)) / (2.5 * sigma)
    first = jnp.clip(jax.random.normal(jax.random.fold_in(key, salt + 1), (BASES, TAPS), jnp.float32), -4.0, 4.0)
    second = jnp.clip(jax.random.normal(jax.random.fold_in(key, salt + 2), (BASES, TAPS), jnp.float32), -4.0, 4.0)
    return profile * (1.0 + 0.3 * first) + 0.12 * second


def draw_row_filters(key, part):
    return filter_bank(key, 301)


def draw_col_filters(key, part):
    return filter_bank(key, 311)


def draw_stamp_blocks(key, part):
    choose = jax.random.randint(jax.random.fold_in(key, 401), (STRIPES, NSTAMP), 0, 2)
    row_id = jnp.arange(STRIPES, dtype=jnp.int32)[:, None]
    slot_id = jnp.arange(NSTAMP, dtype=jnp.int32)[None, :]
    choose = jnp.where((row_id == 0) & (slot_id == 0), 0, choose)
    choose = jnp.where((row_id == 0) & (slot_id == NSTAMP - 1), 1, choose)
    return (2 * slot_id + choose).astype(jnp.int32)


def touch_ends(drawn, own_key, least, largest):
    longest = drawn.shape.index(max(drawn.shape))
    spots = []
    for shift in (0, 1):
        where = [jax.random.randint(jax.random.fold_in(own_key, axis), (), 0, length) for axis, length in enumerate(drawn.shape)]
        where[longest] = (where[longest] + shift) % drawn.shape[longest]
        spots.append(tuple(where))
    return drawn.at[spots[0]].set(least).at[spots[1]].set(largest)


def setup_inputs(seed: int = 0, part: int = 0) -> dict:
    key_of = jax.random.split(jax.random.key(seed), 7)
    own_keys = jax.random.split(jax.random.fold_in(key_of[6], part), 7)
    return {
        "template": draw_template(jax.random.fold_in(jax.random.fold_in(key_of[6], part), 71), part),
        "exposure": draw_exposure(jax.random.fold_in(jax.random.fold_in(key_of[6], part), 71), part),
        "cosmic_mask": touch_ends((jax.random.randint(own_keys[2], (NEXP, NR, COLS), 0, 32) < 31).astype(jnp.int32), jax.random.fold_in(own_keys[2], 1), 0, 1),
        "stamp_blocks": draw_stamp_blocks(jax.random.fold_in(jax.random.fold_in(key_of[6], part), 71), part),
        "row_filters": draw_row_filters(jax.random.fold_in(key_of[6], 71), part),
        "col_filters": draw_col_filters(jax.random.fold_in(key_of[6], 71), part),
    }


def stripe_bases(extended, row_filters, col_filters):
    row_span = extended.shape[0] - 2 * HALF
    col_span = extended.shape[1] - 2 * HALF
    vertical = row_filters[:, 0, None, None] * extended[None, 0:row_span, :]
    for offset in range(1, 2 * HALF + 1):
        vertical = vertical + row_filters[:, offset, None, None] * extended[None, offset:offset + row_span, :]
    result = col_filters[:, 0, None, None] * vertical[:, :, 0:col_span]
    for offset in range(1, 2 * HALF + 1):
        result = result + col_filters[:, offset, None, None] * vertical[:, :, offset:offset + col_span]
    return result

def background_terms(horiz_pos, vert_pos):
    constant = jnp.ones_like(horiz_pos)
    u_square = 0.5 * (3.0 * horiz_pos * horiz_pos - 1.0)
    v_square = 0.5 * (3.0 * vert_pos * vert_pos - 1.0)
    return jnp.stack([constant, horiz_pos, vert_pos, horiz_pos * vert_pos, u_square, v_square, horiz_pos * v_square])

def design_matrix(picked, horiz_pos, vert_pos):
    kernel = jnp.stack([picked, picked * horiz_pos, picked * vert_pos], axis=1).reshape(3 * picked.shape[0], -1)
    background = background_terms(horiz_pos, vert_pos).reshape(7, -1)
    return jnp.concatenate([kernel, background], axis=0).astype(jnp.bfloat16)

def solve_normal(normal_aug):
    factor = jnp.linalg.cholesky(normal_aug[:, :-1])
    lower_sol = jax.scipy.linalg.solve_triangular(factor, normal_aug[:, -1], lower=True)
    return jax.scipy.linalg.solve_triangular(factor, lower_sol, lower=True, trans=1)

def model_values(bases, solution, horiz_pos, vert_pos):
    kernel_part = solution[:3 * BASES].reshape(BASES, 3)
    steady = jnp.einsum('bij,b->ij', bases, kernel_part[:, 0], precision=lax.Precision.HIGHEST)
    along_u = jnp.einsum('bij,b->ij', bases, kernel_part[:, 1], precision=lax.Precision.HIGHEST)
    along_v = jnp.einsum('bij,b->ij', bases, kernel_part[:, 2], precision=lax.Precision.HIGHEST)
    background = background_terms(horiz_pos, vert_pos)
    level = jnp.einsum('mij,m->ij', background, solution[3 * BASES:], precision=lax.Precision.HIGHEST)
    return steady + horiz_pos * along_u + vert_pos * along_v + level

def reference(template, exposure, cosmic_mask, stamp_blocks, row_filters, col_filters):
    padded = jnp.pad(template, ((HALF, HALF), (HALF, HALF)))
    col_index = jnp.arange(COLS, dtype=jnp.int32)
    horiz_all = (2.0 * col_index.astype(jnp.float32) + 1.0) / COLS - 1.0
    offsets = jnp.arange(STAMP_W, dtype=jnp.int32)

    def stripe_rows(stripe_id):
        row_index = stripe_id * ROWS_DEV + jnp.arange(ROWS_DEV, dtype=jnp.int32)
        return (2.0 * row_index.astype(jnp.float32) + 1.0) / NR - 1.0

    def fit_stripe(normal_sum, stripe_id):
        extended = lax.dynamic_slice_in_dim(padded, (stripe_id * ROWS_DEV).astype(jnp.int32), ROWS_DEV + 2 * HALF, 0)
        bases = stripe_bases(extended, row_filters, col_filters)
        blocks = lax.dynamic_index_in_dim(stamp_blocks, stripe_id, 0, keepdims=False)
        chosen = (blocks[:, None] * STAMP_W + offsets[None, :]).reshape(-1).astype(jnp.int32)
        picked = jnp.take(bases, chosen, axis=2)
        horiz_pos = jnp.broadcast_to(horiz_all[chosen][None, :], (ROWS_DEV, chosen.shape[0]))
        vert_pos = jnp.broadcast_to(stripe_rows(stripe_id)[:, None], (ROWS_DEV, chosen.shape[0]))
        design = design_matrix(picked, horiz_pos, vert_pos)
        science = lax.dynamic_slice_in_dim(exposure, (stripe_id * ROWS_DEV).astype(jnp.int32), ROWS_DEV, 1)
        good = lax.dynamic_slice_in_dim(cosmic_mask, (stripe_id * ROWS_DEV).astype(jnp.int32), ROWS_DEV, 1)
        science_sel = jnp.take(science, chosen, axis=2)
        good_sel = jnp.take(good, chosen, axis=2).astype(jnp.float32)
        weighted = design[None] * good_sel.reshape(NEXP, 1, -1).astype(jnp.bfloat16)
        target = (good_sel * science_sel).reshape(NEXP, 1, -1).astype(jnp.bfloat16)
        augmented = jnp.concatenate([weighted, target], axis=1)
        normal = jnp.einsum('enp,emp->enm', weighted.astype(jnp.float32), augmented.astype(jnp.float32), precision=lax.Precision.HIGHEST)
        return (normal_sum + normal, None)
    start_sum = jnp.zeros((NEXP, NCOL, NCOL + 1), jnp.float32)
    normal_total, _ = lax.scan(fit_stripe, start_sum, jnp.arange(STRIPES, dtype=jnp.int32))
    coefficients = jax.vmap(solve_normal)(normal_total)

    def model_stripe(stripe_id):
        extended = lax.dynamic_slice_in_dim(padded, (stripe_id * ROWS_DEV).astype(jnp.int32), ROWS_DEV + 2 * HALF, 0)
        bases = stripe_bases(extended, row_filters, col_filters)
        horiz_pos = jnp.broadcast_to(horiz_all[None, :], (ROWS_DEV, COLS))
        vert_pos = jnp.broadcast_to(stripe_rows(stripe_id)[:, None], (ROWS_DEV, COLS))
        models = jax.vmap(lambda solution: model_values(bases, solution, horiz_pos, vert_pos))(coefficients)
        science = lax.dynamic_slice_in_dim(exposure, (stripe_id * ROWS_DEV).astype(jnp.int32), ROWS_DEV, 1)
        good = lax.dynamic_slice_in_dim(cosmic_mask, (stripe_id * ROWS_DEV).astype(jnp.int32), ROWS_DEV, 1)
        return good.astype(jnp.float32) * (science - models)
    stacked = lax.map(model_stripe, jnp.arange(STRIPES, dtype=jnp.int32))
    difference = jnp.transpose(stacked, (1, 0, 2, 3)).reshape(NEXP, NR, COLS)
    framed = jnp.pad(difference, ((0, 0), (1, 1), (1, 1)))
    neighbours = framed[:, 2:, 1:-1] + framed[:, :-2, 1:-1] + framed[:, 1:-1, 2:] + framed[:, 1:-1, :-2]
    filtered = 4.0 * difference - neighbours
    return (filtered, coefficients)
```

```python
import functools

import jax
import jax.numpy as jnp
from jax import lax
from jax.experimental import pallas as pl
from jax.experimental.pallas import tpu as pltpu
from jax.sharding import PartitionSpec as P

HALF = 9
STAMP_W = 64
EDGE = 128
TILE = 8
BLOCK = 8
REACH = HALF + 1
MESH = pl.DeviceIdType.MESH
LANE_DOT = (((1,), (1,)), ((), ()))


def round_up(n, m):
    return -(-n // m) * m


def row_coords(index, region_rows):
    return (2.0 * index + 1.0) / region_rows - 1.0


def col_coords(first, count, col_total):
    index = lax.broadcasted_iota(jnp.int32, (1, count), 1).astype(jnp.float32) + first
    return (2.0 * index + 1.0) / col_total - 1.0


def background(u, v):
    uu = 0.5 * (3.0 * u * u - 1.0)
    vv = 0.5 * (3.0 * v * v - 1.0)
    return [None, u, v, u * v, uu, vv, u * vv]


def split(x):
    high = x.astype(jnp.bfloat16)
    return high, (x - high.astype(jnp.float32)).astype(jnp.bfloat16)


def shifted_rows(row, count, start):
    return pltpu.roll(jnp.broadcast_to(row, (count, EDGE)), start, 1, stride=1, stride_axis=0)


def iotas(rows):
    return lax.broadcasted_iota(jnp.int32, (rows, EDGE), 0), lax.broadcasted_iota(jnp.int32, (rows, EDGE), 1)


def turn(x, shift, axis):
    return pltpu.roll(x, shift % x.shape[axis], axis)


def squeeze_terms(a, bases, axis):
    padded = round_up(bases, TILE)
    gap = padded - bases
    index = lax.broadcasted_iota(jnp.int32, a.shape, axis)
    out = a
    for t in range(1, 4):
        out = jnp.where(index >= t * bases, turn(a, -t * gap, axis), out)
    return out


def pack_normal(gram, fit):
    half = fit // 2
    rows = gram.shape[0]
    sub, lane = iotas(half)
    one = lane[0:1]
    upper, lower = gram[:half], gram[half:fit]
    merged = jnp.where((lane > sub) & (lane < half), turn(lower, -half, 1), upper)
    fold = half // 2
    body = jnp.where(lane[:fold] < fit, merged[:fold], turn(merged[fold:], fit, 1))
    diag = jnp.sum(jnp.where(lane == sub + half, lower, 0.0), axis=0, keepdims=True)
    last = jnp.where(one < fit, gram[fit : fit + 1], jnp.where(one < fit + half, turn(diag, half, 1), 0.0))
    return body, last


def unpack_normal(body, last, fit):
    half = fit // 2
    sub, lane = iotas(half)
    quad = jnp.concatenate([body, turn(body, fit, 1)], axis=0)
    tall = jnp.concatenate([quad, jnp.broadcast_to(last, (TILE, EDGE))], axis=0)
    flip = jnp.transpose(tall, (1, 0))[:fit]
    flip = jnp.concatenate([flip, jnp.zeros((fit, EDGE - flip.shape[1]), jnp.float32)], axis=1)
    side = turn(flip, half, 1)
    first, second = flip[:half], flip[half:]
    diag = jnp.broadcast_to(turn(last, -fit, 1), (half, EDGE))
    top = jnp.where(lane < half, jnp.where(lane <= sub, quad, first), jnp.where(lane < fit, quad, side[:half]))
    corner = jnp.where(lane > sub, quad, jnp.where(lane == sub, diag, first))
    low = jnp.where(lane < half, second, jnp.where(lane < fit, turn(corner, half, 1), side[half:]))
    return jnp.concatenate([top, low], axis=0)


def eliminate(a, fit):
    sub = lax.broadcasted_iota(jnp.int32, a.shape, 0)
    for first in range(0, fit, BLOCK):
        block = range(first, min(first + BLOCK, fit))
        cols = [jnp.broadcast_to(a[:, k : k + 1], a.shape) for k in block]
        for t, k in enumerate(block):
            inverse = pl.reciprocal(cols[t][k : k + 1, :])
            row = a[k : k + 1, :] * inverse
            a = jnp.where(sub == k, row, a - cols[t] * row)
            for w in range(t + 1, len(block)):
                factor = cols[w][k : k + 1, :] * inverse
                cols[w] = jnp.where(sub == k, factor, cols[w] - cols[t] * factor)
    return jnp.broadcast_to(a[:, fit : fit + 1], a.shape)


def kernel(
    count,
    region_rows,
    radices,
    rounds,
    tmpl_hbm,
    exp_hbm,
    mask_hbm,
    blk_hbm,
    rowf_hbm,
    colf_hbm,
    out_ref,
    row_ref,
    tmpl_ref,
    exp_ref,
    mask_ref,
    blk_ref,
    rowf_ref,
    colf_ref,
    halo_send,
    halo_own,
    halo_other,
    whole,
    edge_send,
    edge_recv,
    ext_ref,
    bandw,
    bandf,
    toep_s,
    toep_f,
    vert,
    design,
    ground,
    vert_f,
    basis,
    coef_ref,
    plane,
    diff,
    send,
    held,
    load_sem,
    halo_ss,
    halo_rs,
    red_ss,
    red_rs,
    hello,
):
    me = lax.axis_index("stripe")
    core = lax.axis_index("exp")
    rows, half = tmpl_ref.shape
    cols = exp_ref.shape[1]
    bases, taps = rowf_ref.shape
    fit = 3 * bases + 7
    pad_b = round_up(bases, TILE)
    ext_rows, wide = ext_ref.shape
    tall = diff.shape[0]
    half_cols = cols // 2
    blocks = half_cols // EDGE
    stamps = 2 * blocks
    tiles = cols // EDGE
    has_up = me > 0
    has_down = me < count - 1
    up_count = has_up.astype(jnp.int32)
    down_count = has_down.astype(jnp.int32)

    barrier = pltpu.get_barrier_semaphore()

    def greet(sem, stripe, exp):
        pl.semaphore_signal(sem, inc=1, device_id={"stripe": stripe, "exp": exp}, device_id_type=MESH)

    @pl.when(has_up)
    def _():
        greet(barrier, me - 1, core)

    @pl.when(has_down)
    def _():
        greet(barrier, me + 1, core)

    greet(barrier, me, 1 - core)

    loads = [
        pltpu.make_async_copy(src, dst, load_sem.at[n])
        for n, (src, dst) in enumerate(
            (
                (tmpl_hbm, tmpl_ref),
                (exp_hbm, exp_ref),
                (mask_hbm, mask_ref),
                (blk_hbm, blk_ref),
                (rowf_hbm, rowf_ref),
                (colf_hbm, colf_ref),
            )
        )
    ]
    for c in loads:
        c.start()

    ext_ref[...] = jnp.zeros_like(ext_ref)

    @pl.when(jnp.logical_not(has_up))
    def _():
        halo_own[0] = jnp.zeros_like(halo_own[0])
        halo_other[0] = jnp.zeros_like(halo_other[0])
        edge_recv[0] = jnp.zeros_like(edge_recv[0])

    @pl.when(jnp.logical_not(has_down))
    def _():
        halo_own[1] = jnp.zeros_like(halo_own[1])
        halo_other[1] = jnp.zeros_like(halo_other[1])
        edge_recv[1] = jnp.zeros_like(edge_recv[1])

    def copy(src, dst, n, stripe, exp):
        return pltpu.make_async_remote_copy(
            src_ref=src,
            dst_ref=dst,
            send_sem=halo_ss.at[n],
            recv_sem=halo_rs.at[n],
            device_id={"stripe": stripe, "exp": exp},
            device_id_type=MESH,
        )

    def halo(way):
        return copy(halo_send.at[way], halo_own.at[way], way, me + 1 - 2 * way, core)

    def edge(way):
        return copy(edge_send.at[way], edge_recv.at[way], 2 + way, me + 1 - 2 * way, core)

    def relay(way):
        return copy(halo_own.at[way], halo_other.at[way], 4 + way, me, 1 - core)

    more = REACH - TILE
    for c in loads:
        c.wait()
    halo_send[0, 0:TILE] = tmpl_ref[rows - TILE : rows]
    halo_send[0, TILE:REACH] = tmpl_ref[rows - REACH : rows - TILE]
    halo_send[1] = tmpl_ref[0:REACH]
    edge_send[0, 0:1, :] = exp_ref[rows - 1 : rows, :]
    edge_send[0, 1:2, :] = mask_ref[rows - 1 : rows, :].astype(jnp.float32)
    edge_send[1, 0:1, :] = exp_ref[0:1, :]
    edge_send[1, 1:2, :] = mask_ref[0:1, :].astype(jnp.float32)

    pl.semaphore_wait(barrier, 1 + up_count + down_count)

    @pl.when(has_down)
    def _():
        halo(0).start()

    @pl.when(has_up)
    def _():
        halo(1).start()

    across = copy(tmpl_ref, whole, 6, me, 1 - core)
    across.start()

    @pl.when(has_down)
    def _():
        edge(0).start()

    @pl.when(has_up)
    def _():
        edge(1).start()

    def call(n):
        reach = 1 << n

        @pl.when(me >= reach)
        def _():
            greet(hello.at[n], me - reach, core)

        @pl.when(me + reach < count)
        def _():
            greet(hello.at[n], me + reach, core)

    def listen(n):
        reach = 1 << n
        heard = (me >= reach).astype(jnp.int32) + (me + reach < count).astype(jnp.int32)
        pl.semaphore_wait(hello.at[n], heard)

    if rounds:
        call(0)

    lanes = jnp.zeros((1, EDGE - taps), jnp.float32)
    low = lax.broadcasted_iota(jnp.int32, (1, EDGE), 1) < STAMP_W
    parity = [blk_ref[0, s] % 2 == 1 for s in range(stamps)]

    def pick(x):
        parts = []
        for m in range(blocks):
            a = x[:, 2 * m * EDGE : (2 * m + 1) * EDGE]
            b = x[:, (2 * m + 1) * EDGE : (2 * m + 2) * EDGE]
            a = jnp.where(parity[2 * m], pltpu.roll(a, STAMP_W, 1), a)
            b = jnp.where(parity[2 * m + 1], b, pltpu.roll(b, STAMP_W, 1))
            parts.append(jnp.where(low, a, b))
        return jnp.concatenate(parts, axis=1)

    start = ext_rows // 2 - rows // 2 - HALF
    sub_e, lane_e = iotas(EDGE)
    sub_t = lax.broadcasted_iota(jnp.int32, (TILE, EDGE), 0)
    for b in range(bases):
        row = jnp.concatenate([rowf_ref[b : b + 1, :], lanes], axis=1)
        high = row.astype(jnp.bfloat16).astype(jnp.float32)

        def placed(x, offset):
            body = shifted_rows(x, rows + TILE, start + offset)
            above = pltpu.roll(jnp.broadcast_to(x, (TILE, EDGE)), start + offset - 1, 1)
            tail = jnp.where(sub_t == TILE - 1, above, body[rows:])
            return body[:rows], jnp.concatenate([body[:rows], tail], axis=0)

        (h0, h0f), (h1, h1f), (r0, r0f) = placed(high, 0), placed(high, ext_rows), placed(row - high, 0)
        bandw[b * rows : (b + 1) * rows, :] = jnp.concatenate([h0 + h1, r0], axis=1)
        bandf[b * tall : (b + 1) * tall, :] = jnp.concatenate([h0f + h1f, r0f], axis=1)
        row = jnp.concatenate([colf_ref[b : b + 1, :], lanes], axis=1)
        spread = shifted_rows(row, EDGE, 0)
        t_high, t_rest = split(spread[:STAMP_W])
        upper = jnp.concatenate([t_high, t_high], axis=1)
        lower = jnp.concatenate([t_rest, jnp.zeros_like(t_rest)], axis=1)
        toep_s[b] = jnp.concatenate([upper, lower], axis=0)
        inside = jnp.where(lane_e >= sub_e, spread, 0.0)
        f_high, f_rest = split(jnp.concatenate([inside, spread - inside], axis=1))
        upper = jnp.concatenate([f_high, f_high], axis=1)
        lower = jnp.concatenate([f_rest, jnp.zeros_like(f_rest)], axis=1)
        toep_f[b] = jnp.concatenate([upper, lower], axis=0)

    first = (me * rows).astype(jnp.float32)
    index = lax.broadcasted_iota(jnp.int32, (rows, 1), 0).astype(jnp.float32)
    v = jnp.broadcast_to(row_coords(index + first, region_rows), (rows, half_cols))
    u_all = jnp.broadcast_to(col_coords(0.0, cols, cols), (TILE, cols))
    u_sel = pick(u_all)
    u = jnp.concatenate([u_sel] * (rows // TILE), axis=0)
    good = pick(mask_ref[...].astype(jnp.float32))
    terms = background(u, v)
    terms[0] = jnp.ones_like(u)
    terms.append(pick(exp_ref[...]))
    for k, term in enumerate(terms):
        x = term * good
        for m in range(blocks):
            ground[m, pl.ds(k, rows, stride=TILE), :] = x[:, m * EDGE : (m + 1) * EDGE]
    zero = jnp.zeros((rows, EDGE), jnp.float32)
    for b in range(bases, pad_b):
        for m in range(blocks):
            design[m, pl.ds(b, rows, stride=pad_b), :] = zero

    if rounds:
        listen(0)
    if rounds > 1:
        call(1)

    @pl.when(has_up)
    def _():
        halo(0).wait_recv()
        relay(0).start()

    @pl.when(has_down)
    def _():
        halo(1).wait_recv()
        relay(1).start()

    across.wait_recv()
    mine = pl.ds(pl.multiple_of(EDGE + core * half, EDGE), half)
    theirs = pl.ds(pl.multiple_of(EDGE + (1 - core) * half, EDGE), half)
    ext_ref[rows : 2 * rows, mine] = tmpl_ref[...]
    ext_ref[rows : 2 * rows, theirs] = whole[...]

    @pl.when(has_up)
    def _():
        relay(0).wait_recv()

    @pl.when(has_down)
    def _():
        relay(1).wait_recv()

    for n, (buf, where) in enumerate(((halo_own, mine), (halo_other, theirs))):
        ext_ref[rows - TILE : rows, where] = buf[0, 0:TILE]
        ext_ref[rows - REACH : rows - TILE, where] = buf[0, TILE:REACH]
        ext_ref[2 * rows : 2 * rows + REACH, where] = buf[1]
    ext = turn(ext_ref[...], -(EDGE - HALF), 1)
    ext_ref[...] = ext

    for n in range(1, rounds):
        listen(n)
        if n + 1 < rounds:
            call(n + 1)

    windows = []
    for s in range(stamps):
        early = ext[:, s * EDGE : (s + 1) * EDGE]
        after = ext[:, (s + 1) * EDGE : (s + 2) * EDGE]
        late = pltpu.roll(jnp.where(low, after, early), STAMP_W, 1)
        windows.append(jnp.where(parity[s], late, early))

    def stack(x):
        high, rest = split(x)
        gap = jnp.zeros((EDGE - 2 * ext_rows, x.shape[1]), jnp.bfloat16)
        gap2 = jnp.zeros((EDGE - ext_rows, x.shape[1]), jnp.bfloat16)
        return jnp.concatenate([high, rest, gap, high, gap2], axis=0)

    window = jnp.concatenate(windows, axis=1)
    vert[...] = jnp.dot(bandw[...].astype(jnp.bfloat16), stack(window), preferred_element_type=jnp.float32)

    for b in range(bases):
        x = vert[b * rows : (b + 1) * rows, :]
        x = jnp.concatenate([x[:, s * EDGE : (s + 1) * EDGE] for s in range(stamps)], axis=0)
        y = lax.dot_general(
            jnp.concatenate(split(x), axis=1), toep_s[b], LANE_DOT, preferred_element_type=jnp.float32
        )
        y = y + pltpu.roll(y, STAMP_W, 1)
        for m in range(blocks):
            picked = jnp.where(low, y[2 * m * rows : (2 * m + 1) * rows], y[(2 * m + 1) * rows : (2 * m + 2) * rows])
            design[m, pl.ds(b, rows, stride=pad_b), :] = picked * good[:, m * EDGE : (m + 1) * EDGE]

    total = 3 * pad_b + TILE
    acc = jnp.zeros((total, total), jnp.float32)
    for r in range(rows):
        parts = []
        for m in range(blocks):
            d = design[m, r * pad_b : (r + 1) * pad_b, :]
            um = u_sel[0:1, m * EDGE : (m + 1) * EDGE]
            vm = v[r : r + 1, 0:EDGE]
            parts.append(jnp.concatenate([d, d * um, d * vm, ground[m, r * TILE : (r + 1) * TILE, :]], axis=0))
        x = jnp.concatenate(parts, axis=1).astype(jnp.bfloat16)
        acc = acc + lax.dot_general(x, x, LANE_DOT, preferred_element_type=jnp.float32)
    gram = jnp.concatenate([acc, jnp.zeros((total, EDGE - total), jnp.float32)], axis=1)
    gram = squeeze_terms(squeeze_terms(gram, bases, 0), bases, 1)
    body, last = pack_normal(gram, fit)

    def reduce_start(phase, base, stride, radix):
        digit = (me // stride) % radix
        copies = []
        for k in range(radix - 1, 0, -1):
            other = digit * 0
            for bit in range((radix - 1).bit_length()):
                on = (digit // (1 << bit)) % 2
                other = other + ((1 - on) if (k >> bit) & 1 else on) * (1 << bit)
            copies.append(
                pltpu.make_async_remote_copy(
                    src_ref=send.at[phase],
                    dst_ref=held.at[base + k - 1],
                    send_sem=red_ss.at[base + k - 1],
                    recv_sem=red_rs.at[base + k - 1],
                    device_id={"stripe": me + (other - digit) * stride},
                    device_id_type=MESH,
                )
            )
        for c in copies:
            c.start()
        return copies

    fold = body.shape[0]

    def put(phase, parts):
        send[phase, 0:fold] = parts[0]
        send[phase, fold : fold + 1] = parts[1]

    def tree(values):
        while len(values) > 1:
            values = [values[q] + values[q + 1] for q in range(0, len(values), 2)]
        return values[0]

    base, stride, flying = 0, 1, []
    for phase, radix in enumerate(radices):
        put(phase, (body, last))
        copies = reduce_start(phase, base, stride, radix)
        flying += copies
        if phase == 0:
            vert_f[...] = jnp.dot(
                bandf[...].astype(jnp.bfloat16), stack(ext_ref[...]), preferred_element_type=jnp.float32
            )
            for b in range(bases):
                x = vert_f[b * tall : (b + 1) * tall, :]
                x = jnp.concatenate([x[:, m * EDGE : (m + 2) * EDGE] for m in range(tiles)], axis=0)
                y = lax.dot_general(
                    jnp.concatenate(split(x), axis=1), toep_f[b], LANE_DOT, preferred_element_type=jnp.float32
                )
                basis[b] = y[:, :EDGE] + y[:, EDGE:]
        for c in copies:
            c.wait_recv()
        body = tree([send[phase, 0:fold]] + [held[base + k, 0:fold] for k in range(radix - 1)])
        last = tree([send[phase, fold : fold + 1]] + [held[base + k, fold : fold + 1] for k in range(radix - 1)])
        base += radix - 1
        stride *= radix

    answer = eliminate(unpack_normal(body, last, fit), fit)
    coef_ref[...] = answer
    n = lax.broadcasted_iota(jnp.int32, (fit, fit), 0)
    term = (n >= bases).astype(jnp.int32) + (n >= 2 * bases).astype(jnp.int32)
    spot = jnp.where(n < 3 * bases, 3 * (n - bases * term) + term, n)
    same = spot == lax.broadcasted_iota(jnp.int32, (fit, fit), 1)
    row_ref[...] = jnp.sum(jnp.where(same, answer[:, :fit], 0.0), axis=0, keepdims=True)

    for c in (0, 1):
        @pl.when((has_up, has_down)[c])
        def _():
            edge(c).wait_recv()

    def coef(n):
        return coef_ref[pl.ds(n, TILE, stride=0), :]

    def three(x):
        return jnp.concatenate([x] * (tall // TILE), axis=0)

    place = lax.broadcasted_iota(jnp.int32, (tall, EDGE), 0)
    place = jnp.where(place == tall - 1, -1, place).astype(jnp.float32)
    v = row_coords(place + first, region_rows)
    vv = 0.5 * (3.0 * v * v - 1.0)
    for b in range(bases):
        plane[b, 0:tall] = three(coef(b)) + v * three(coef(2 * bases + b))
        plane[b, tall : tall + TILE] = coef(bases + b)
    q = [coef(3 * bases + k) for k in range(7)]
    flat = three(q[0]) + v * three(q[2]) + vv * three(q[5])
    slope = three(q[1]) + v * three(q[3]) + vv * three(q[6])
    u_all = col_coords(0.0, cols, cols)
    spare = jnp.zeros((tall - rows - 2, EDGE), jnp.float32)
    for m in range(tiles):
        at = slice(m * EDGE, (m + 1) * EDGE)
        um = jnp.broadcast_to(u_all[:, at], (TILE, EDGE))
        uu = 0.5 * (3.0 * um * um - 1.0)
        model = flat + three(um) * slope + three(q[4] * uu)
        for b in range(bases):
            factor = plane[b, 0:tall] + three(um * plane[b, tall : tall + TILE])
            model = model + factor * basis[b, m * tall : (m + 1) * tall]
        science = jnp.concatenate([exp_ref[:, at], edge_recv[1, 0:1, at], spare, edge_recv[0, 0:1, at]], axis=0)
        clean = jnp.concatenate(
            [mask_ref[:, at].astype(jnp.float32), edge_recv[1, 1:2, at], spare, edge_recv[0, 1:2, at]], axis=0
        )
        diff[:, at] = clean * (science - model)
    lane = lax.broadcasted_iota(jnp.int32, (rows, cols), 1)
    every = diff[...]
    mid = every[:rows]
    left = jnp.where(lane == 0, 0.0, turn(mid, 1, 1))
    right = jnp.where(lane == cols - 1, 0.0, turn(mid, -1, 1))
    around = turn(every, -1, 0)[:rows] + turn(every, 1, 0)[:rows] + right + left
    out_ref[...] = 4.0 * mid - around

    across.wait_send()
    for c in flying:
        c.wait_send()

    @pl.when(has_down)
    def _():
        halo(0).wait_send()
        edge(0).wait_send()
        relay(1).wait_send()

    @pl.when(has_up)
    def _():
        halo(1).wait_send()
        edge(1).wait_send()
        relay(0).wait_send()


def shards(template, exposure, cosmic_mask, stamp_blocks, row_filters, col_filters):
    rows, cols = exposure.shape[1:]
    bases, taps = row_filters.shape
    fit = 3 * bases + 7
    stripes = lax.axis_size("stripe")
    half = template.shape[1]
    ext_rows = 3 * rows
    wide = cols + 2 * EDGE
    tall = round_up(rows + 2, TILE)
    pad_b = round_up(bases, TILE)
    blocks = cols // (2 * EDGE)
    tiles = cols // EDGE
    radices = []
    rest = stripes
    while rest > 1:
        radices.append(min(rest, 8))
        rest //= radices[-1]
    slots = max(1, sum(r - 1 for r in radices))
    rounds = (stripes - 2).bit_length() if stripes > 2 else 0
    packed = fit // 4 + 1
    f32, bf16 = jnp.float32, jnp.bfloat16
    vmem = pl.BlockSpec(memory_space=pltpu.VMEM)
    anywhere = pl.BlockSpec(memory_space=pl.ANY)
    filtered, coef_row = pl.pallas_call(
        functools.partial(kernel, stripes, float(rows * stripes), radices, rounds),
        out_shape=(jax.ShapeDtypeStruct((rows, cols), f32), jax.ShapeDtypeStruct((1, fit), f32)),
        in_specs=[anywhere] * 6,
        out_specs=(vmem, vmem),
        scratch_shapes=[
            pltpu.VMEM((rows, half), f32),
            pltpu.VMEM((rows, cols), f32),
            pltpu.VMEM((rows, cols), jnp.int32),
            pltpu.SMEM(stamp_blocks.shape, jnp.int32),
            pltpu.VMEM((bases, taps), f32),
            pltpu.VMEM((bases, taps), f32),
            pltpu.VMEM((2, REACH, half), f32),
            pltpu.VMEM((2, REACH, half), f32),
            pltpu.VMEM((2, REACH, half), f32),
            pltpu.VMEM((rows, half), f32),
            pltpu.VMEM((2, 2, cols), f32),
            pltpu.VMEM((2, 2, cols), f32),
            pltpu.VMEM((ext_rows, wide), f32),
            pltpu.VMEM((bases * rows, 2 * EDGE), f32),
            pltpu.VMEM((bases * tall, 2 * EDGE), f32),
            pltpu.VMEM((bases, EDGE, 2 * EDGE), bf16),
            pltpu.VMEM((bases, 2 * EDGE, 4 * EDGE), bf16),
            pltpu.VMEM((bases * rows, cols), f32),
            pltpu.VMEM((blocks, rows * pad_b, EDGE), f32),
            pltpu.VMEM((blocks, rows * TILE, EDGE), f32),
            pltpu.VMEM((bases * tall, wide), f32),
            pltpu.VMEM((bases, tiles * tall, EDGE), f32),
            pltpu.VMEM((fit, EDGE), f32),
            pltpu.VMEM((bases, tall + TILE, EDGE), f32),
            pltpu.VMEM((tall, cols), f32),
            pltpu.VMEM((max(1, len(radices)), packed, EDGE), f32),
            pltpu.VMEM((slots, packed, EDGE), f32),
            pltpu.SemaphoreType.DMA((6,)),
            pltpu.SemaphoreType.DMA((7,)),
            pltpu.SemaphoreType.DMA((7,)),
            pltpu.SemaphoreType.DMA((slots,)),
            pltpu.SemaphoreType.DMA((slots,)),
            pltpu.SemaphoreType.REGULAR((max(1, rounds),)),
        ],
        compiler_params=pltpu.CompilerParams(collective_id=0, has_side_effects=True),
        name="fused",
    )(template, exposure[0], cosmic_mask[0], stamp_blocks, row_filters, col_filters)
    return (filtered[None], coef_row)


def solution(mesh):
    placed = (
        P(("groups", "stripe"), "exp"),
        P(("groups", "exp"), "stripe", None),
        P(("groups", "exp"), "stripe", None),
        P(("groups", "stripe"), None),
        P(),
        P(),
    )
    return jax.shard_map(
        shards,
        mesh=mesh,
        in_specs=placed,
        out_specs=(P(("groups", "exp"), "stripe", None), P(("groups", "exp"), None)),
        check_vma=False,
    )
```

```python
import functools

import jax
import jax.numpy as jnp
from jax import lax
from jax.experimental import pallas as pl
from jax.experimental.pallas import tpu as pltpu
from jax.sharding import PartitionSpec as P

HALF = 9
STAMP_W = 64
EDGE = 128
TILE = 8
BLOCK = 8
REACH = HALF + 1
VMEM_GRANT = 32 * 1024 * 1024
MESH = pl.DeviceIdType.MESH
LANE_DOT = (((1,), (1,)), ((), ()))


def round_up(n, m):
    return -(-n // m) * m


def row_coords(index, region_rows):
    return (2.0 * index + 1.0) / region_rows - 1.0


def col_coords(first, count, col_total):
    index = lax.broadcasted_iota(jnp.int32, (1, count), 1).astype(jnp.float32) + first
    return (2.0 * index + 1.0) / col_total - 1.0


def background(u, v):
    uu = 0.5 * (3.0 * u * u - 1.0)
    vv = 0.5 * (3.0 * v * v - 1.0)
    return [None, u, v, u * v, uu, vv, u * vv]


def split(x):
    high = x.astype(jnp.bfloat16)
    return high, (x - high.astype(jnp.float32)).astype(jnp.bfloat16)


def shifted_rows(row, count, start):
    return pltpu.roll(jnp.broadcast_to(row, (count, EDGE)), start, 1, stride=1, stride_axis=0)


def iotas(rows):
    return lax.broadcasted_iota(jnp.int32, (rows, EDGE), 0), lax.broadcasted_iota(jnp.int32, (rows, EDGE), 1)


def turn(x, shift, axis):
    return pltpu.roll(x, shift % x.shape[axis], axis)


def squeeze_terms(a, bases, axis):
    padded = round_up(bases, TILE)
    gap = padded - bases
    index = lax.broadcasted_iota(jnp.int32, a.shape, axis)
    out = a
    for t in range(1, 4):
        out = jnp.where(index >= t * bases, turn(a, -t * gap, axis), out)
    return out


def pack_normal(gram, fit):
    half = fit // 2
    rows = gram.shape[0]
    sub, lane = iotas(half)
    one = lane[0:1]
    upper, lower = gram[:half], gram[half:fit]
    merged = jnp.where((lane > sub) & (lane < half), turn(lower, -half, 1), upper)
    fold = half // 2
    body = jnp.where(lane[:fold] < fit, merged[:fold], turn(merged[fold:], fit, 1))
    diag = jnp.sum(jnp.where(lane == sub + half, lower, 0.0), axis=0, keepdims=True)
    last = jnp.where(one < fit, gram[fit : fit + 1], jnp.where(one < fit + half, turn(diag, half, 1), 0.0))
    return body, last


def unpack_normal(body, last, fit):
    half = fit // 2
    sub, lane = iotas(half)
    quad = jnp.concatenate([body, turn(body, fit, 1)], axis=0)
    tall = jnp.concatenate([quad, jnp.broadcast_to(last, (TILE, EDGE))], axis=0)
    flip = jnp.transpose(tall, (1, 0))[:fit]
    flip = jnp.concatenate([flip, jnp.zeros((fit, EDGE - flip.shape[1]), jnp.float32)], axis=1)
    side = turn(flip, half, 1)
    first, second = flip[:half], flip[half:]
    diag = jnp.broadcast_to(turn(last, -fit, 1), (half, EDGE))
    top = jnp.where(lane < half, jnp.where(lane <= sub, quad, first), jnp.where(lane < fit, quad, side[:half]))
    corner = jnp.where(lane > sub, quad, jnp.where(lane == sub, diag, first))
    low = jnp.where(lane < half, second, jnp.where(lane < fit, turn(corner, half, 1), side[half:]))
    return jnp.concatenate([top, low], axis=0)


def eliminate(a, fit):
    sub = lax.broadcasted_iota(jnp.int32, a.shape, 0)
    for first in range(0, fit, BLOCK):
        block = range(first, min(first + BLOCK, fit))
        cols = [jnp.broadcast_to(a[:, k : k + 1], a.shape) for k in block]
        for t, k in enumerate(block):
            inverse = pl.reciprocal(cols[t][k : k + 1, :])
            row = a[k : k + 1, :] * inverse
            a = jnp.where(sub == k, row, a - cols[t] * row)
            for w in range(t + 1, len(block)):
                factor = cols[w][k : k + 1, :] * inverse
                cols[w] = jnp.where(sub == k, factor, cols[w] - cols[t] * factor)
    return jnp.broadcast_to(a[:, fit : fit + 1], a.shape)


def kernel(
    count,
    region_rows,
    radices,
    rounds,
    tmpl_hbm,
    exp_hbm,
    mask_hbm,
    blk_hbm,
    rowf_hbm,
    colf_hbm,
    diff,
    row_ref,
    tmpl_ref,
    exp_ref,
    mask_ref,
    blk_ref,
    rowf_ref,
    colf_ref,
    halo_send,
    halo_own,
    halo_other,
    whole,
    edge_send,
    edge_recv,
    ext_ref,
    bandw,
    bandf,
    toep_s,
    toep_f,
    vert,
    design,
    ground,
    vert_f,
    basis,
    coef_ref,
    plane,
    send,
    held,
    load_sem,
    halo_ss,
    halo_rs,
    red_ss,
    red_rs,
    hello,
):
    me = lax.axis_index("stripe")
    core = lax.axis_index("exp")
    rows, half = tmpl_ref.shape
    cols = exp_ref.shape[1]
    bases, taps = rowf_ref.shape
    fit = 3 * bases + 7
    pad_b = round_up(bases, TILE)
    ext_rows, wide = ext_ref.shape
    tall = diff.shape[0]
    half_cols = cols // 2
    blocks = half_cols // EDGE
    stamps = 2 * blocks
    tiles = cols // EDGE
    has_up = me > 0
    has_down = me < count - 1
    up_count = has_up.astype(jnp.int32)
    down_count = has_down.astype(jnp.int32)

    barrier = pltpu.get_barrier_semaphore()

    def greet(sem, stripe, exp):
        pl.semaphore_signal(sem, inc=1, device_id={"stripe": stripe, "exp": exp}, device_id_type=MESH)

    @pl.when(has_up)
    def _():
        greet(barrier, me - 1, core)

    @pl.when(has_down)
    def _():
        greet(barrier, me + 1, core)

    greet(barrier, me, 1 - core)

    loads = [
        pltpu.make_async_copy(src, dst, load_sem.at[n])
        for n, (src, dst) in enumerate(
            (
                (tmpl_hbm, tmpl_ref),
                (exp_hbm, exp_ref),
                (mask_hbm, mask_ref),
                (blk_hbm, blk_ref),
                (rowf_hbm, rowf_ref),
                (colf_hbm, colf_ref),
            )
        )
    ]
    for c in loads:
        c.start()

    ext_ref[...] = jnp.zeros_like(ext_ref)

    @pl.when(jnp.logical_not(has_up))
    def _():
        halo_own[0] = jnp.zeros_like(halo_own[0])
        halo_other[0] = jnp.zeros_like(halo_other[0])
        edge_recv[0] = jnp.zeros_like(edge_recv[0])

    @pl.when(jnp.logical_not(has_down))
    def _():
        halo_own[1] = jnp.zeros_like(halo_own[1])
        halo_other[1] = jnp.zeros_like(halo_other[1])
        edge_recv[1] = jnp.zeros_like(edge_recv[1])

    def copy(src, dst, n, stripe, exp):
        return pltpu.make_async_remote_copy(
            src_ref=src,
            dst_ref=dst,
            send_sem=halo_ss.at[n],
            recv_sem=halo_rs.at[n],
            device_id={"stripe": stripe, "exp": exp},
            device_id_type=MESH,
        )

    def halo(way):
        return copy(halo_send.at[way], halo_own.at[way], way, me + 1 - 2 * way, core)

    def edge(way):
        return copy(edge_send.at[way], edge_recv.at[way], 2 + way, me + 1 - 2 * way, core)

    def relay(way):
        return copy(halo_own.at[way], halo_other.at[way], 4 + way, me, 1 - core)

    more = REACH - TILE
    for c in loads:
        c.wait()
    halo_send[0, 0:TILE] = tmpl_ref[rows - TILE : rows]
    halo_send[0, TILE:REACH] = tmpl_ref[rows - REACH : rows - TILE]
    halo_send[1] = tmpl_ref[0:REACH]
    edge_send[0, 0:1, :] = exp_ref[rows - 1 : rows, :]
    edge_send[0, 1:2, :] = mask_ref[rows - 1 : rows, :].astype(jnp.float32)
    edge_send[1, 0:1, :] = exp_ref[0:1, :]
    edge_send[1, 1:2, :] = mask_ref[0:1, :].astype(jnp.float32)

    pl.semaphore_wait(barrier, 1 + up_count + down_count)

    @pl.when(has_down)
    def _():
        halo(0).start()

    @pl.when(has_up)
    def _():
        halo(1).start()

    across = copy(tmpl_ref, whole, 6, me, 1 - core)
    across.start()

    @pl.when(has_down)
    def _():
        edge(0).start()

    @pl.when(has_up)
    def _():
        edge(1).start()

    def call(n):
        reach = 1 << n

        @pl.when(me >= reach)
        def _():
            greet(hello.at[n], me - reach, core)

        @pl.when(me + reach < count)
        def _():
            greet(hello.at[n], me + reach, core)

    def listen(n):
        reach = 1 << n
        heard = (me >= reach).astype(jnp.int32) + (me + reach < count).astype(jnp.int32)
        pl.semaphore_wait(hello.at[n], heard)

    if rounds:
        call(0)

    lanes = jnp.zeros((1, EDGE - taps), jnp.float32)
    low = lax.broadcasted_iota(jnp.int32, (1, EDGE), 1) < STAMP_W
    parity = [blk_ref[0, s] % 2 == 1 for s in range(stamps)]

    def pick(x):
        parts = []
        for m in range(blocks):
            a = x[:, 2 * m * EDGE : (2 * m + 1) * EDGE]
            b = x[:, (2 * m + 1) * EDGE : (2 * m + 2) * EDGE]
            a = jnp.where(parity[2 * m], pltpu.roll(a, STAMP_W, 1), a)
            b = jnp.where(parity[2 * m + 1], b, pltpu.roll(b, STAMP_W, 1))
            parts.append(jnp.where(low, a, b))
        return jnp.concatenate(parts, axis=1)

    start = ext_rows // 2 - rows // 2 - HALF
    sub_e, lane_e = iotas(EDGE)
    sub_t = lax.broadcasted_iota(jnp.int32, (TILE, EDGE), 0)
    for b in range(bases):
        row = jnp.concatenate([rowf_ref[b : b + 1, :], lanes], axis=1)
        high = row.astype(jnp.bfloat16).astype(jnp.float32)

        def placed(x, offset):
            body = shifted_rows(x, rows + TILE, start + offset)
            above = pltpu.roll(jnp.broadcast_to(x, (TILE, EDGE)), start + offset - 1, 1)
            tail = jnp.where(sub_t == TILE - 1, above, body[rows:])
            return body[:rows], jnp.concatenate([body[:rows], tail], axis=0)

        (h0, h0f), (h1, h1f), (r0, r0f) = placed(high, 0), placed(high, ext_rows), placed(row - high, 0)
        bandw[b * rows : (b + 1) * rows, :] = jnp.concatenate([h0 + h1, r0], axis=1)
        bandf[b * tall : (b + 1) * tall, :] = jnp.concatenate([h0f + h1f, r0f], axis=1)
        row = jnp.concatenate([colf_ref[b : b + 1, :], lanes], axis=1)
        spread = shifted_rows(row, EDGE, 0)
        t_high, t_rest = split(spread[:STAMP_W])
        upper = jnp.concatenate([t_high, t_high], axis=1)
        lower = jnp.concatenate([t_rest, jnp.zeros_like(t_rest)], axis=1)
        toep_s[b] = jnp.concatenate([upper, lower], axis=0)
        inside = jnp.where(lane_e >= sub_e, spread, 0.0)
        f_high, f_rest = split(jnp.concatenate([inside, spread - inside], axis=1))
        upper = jnp.concatenate([f_high, f_high], axis=1)
        lower = jnp.concatenate([f_rest, jnp.zeros_like(f_rest)], axis=1)
        toep_f[b] = jnp.concatenate([upper, lower], axis=0)

    first = (me * rows).astype(jnp.float32)
    index = lax.broadcasted_iota(jnp.int32, (rows, 1), 0).astype(jnp.float32)
    v = jnp.broadcast_to(row_coords(index + first, region_rows), (rows, half_cols))
    u_all = jnp.broadcast_to(col_coords(0.0, cols, cols), (TILE, cols))
    u_sel = pick(u_all)
    u = jnp.concatenate([u_sel] * (rows // TILE), axis=0)
    good = pick(mask_ref[...].astype(jnp.float32))
    terms = background(u, v)
    terms[0] = jnp.ones_like(u)
    terms.append(pick(exp_ref[...]))
    for k, term in enumerate(terms):
        x = term * good
        for m in range(blocks):
            ground[m, pl.ds(k, rows, stride=TILE), :] = x[:, m * EDGE : (m + 1) * EDGE]
    zero = jnp.zeros((rows, EDGE), jnp.float32)
    for b in range(bases, pad_b):
        for m in range(blocks):
            design[m, pl.ds(b, rows, stride=pad_b), :] = zero

    if rounds:
        listen(0)
    if rounds > 1:
        call(1)

    @pl.when(has_up)
    def _():
        halo(0).wait_recv()
        relay(0).start()

    @pl.when(has_down)
    def _():
        halo(1).wait_recv()
        relay(1).start()

    across.wait_recv()
    mine = pl.ds(pl.multiple_of(EDGE + core * half, EDGE), half)
    theirs = pl.ds(pl.multiple_of(EDGE + (1 - core) * half, EDGE), half)
    ext_ref[rows : 2 * rows, mine] = tmpl_ref[...]
    ext_ref[rows : 2 * rows, theirs] = whole[...]

    @pl.when(has_up)
    def _():
        relay(0).wait_recv()

    @pl.when(has_down)
    def _():
        relay(1).wait_recv()

    for n, (buf, where) in enumerate(((halo_own, mine), (halo_other, theirs))):
        ext_ref[rows - TILE : rows, where] = buf[0, 0:TILE]
        ext_ref[rows - REACH : rows - TILE, where] = buf[0, TILE:REACH]
        ext_ref[2 * rows : 2 * rows + REACH, where] = buf[1]
    ext = turn(ext_ref[...], -(EDGE - HALF), 1)
    ext_ref[...] = ext

    for n in range(1, rounds):
        listen(n)
        if n + 1 < rounds:
            call(n + 1)

    windows = []
    for s in range(stamps):
        early = ext[:, s * EDGE : (s + 1) * EDGE]
        after = ext[:, (s + 1) * EDGE : (s + 2) * EDGE]
        late = pltpu.roll(jnp.where(low, after, early), STAMP_W, 1)
        windows.append(jnp.where(parity[s], late, early))

    def stack(x):
        high, rest = split(x)
        gap = jnp.zeros((EDGE - 2 * ext_rows, x.shape[1]), jnp.bfloat16)
        gap2 = jnp.zeros((EDGE - ext_rows, x.shape[1]), jnp.bfloat16)
        return jnp.concatenate([high, rest, gap, high, gap2], axis=0)

    window = jnp.concatenate(windows, axis=1)
    vert[...] = jnp.dot(bandw[...].astype(jnp.bfloat16), stack(window), preferred_element_type=jnp.float32)

    for b in range(bases):
        x = vert[b * rows : (b + 1) * rows, :]
        x = jnp.concatenate([x[:, s * EDGE : (s + 1) * EDGE] for s in range(stamps)], axis=0)
        y = lax.dot_general(
            jnp.concatenate(split(x), axis=1), toep_s[b], LANE_DOT, preferred_element_type=jnp.float32
        )
        y = y + pltpu.roll(y, STAMP_W, 1)
        for m in range(blocks):
            picked = jnp.where(low, y[2 * m * rows : (2 * m + 1) * rows], y[(2 * m + 1) * rows : (2 * m + 2) * rows])
            design[m, pl.ds(b, rows, stride=pad_b), :] = picked * good[:, m * EDGE : (m + 1) * EDGE]

    total = 3 * pad_b + TILE
    acc = jnp.zeros((total, total), jnp.float32)
    for r in range(rows):
        parts = []
        for m in range(blocks):
            d = design[m, r * pad_b : (r + 1) * pad_b, :]
            um = u_sel[0:1, m * EDGE : (m + 1) * EDGE]
            vm = v[r : r + 1, 0:EDGE]
            parts.append(jnp.concatenate([d, d * um, d * vm, ground[m, r * TILE : (r + 1) * TILE, :]], axis=0))
        x = jnp.concatenate(parts, axis=1).astype(jnp.bfloat16)
        acc = acc + lax.dot_general(x, x, LANE_DOT, preferred_element_type=jnp.float32)
    gram = jnp.concatenate([acc, jnp.zeros((total, EDGE - total), jnp.float32)], axis=1)
    gram = squeeze_terms(squeeze_terms(gram, bases, 0), bases, 1)
    body, last = pack_normal(gram, fit)

    def reduce_start(phase, base, stride, radix):
        digit = (me // stride) % radix
        copies = []
        for k in range(radix - 1, 0, -1):
            other = digit * 0
            for bit in range((radix - 1).bit_length()):
                on = (digit // (1 << bit)) % 2
                other = other + ((1 - on) if (k >> bit) & 1 else on) * (1 << bit)
            copies.append(
                pltpu.make_async_remote_copy(
                    src_ref=send.at[phase],
                    dst_ref=held.at[base + k - 1],
                    send_sem=red_ss.at[base + k - 1],
                    recv_sem=red_rs.at[base + k - 1],
                    device_id={"stripe": me + (other - digit) * stride},
                    device_id_type=MESH,
                )
            )
        for c in copies:
            c.start()
        return copies

    fold = body.shape[0]

    def put(phase, parts):
        send[phase, 0:fold] = parts[0]
        send[phase, fold : fold + 1] = parts[1]

    def tree(values):
        while len(values) > 1:
            values = [values[q] + values[q + 1] for q in range(0, len(values), 2)]
        return values[0]

    base, stride, flying = 0, 1, []
    for phase, radix in enumerate(radices):
        put(phase, (body, last))
        copies = reduce_start(phase, base, stride, radix)
        flying += copies
        if phase == 0:
            vert_f[...] = jnp.dot(
                bandf[...].astype(jnp.bfloat16), stack(ext_ref[...]), preferred_element_type=jnp.float32
            )
            for b in range(bases):
                x = vert_f[b * tall : (b + 1) * tall, :]
                x = jnp.concatenate([x[:, m * EDGE : (m + 2) * EDGE] for m in range(tiles)], axis=0)
                y = lax.dot_general(
                    jnp.concatenate(split(x), axis=1), toep_f[b], LANE_DOT, preferred_element_type=jnp.float32
                )
                basis[b] = y[:, :EDGE] + y[:, EDGE:]
        for c in copies:
            c.wait_recv()
        body = tree([send[phase, 0:fold]] + [held[base + k, 0:fold] for k in range(radix - 1)])
        last = tree([send[phase, fold : fold + 1]] + [held[base + k, fold : fold + 1] for k in range(radix - 1)])
        base += radix - 1
        stride *= radix

    answer = eliminate(unpack_normal(body, last, fit), fit)
    coef_ref[...] = answer
    n = lax.broadcasted_iota(jnp.int32, (fit, fit), 0)
    term = (n >= bases).astype(jnp.int32) + (n >= 2 * bases).astype(jnp.int32)
    spot = jnp.where(n < 3 * bases, 3 * (n - bases * term) + term, n)
    same = spot == lax.broadcasted_iota(jnp.int32, (fit, fit), 1)
    row_ref[...] = jnp.sum(jnp.where(same, answer[:, :fit], 0.0), axis=0, keepdims=True)

    for c in (0, 1):
        @pl.when((has_up, has_down)[c])
        def _():
            edge(c).wait_recv()

    def coef(n):
        return coef_ref[pl.ds(n, TILE, stride=0), :]

    def three(x):
        return jnp.concatenate([x] * (tall // TILE), axis=0)

    place = lax.broadcasted_iota(jnp.int32, (tall, EDGE), 0)
    place = jnp.where(place == tall - 1, -1, place).astype(jnp.float32)
    v = row_coords(place + first, region_rows)
    vv = 0.5 * (3.0 * v * v - 1.0)
    for b in range(bases):
        plane[b, 0:tall] = three(coef(b)) + v * three(coef(2 * bases + b))
        plane[b, tall : tall + TILE] = coef(bases + b)
    q = [coef(3 * bases + k) for k in range(7)]
    flat = three(q[0]) + v * three(q[2]) + vv * three(q[5])
    slope = three(q[1]) + v * three(q[3]) + vv * three(q[6])
    u_all = col_coords(0.0, cols, cols)
    spare = jnp.zeros((tall - rows - 2, EDGE), jnp.float32)
    for m in range(tiles):
        at = slice(m * EDGE, (m + 1) * EDGE)
        um = jnp.broadcast_to(u_all[:, at], (TILE, EDGE))
        uu = 0.5 * (3.0 * um * um - 1.0)
        model = flat + three(um) * slope + three(q[4] * uu)
        for b in range(bases):
            factor = plane[b, 0:tall] + three(um * plane[b, tall : tall + TILE])
            model = model + factor * basis[b, m * tall : (m + 1) * tall]
        science = jnp.concatenate([exp_ref[:, at], edge_recv[1, 0:1, at], spare, edge_recv[0, 0:1, at]], axis=0)
        clean = jnp.concatenate(
            [mask_ref[:, at].astype(jnp.float32), edge_recv[1, 1:2, at], spare, edge_recv[0, 1:2, at]], axis=0
        )
        diff[:, at] = clean * (science - model)

    across.wait_send()
    for c in flying:
        c.wait_send()

    @pl.when(has_down)
    def _():
        halo(0).wait_send()
        edge(0).wait_send()
        relay(1).wait_send()

    @pl.when(has_up)
    def _():
        halo(1).wait_send()
        edge(1).wait_send()
        relay(0).wait_send()


def finish_kernel(diff_ref, coef_ref, out_ref, row_ref):
    rows, cols = out_ref.shape
    lane = lax.broadcasted_iota(jnp.int32, (rows, cols), 1)
    every = diff_ref[...]
    mid = every[:rows]
    left = jnp.where(lane == 0, 0.0, turn(mid, 1, 1))
    right = jnp.where(lane == cols - 1, 0.0, turn(mid, -1, 1))
    around = turn(every, -1, 0)[:rows] + turn(every, 1, 0)[:rows] + right + left
    out_ref[...] = 4.0 * mid - around
    row_ref[...] = coef_ref[...]


def shards(template, exposure, cosmic_mask, stamp_blocks, row_filters, col_filters):
    rows, cols = exposure.shape[1:]
    bases, taps = row_filters.shape
    fit = 3 * bases + 7
    stripes = lax.axis_size("stripe")
    half = template.shape[1]
    ext_rows = 3 * rows
    wide = cols + 2 * EDGE
    tall = round_up(rows + 2, TILE)
    pad_b = round_up(bases, TILE)
    blocks = cols // (2 * EDGE)
    tiles = cols // EDGE
    radices = []
    rest = stripes
    while rest > 1:
        radices.append(min(rest, 8))
        rest //= radices[-1]
    slots = max(1, sum(r - 1 for r in radices))
    rounds = (stripes - 2).bit_length() if stripes > 2 else 0
    packed = fit // 4 + 1
    f32, bf16 = jnp.float32, jnp.bfloat16
    vmem = pl.BlockSpec(memory_space=pltpu.VMEM)
    anywhere = pl.BlockSpec(memory_space=pltpu.HBM)
    operands = (template, exposure[0], cosmic_mask[0], stamp_blocks, row_filters, col_filters)
    operands = [pltpu.with_memory_space_constraint(x, pltpu.HBM) for x in operands]
    diff, coef_row = pl.pallas_call(
        functools.partial(kernel, stripes, float(rows * stripes), radices, rounds),
        out_shape=(jax.ShapeDtypeStruct((tall, cols), f32), jax.ShapeDtypeStruct((1, fit), f32)),
        in_specs=[anywhere] * 6,
        out_specs=(vmem, vmem),
        scratch_shapes=[
            pltpu.VMEM((rows, half), f32),
            pltpu.VMEM((rows, cols), f32),
            pltpu.VMEM((rows, cols), jnp.int32),
            pltpu.SMEM(stamp_blocks.shape, jnp.int32),
            pltpu.VMEM((bases, taps), f32),
            pltpu.VMEM((bases, taps), f32),
            pltpu.VMEM((2, REACH, half), f32),
            pltpu.VMEM((2, REACH, half), f32),
            pltpu.VMEM((2, REACH, half), f32),
            pltpu.VMEM((rows, half), f32),
            pltpu.VMEM((2, 2, cols), f32),
            pltpu.VMEM((2, 2, cols), f32),
            pltpu.VMEM((ext_rows, wide), f32),
            pltpu.VMEM((bases * rows, 2 * EDGE), f32),
            pltpu.VMEM((bases * tall, 2 * EDGE), f32),
            pltpu.VMEM((bases, EDGE, 2 * EDGE), bf16),
            pltpu.VMEM((bases, 2 * EDGE, 4 * EDGE), bf16),
            pltpu.VMEM((bases * rows, cols), f32),
            pltpu.VMEM((blocks, rows * pad_b, EDGE), f32),
            pltpu.VMEM((blocks, rows * TILE, EDGE), f32),
            pltpu.VMEM((bases * tall, wide), f32),
            pltpu.VMEM((bases, tiles * tall, EDGE), f32),
            pltpu.VMEM((fit, EDGE), f32),
            pltpu.VMEM((bases, tall + TILE, EDGE), f32),
            pltpu.VMEM((max(1, len(radices)), packed, EDGE), f32),
            pltpu.VMEM((slots, packed, EDGE), f32),
            pltpu.SemaphoreType.DMA((6,)),
            pltpu.SemaphoreType.DMA((7,)),
            pltpu.SemaphoreType.DMA((7,)),
            pltpu.SemaphoreType.DMA((slots,)),
            pltpu.SemaphoreType.DMA((slots,)),
            pltpu.SemaphoreType.REGULAR((max(1, rounds),)),
        ],
        compiler_params=pltpu.CompilerParams(
            collective_id=0, has_side_effects=True, vmem_limit_bytes=VMEM_GRANT
        ),
        name="fused",
    )(*operands)
    filtered, coef_row = pl.pallas_call(
        finish_kernel,
        out_shape=(jax.ShapeDtypeStruct((rows, cols), f32), jax.ShapeDtypeStruct((1, fit), f32)),
        in_specs=[vmem, vmem],
        out_specs=(vmem, vmem),
        compiler_params=pltpu.CompilerParams(vmem_limit_bytes=VMEM_GRANT),
        name="finish",
    )(diff, coef_row)
    return (filtered[None], coef_row)


def solution(mesh):
    placed = (
        P(("groups", "stripe"), "exp"),
        P(("groups", "exp"), "stripe", None),
        P(("groups", "exp"), "stripe", None),
        P(("groups", "stripe"), None),
        P(),
        P(),
    )
    return jax.shard_map(
        shards,
        mesh=mesh,
        in_specs=placed,
        out_specs=(P(("groups", "exp"), "stripe", None), P(("groups", "exp"), None)),
        check_vma=False,
    )
```

```python
import functools

import jax
import jax.numpy as jnp
from jax import lax
from jax.experimental import pallas as pl
from jax.experimental.pallas import tpu as pltpu
from jax.sharding import PartitionSpec as P

HALF = 9
STAMP_W = 64
EDGE = 128
TILE = 8
BLOCK = 8
REACH = HALF + 1
VMEM_GRANT = 32 * 1024 * 1024
MESH = pl.DeviceIdType.MESH
LANE_DOT = (((1,), (1,)), ((), ()))


def round_up(n, m):
    return -(-n // m) * m


def row_coords(index, region_rows):
    return (2.0 * index + 1.0) / region_rows - 1.0


def col_coords(first, count, col_total):
    index = lax.broadcasted_iota(jnp.int32, (1, count), 1).astype(jnp.float32) + first
    return (2.0 * index + 1.0) / col_total - 1.0


def background(u, v):
    uu = 0.5 * (3.0 * u * u - 1.0)
    vv = 0.5 * (3.0 * v * v - 1.0)
    return [None, u, v, u * v, uu, vv, u * vv]


def split(x):
    high = x.astype(jnp.bfloat16)
    return high, (x - high.astype(jnp.float32)).astype(jnp.bfloat16)


def shifted_rows(row, count, start):
    return pltpu.roll(jnp.broadcast_to(row, (count, EDGE)), start, 1, stride=1, stride_axis=0)


def iotas(rows):
    return lax.broadcasted_iota(jnp.int32, (rows, EDGE), 0), lax.broadcasted_iota(jnp.int32, (rows, EDGE), 1)


def turn(x, shift, axis):
    return pltpu.roll(x, shift % x.shape[axis], axis)


def squeeze_terms(a, bases, axis):
    padded = round_up(bases, TILE)
    gap = padded - bases
    index = lax.broadcasted_iota(jnp.int32, a.shape, axis)
    out = a
    for t in range(1, 4):
        out = jnp.where(index >= t * bases, turn(a, -t * gap, axis), out)
    return out


def pack_normal(gram, fit):
    half = fit // 2
    rows = gram.shape[0]
    sub, lane = iotas(half)
    one = lane[0:1]
    upper, lower = gram[:half], gram[half:fit]
    merged = jnp.where((lane > sub) & (lane < half), turn(lower, -half, 1), upper)
    fold = half // 2
    body = jnp.where(lane[:fold] < fit, merged[:fold], turn(merged[fold:], fit, 1))
    diag = jnp.sum(jnp.where(lane == sub + half, lower, 0.0), axis=0, keepdims=True)
    last = jnp.where(one < fit, gram[fit : fit + 1], jnp.where(one < fit + half, turn(diag, half, 1), 0.0))
    return body, last


def unpack_normal(body, last, fit):
    half = fit // 2
    sub, lane = iotas(half)
    quad = jnp.concatenate([body, turn(body, fit, 1)], axis=0)
    tall = jnp.concatenate([quad, jnp.broadcast_to(last, (TILE, EDGE))], axis=0)
    flip = jnp.transpose(tall, (1, 0))[:fit]
    flip = jnp.concatenate([flip, jnp.zeros((fit, EDGE - flip.shape[1]), jnp.float32)], axis=1)
    side = turn(flip, half, 1)
    first, second = flip[:half], flip[half:]
    diag = jnp.broadcast_to(turn(last, -fit, 1), (half, EDGE))
    top = jnp.where(lane < half, jnp.where(lane <= sub, quad, first), jnp.where(lane < fit, quad, side[:half]))
    corner = jnp.where(lane > sub, quad, jnp.where(lane == sub, diag, first))
    low = jnp.where(lane < half, second, jnp.where(lane < fit, turn(corner, half, 1), side[half:]))
    return jnp.concatenate([top, low], axis=0)


def eliminate(a, fit):
    sub = lax.broadcasted_iota(jnp.int32, a.shape, 0)
    for first in range(0, fit, BLOCK):
        block = range(first, min(first + BLOCK, fit))
        cols = [jnp.broadcast_to(a[:, k : k + 1], a.shape) for k in block]
        for t, k in enumerate(block):
            inverse = pl.reciprocal(cols[t][k : k + 1, :])
            row = a[k : k + 1, :] * inverse
            a = jnp.where(sub == k, row, a - cols[t] * row)
            for w in range(t + 1, len(block)):
                factor = cols[w][k : k + 1, :] * inverse
                cols[w] = jnp.where(sub == k, factor, cols[w] - cols[t] * factor)
    return jnp.broadcast_to(a[:, fit : fit + 1], a.shape)


def kernel(
    count,
    region_rows,
    radices,
    rounds,
    tmpl_hbm,
    exp_hbm,
    mask_hbm,
    blk_hbm,
    rowf_hbm,
    colf_hbm,
    diff,
    row_ref,
    tmpl_ref,
    exp_ref,
    mask_ref,
    blk_ref,
    rowf_ref,
    colf_ref,
    halo_send,
    halo_own,
    halo_other,
    whole,
    edge_send,
    edge_recv,
    ext_ref,
    bandw,
    bandf,
    toep_s,
    toep_f,
    vert,
    design,
    ground,
    clear,
    across_u,
    grams,
    vert_f,
    basis,
    coef_ref,
    plane,
    send,
    held,
    load_sem,
    halo_ss,
    halo_rs,
    red_ss,
    red_rs,
    hello,
):
    me = lax.axis_index("stripe")
    core = lax.axis_index("exp")
    rows, half = tmpl_ref.shape
    cols = exp_ref.shape[1]
    bases, taps = rowf_ref.shape
    fit = 3 * bases + 7
    pad_b = round_up(bases, TILE)
    ext_rows, wide = ext_ref.shape
    tall = diff.shape[0]
    half_cols = cols // 2
    blocks = half_cols // EDGE
    stamps = 2 * blocks
    tiles = cols // EDGE
    has_up = me > 0
    has_down = me < count - 1
    up_count = has_up.astype(jnp.int32)
    down_count = has_down.astype(jnp.int32)

    barrier = pltpu.get_barrier_semaphore()

    def greet(sem, stripe, exp):
        pl.semaphore_signal(sem, inc=1, device_id={"stripe": stripe, "exp": exp}, device_id_type=MESH)

    @pl.when(has_up)
    def _():
        greet(barrier, me - 1, core)

    @pl.when(has_down)
    def _():
        greet(barrier, me + 1, core)

    greet(barrier, me, 1 - core)

    loads = [
        pltpu.make_async_copy(src, dst, load_sem.at[n])
        for n, (src, dst) in enumerate(
            (
                (tmpl_hbm, tmpl_ref),
                (exp_hbm, exp_ref),
                (mask_hbm, mask_ref),
                (blk_hbm, blk_ref),
                (rowf_hbm, rowf_ref),
                (colf_hbm, colf_ref),
            )
        )
    ]
    for c in loads:
        c.start()

    ext_ref[...] = jnp.zeros_like(ext_ref)

    @pl.when(jnp.logical_not(has_up))
    def _():
        halo_own[0] = jnp.zeros_like(halo_own[0])
        halo_other[0] = jnp.zeros_like(halo_other[0])
        edge_recv[0] = jnp.zeros_like(edge_recv[0])

    @pl.when(jnp.logical_not(has_down))
    def _():
        halo_own[1] = jnp.zeros_like(halo_own[1])
        halo_other[1] = jnp.zeros_like(halo_other[1])
        edge_recv[1] = jnp.zeros_like(edge_recv[1])

    def copy(src, dst, n, stripe, exp):
        return pltpu.make_async_remote_copy(
            src_ref=src,
            dst_ref=dst,
            send_sem=halo_ss.at[n],
            recv_sem=halo_rs.at[n],
            device_id={"stripe": stripe, "exp": exp},
            device_id_type=MESH,
        )

    def halo(way):
        return copy(halo_send.at[way], halo_own.at[way], way, me + 1 - 2 * way, core)

    def edge(way):
        return copy(edge_send.at[way], edge_recv.at[way], 2 + way, me + 1 - 2 * way, core)

    def relay(way):
        return copy(halo_own.at[way], halo_other.at[way], 4 + way, me, 1 - core)

    more = REACH - TILE
    for c in loads:
        c.wait()
    halo_send[0, 0:TILE] = tmpl_ref[rows - TILE : rows]
    halo_send[0, TILE:REACH] = tmpl_ref[rows - REACH : rows - TILE]
    halo_send[1] = tmpl_ref[0:REACH]
    edge_send[0, 0:1, :] = exp_ref[rows - 1 : rows, :]
    edge_send[0, 1:2, :] = mask_ref[rows - 1 : rows, :].astype(jnp.float32)
    edge_send[1, 0:1, :] = exp_ref[0:1, :]
    edge_send[1, 1:2, :] = mask_ref[0:1, :].astype(jnp.float32)

    pl.semaphore_wait(barrier, 1 + up_count + down_count)

    @pl.when(has_down)
    def _():
        halo(0).start()

    @pl.when(has_up)
    def _():
        halo(1).start()

    across = copy(tmpl_ref, whole, 6, me, 1 - core)
    across.start()

    def call(n):
        reach = 1 << n

        @pl.when(me >= reach)
        def _():
            greet(hello.at[n], me - reach, core)

        @pl.when(me + reach < count)
        def _():
            greet(hello.at[n], me + reach, core)

    def listen(n):
        reach = 1 << n
        heard = (me >= reach).astype(jnp.int32) + (me + reach < count).astype(jnp.int32)
        pl.semaphore_wait(hello.at[n], heard)

    if rounds:
        call(0)

    lanes = jnp.zeros((1, EDGE - taps), jnp.float32)
    low = lax.broadcasted_iota(jnp.int32, (1, EDGE), 1) < STAMP_W
    parity = [blk_ref[0, s] % 2 == 1 for s in range(stamps)]

    def pick(x):
        parts = []
        for m in range(blocks):
            a = x[:, 2 * m * EDGE : (2 * m + 1) * EDGE]
            b = x[:, (2 * m + 1) * EDGE : (2 * m + 2) * EDGE]
            a = jnp.where(parity[2 * m], pltpu.roll(a, STAMP_W, 1), a)
            b = jnp.where(parity[2 * m + 1], b, pltpu.roll(b, STAMP_W, 1))
            parts.append(jnp.where(low, a, b))
        return jnp.concatenate(parts, axis=1)

    start = ext_rows // 2 - rows // 2 - HALF
    sub_e, lane_e = iotas(EDGE)
    sub_t = lax.broadcasted_iota(jnp.int32, (TILE, EDGE), 0)
    for b in range(bases):
        row = jnp.concatenate([rowf_ref[b : b + 1, :], lanes], axis=1)
        high = row.astype(jnp.bfloat16).astype(jnp.float32)

        def placed(x, offset):
            body = shifted_rows(x, rows + TILE, start + offset)
            above = pltpu.roll(jnp.broadcast_to(x, (TILE, EDGE)), start + offset - 1, 1)
            tail = jnp.where(sub_t == TILE - 1, above, body[rows:])
            return body[:rows], jnp.concatenate([body[:rows], tail], axis=0)

        (h0, h0f), (h1, h1f), (r0, r0f) = placed(high, 0), placed(high, ext_rows), placed(row - high, 0)
        bandw[b * rows : (b + 1) * rows, :] = jnp.concatenate([h0 + h1, r0], axis=1)
        bandf[b * tall : (b + 1) * tall, :] = jnp.concatenate([h0f + h1f, r0f], axis=1)
        row = jnp.concatenate([colf_ref[b : b + 1, :], lanes], axis=1)
        spread = shifted_rows(row, EDGE, 0)
        t_high, t_rest = split(spread[:STAMP_W])
        upper = jnp.concatenate([t_high, t_high], axis=1)
        lower = jnp.concatenate([t_rest, jnp.zeros_like(t_rest)], axis=1)
        toep_s[b] = jnp.concatenate([upper, lower], axis=0)
        inside = jnp.where(lane_e >= sub_e, spread, 0.0)
        f_high, f_rest = split(jnp.concatenate([inside, spread - inside], axis=1))
        upper = jnp.concatenate([f_high, f_high], axis=1)
        lower = jnp.concatenate([f_rest, jnp.zeros_like(f_rest)], axis=1)
        toep_f[b] = jnp.concatenate([upper, lower], axis=0)

    if rounds:
        listen(0)
    if rounds > 1:
        call(1)

    first = (me * rows).astype(jnp.float32)
    index = lax.broadcasted_iota(jnp.int32, (rows, 1), 0).astype(jnp.float32)
    v = jnp.broadcast_to(row_coords(index + first, region_rows), (rows, half_cols))
    u_all = jnp.broadcast_to(col_coords(0.0, cols, cols), (TILE, cols))
    u_sel = pick(u_all)
    u = jnp.concatenate([u_sel] * (rows // TILE), axis=0)
    good = pick(mask_ref[...].astype(jnp.float32))
    for m in range(blocks):
        clear[m] = good[:, m * EDGE : (m + 1) * EDGE]
        across_u[m] = u_sel[:, m * EDGE : (m + 1) * EDGE]
    terms = background(u, v)
    terms[0] = jnp.ones_like(u)
    terms.append(pick(exp_ref[...]))
    for k, term in enumerate(terms):
        x = term * good
        for m in range(blocks):
            ground[m, pl.ds(k, rows, stride=TILE), :] = x[:, m * EDGE : (m + 1) * EDGE]
    zero = jnp.zeros((rows, EDGE), jnp.float32)
    for b in range(bases, pad_b):
        for m in range(blocks):
            design[m, pl.ds(b, rows, stride=pad_b), :] = zero

    @pl.when(has_up)
    def _():
        halo(0).wait_recv()
        relay(0).start()

    @pl.when(has_down)
    def _():
        halo(1).wait_recv()
        relay(1).start()

    mine = pl.ds(pl.multiple_of(EDGE + core * half, EDGE), half)
    theirs = pl.ds(pl.multiple_of(EDGE + (1 - core) * half, EDGE), half)

    def settle(where, body, buf):
        ext_ref[rows : 2 * rows, where] = body[...]
        ext_ref[rows - TILE : rows, where] = buf[0, 0:TILE]
        ext_ref[rows - REACH : rows - TILE, where] = buf[0, TILE:REACH]
        ext_ref[2 * rows : 2 * rows + REACH, where] = buf[1]

    def stack(x):
        high, rest = split(x)
        gap = jnp.zeros((EDGE - 2 * ext_rows, x.shape[1]), jnp.bfloat16)
        gap2 = jnp.zeros((EDGE - ext_rows, x.shape[1]), jnp.bfloat16)
        return jnp.concatenate([high, rest, gap, high, gap2], axis=0)

    total = 3 * pad_b + TILE

    def stamp_sums(first_block, n, slot):
        span = 2 * n * EDGE
        at = pl.multiple_of(first_block * 2 * EDGE, EDGE)
        ext = turn(ext_ref[:, pl.ds(at, span + 2 * EDGE)], -(EDGE - HALF), 1)
        windows = []
        for s in range(2 * n):
            odd = blk_ref[0, 2 * first_block + s] % 2 == 1
            early = ext[:, s * EDGE : (s + 1) * EDGE]
            after = ext[:, (s + 1) * EDGE : (s + 2) * EDGE]
            late = pltpu.roll(jnp.where(low, after, early), STAMP_W, 1)
            windows.append(jnp.where(odd, late, early))
        window = jnp.concatenate(windows, axis=1)
        vert[:, :span] = jnp.dot(bandw[...].astype(jnp.bfloat16), stack(window), preferred_element_type=jnp.float32)
        for b in range(bases):
            x = vert[b * rows : (b + 1) * rows, :span]
            x = jnp.concatenate([x[:, s * EDGE : (s + 1) * EDGE] for s in range(2 * n)], axis=0)
            y = lax.dot_general(
                jnp.concatenate(split(x), axis=1), toep_s[b], LANE_DOT, preferred_element_type=jnp.float32
            )
            y = y + pltpu.roll(y, STAMP_W, 1)
            for m in range(n):
                near, far = y[2 * m * rows : (2 * m + 1) * rows], y[(2 * m + 1) * rows : (2 * m + 2) * rows]
                design[m, pl.ds(b, rows, stride=pad_b), :] = jnp.where(low, near, far) * clear[first_block + m]
        sums = [jnp.zeros((total, total), jnp.float32) for _ in range(2)]
        for pair in range(rows // 2):
            parts = []
            for r in (2 * pair, 2 * pair + 1):
                vm = v[r : r + 1, 0:EDGE]
                for m in range(n):
                    d = design[m, r * pad_b : (r + 1) * pad_b, :]
                    um = across_u[first_block + m, 0:1]
                    rest = ground[first_block + m, r * TILE : (r + 1) * TILE, :]
                    parts.append(jnp.concatenate([d, d * um, d * vm, rest], axis=0))
            x = jnp.concatenate(parts, axis=1).astype(jnp.bfloat16)
            sums[pair % 2] = sums[pair % 2] + lax.dot_general(x, x, LANE_DOT, preferred_element_type=jnp.float32)
        for h in range(2):
            grams[slot + h, :, 0:total] = sums[h]

    settle(mine, tmpl_ref, halo_own)
    ahead = blocks // 2 - 1
    if ahead:
        stamp_sums(core * (blocks - ahead), ahead, 0)
    if rounds > 1:
        listen(1)
    if rounds > 2:
        call(2)
    across.wait_recv()

    @pl.when(has_up)
    def _():
        relay(0).wait_recv()

    @pl.when(has_down)
    def _():
        relay(1).wait_recv()

    settle(theirs, whole, halo_other)
    stamp_sums((1 - core) * ahead, blocks - ahead, 2)
    @pl.when(has_down)
    def _():
        edge(0).start()

    @pl.when(has_up)
    def _():
        edge(1).start()

    acc = grams[2, :, 0:total] + grams[3, :, 0:total]
    if ahead:
        acc = acc + (grams[0, :, 0:total] + grams[1, :, 0:total])
    gram = jnp.concatenate([acc, jnp.zeros((total, EDGE - total), jnp.float32)], axis=1)
    gram = squeeze_terms(squeeze_terms(gram, bases, 0), bases, 1)
    body, last = pack_normal(gram, fit)
    for n in range(2, rounds):
        listen(n)
        if n + 1 < rounds:
            call(n + 1)

    def reduce_start(phase, base, stride, radix):
        digit = (me // stride) % radix
        copies = []
        for k in range(radix - 1, 0, -1):
            other = digit * 0
            for bit in range((radix - 1).bit_length()):
                on = (digit // (1 << bit)) % 2
                other = other + ((1 - on) if (k >> bit) & 1 else on) * (1 << bit)
            copies.append(
                pltpu.make_async_remote_copy(
                    src_ref=send.at[phase],
                    dst_ref=held.at[base + k - 1],
                    send_sem=red_ss.at[base + k - 1],
                    recv_sem=red_rs.at[base + k - 1],
                    device_id={"stripe": me + (other - digit) * stride},
                    device_id_type=MESH,
                )
            )
        for c in copies:
            c.start()
        return copies

    fold = body.shape[0]

    def put(phase, parts):
        send[phase, 0:fold] = parts[0]
        send[phase, fold : fold + 1] = parts[1]

    def tree(values):
        while len(values) > 1:
            values = [values[q] + values[q + 1] for q in range(0, len(values), 2)]
        return values[0]

    base, stride, flying = 0, 1, []
    for phase, radix in enumerate(radices):
        put(phase, (body, last))
        copies = reduce_start(phase, base, stride, radix)
        flying += copies
        if phase == 0:
            vert_f[...] = jnp.dot(
                bandf[...].astype(jnp.bfloat16), stack(turn(ext_ref[...], -(EDGE - HALF), 1)), preferred_element_type=jnp.float32
            )
            for b in range(bases):
                x = vert_f[b * tall : (b + 1) * tall, :]
                x = jnp.concatenate([x[:, m * EDGE : (m + 2) * EDGE] for m in range(tiles)], axis=0)
                y = lax.dot_general(
                    jnp.concatenate(split(x), axis=1), toep_f[b], LANE_DOT, preferred_element_type=jnp.float32
                )
                basis[b] = y[:, :EDGE] + y[:, EDGE:]
        for c in copies:
            c.wait_recv()
        body = tree([send[phase, 0:fold]] + [held[base + k, 0:fold] for k in range(radix - 1)])
        last = tree([send[phase, fold : fold + 1]] + [held[base + k, fold : fold + 1] for k in range(radix - 1)])
        base += radix - 1
        stride *= radix

    answer = eliminate(unpack_normal(body, last, fit), fit)
    coef_ref[...] = answer
    n = lax.broadcasted_iota(jnp.int32, (fit, fit), 0)
    term = (n >= bases).astype(jnp.int32) + (n >= 2 * bases).astype(jnp.int32)
    spot = jnp.where(n < 3 * bases, 3 * (n - bases * term) + term, n)
    same = spot == lax.broadcasted_iota(jnp.int32, (fit, fit), 1)
    row_ref[...] = jnp.sum(jnp.where(same, answer[:, :fit], 0.0), axis=0, keepdims=True)

    for c in (0, 1):
        @pl.when((has_up, has_down)[c])
        def _():
            edge(c).wait_recv()

    def coef(n):
        return coef_ref[pl.ds(n, TILE, stride=0), :]

    def three(x):
        return jnp.concatenate([x] * (tall // TILE), axis=0)

    place = lax.broadcasted_iota(jnp.int32, (tall, EDGE), 0)
    place = jnp.where(place == tall - 1, -1, place).astype(jnp.float32)
    v = row_coords(place + first, region_rows)
    vv = 0.5 * (3.0 * v * v - 1.0)
    for b in range(bases):
        plane[b, 0:tall] = three(coef(b)) + v * three(coef(2 * bases + b))
        plane[b, tall : tall + TILE] = coef(bases + b)
    q = [coef(3 * bases + k) for k in range(7)]
    flat = three(q[0]) + v * three(q[2]) + vv * three(q[5])
    slope = three(q[1]) + v * three(q[3]) + vv * three(q[6])
    u_all = col_coords(0.0, cols, cols)
    spare = jnp.zeros((tall - rows - 2, EDGE), jnp.float32)
    for m in range(tiles):
        at = slice(m * EDGE, (m + 1) * EDGE)
        um = jnp.broadcast_to(u_all[:, at], (TILE, EDGE))
        uu = 0.5 * (3.0 * um * um - 1.0)
        model = flat + three(um) * slope + three(q[4] * uu)
        for b in range(bases):
            factor = plane[b, 0:tall] + three(um * plane[b, tall : tall + TILE])
            model = model + factor * basis[b, m * tall : (m + 1) * tall]
        science = jnp.concatenate([exp_ref[:, at], edge_recv[1, 0:1, at], spare, edge_recv[0, 0:1, at]], axis=0)
        clean = jnp.concatenate(
            [mask_ref[:, at].astype(jnp.float32), edge_recv[1, 1:2, at], spare, edge_recv[0, 1:2, at]], axis=0
        )
        diff[:, at] = clean * (science - model)

    across.wait_send()
    for c in flying:
        c.wait_send()

    @pl.when(has_down)
    def _():
        halo(0).wait_send()
        edge(0).wait_send()
        relay(1).wait_send()

    @pl.when(has_up)
    def _():
        halo(1).wait_send()
        edge(1).wait_send()
        relay(0).wait_send()


def finish_kernel(diff_ref, coef_ref, out_ref, row_ref):
    rows, cols = out_ref.shape
    lane = lax.broadcasted_iota(jnp.int32, (rows, cols), 1)
    every = diff_ref[...]
    mid = every[:rows]
    left = jnp.where(lane == 0, 0.0, turn(mid, 1, 1))
    right = jnp.where(lane == cols - 1, 0.0, turn(mid, -1, 1))
    around = turn(every, -1, 0)[:rows] + turn(every, 1, 0)[:rows] + right + left
    out_ref[...] = 4.0 * mid - around
    row_ref[...] = coef_ref[...]


def shards(template, exposure, cosmic_mask, stamp_blocks, row_filters, col_filters):
    rows, cols = exposure.shape[1:]
    bases, taps = row_filters.shape
    fit = 3 * bases + 7
    stripes = lax.axis_size("stripe")
    half = template.shape[1]
    ext_rows = 3 * rows
    wide = cols + 2 * EDGE
    tall = round_up(rows + 2, TILE)
    pad_b = round_up(bases, TILE)
    blocks = cols // (2 * EDGE)
    tiles = cols // EDGE
    radices = []
    rest = stripes
    while rest > 1:
        radices.append(min(rest, 8))
        rest //= radices[-1]
    slots = max(1, sum(r - 1 for r in radices))
    rounds = (stripes - 2).bit_length() if stripes > 2 else 0
    packed = fit // 4 + 1
    f32, bf16 = jnp.float32, jnp.bfloat16
    vmem = pl.BlockSpec(memory_space=pltpu.VMEM)
    anywhere = pl.BlockSpec(memory_space=pltpu.HBM)
    operands = (template, exposure[0], cosmic_mask[0], stamp_blocks, row_filters, col_filters)
    operands = [pltpu.with_memory_space_constraint(x, pltpu.HBM) for x in operands]
    diff, coef_row = pl.pallas_call(
        functools.partial(kernel, stripes, float(rows * stripes), radices, rounds),
        out_shape=(jax.ShapeDtypeStruct((tall, cols), f32), jax.ShapeDtypeStruct((1, fit), f32)),
        in_specs=[anywhere] * 6,
        out_specs=(vmem, vmem),
        scratch_shapes=[
            pltpu.VMEM((rows, half), f32),
            pltpu.VMEM((rows, cols), f32),
            pltpu.VMEM((rows, cols), jnp.int32),
            pltpu.SMEM(stamp_blocks.shape, jnp.int32),
            pltpu.VMEM((bases, taps), f32),
            pltpu.VMEM((bases, taps), f32),
            pltpu.VMEM((2, REACH, half), f32),
            pltpu.VMEM((2, REACH, half), f32),
            pltpu.VMEM((2, REACH, half), f32),
            pltpu.VMEM((rows, half), f32),
            pltpu.VMEM((2, 2, cols), f32),
            pltpu.VMEM((2, 2, cols), f32),
            pltpu.VMEM((ext_rows, wide), f32),
            pltpu.VMEM((bases * rows, 2 * EDGE), f32),
            pltpu.VMEM((bases * tall, 2 * EDGE), f32),
            pltpu.VMEM((bases, EDGE, 2 * EDGE), bf16),
            pltpu.VMEM((bases, 2 * EDGE, 4 * EDGE), bf16),
            pltpu.VMEM((bases * rows, cols), f32),
            pltpu.VMEM((blocks, rows * pad_b, EDGE), f32),
            pltpu.VMEM((blocks, rows * TILE, EDGE), f32),
            pltpu.VMEM((blocks, rows, EDGE), f32),
            pltpu.VMEM((blocks, TILE, EDGE), f32),
            pltpu.VMEM((4, 3 * pad_b + TILE, EDGE), f32),
            pltpu.VMEM((bases * tall, wide), f32),
            pltpu.VMEM((bases, tiles * tall, EDGE), f32),
            pltpu.VMEM((fit, EDGE), f32),
            pltpu.VMEM((bases, tall + TILE, EDGE), f32),
            pltpu.VMEM((max(1, len(radices)), packed, EDGE), f32),
            pltpu.VMEM((slots, packed, EDGE), f32),
            pltpu.SemaphoreType.DMA((6,)),
            pltpu.SemaphoreType.DMA((7,)),
            pltpu.SemaphoreType.DMA((7,)),
            pltpu.SemaphoreType.DMA((slots,)),
            pltpu.SemaphoreType.DMA((slots,)),
            pltpu.SemaphoreType.REGULAR((max(1, rounds),)),
        ],
        compiler_params=pltpu.CompilerParams(
            collective_id=0, has_side_effects=True, vmem_limit_bytes=VMEM_GRANT
        ),
        name="fused",
    )(*operands)
    filtered, coef_row = pl.pallas_call(
        finish_kernel,
        out_shape=(jax.ShapeDtypeStruct((rows, cols), f32), jax.ShapeDtypeStruct((1, fit), f32)),
        in_specs=[vmem, vmem],
        out_specs=(vmem, vmem),
        compiler_params=pltpu.CompilerParams(vmem_limit_bytes=VMEM_GRANT),
        name="finish",
    )(diff, coef_row)
    return (filtered[None], coef_row)


def solution(mesh):
    placed = (
        P(("groups", "stripe"), "exp"),
        P(("groups", "exp"), "stripe", None),
        P(("groups", "exp"), "stripe", None),
        P(("groups", "stripe"), None),
        P(),
        P(),
    )
    return jax.shard_map(
        shards,
        mesh=mesh,
        in_specs=placed,
        out_specs=(P(("groups", "exp"), "stripe", None), P(("groups", "exp"), None)),
        check_vma=False,
    )
```

```python
import functools

import jax
import jax.numpy as jnp
from jax import lax
from jax.experimental import pallas as pl
from jax.experimental.pallas import tpu as pltpu
from jax.sharding import PartitionSpec as P

HALF = 9
STAMP_W = 64
EDGE = 128
TILE = 8
BLOCK = 8
REACH = HALF + 1
VMEM_GRANT = 32 * 1024 * 1024
MESH = pl.DeviceIdType.MESH
LANE_DOT = (((1,), (1,)), ((), ()))


def round_up(n, m):
    return -(-n // m) * m


def row_coords(index, region_rows):
    return (2.0 * index + 1.0) / region_rows - 1.0


def col_coords(first, count, col_total):
    index = lax.broadcasted_iota(jnp.int32, (1, count), 1).astype(jnp.float32) + first
    return (2.0 * index + 1.0) / col_total - 1.0


def background(u, v):
    uu = 0.5 * (3.0 * u * u - 1.0)
    vv = 0.5 * (3.0 * v * v - 1.0)
    return [None, u, v, u * v, uu, vv, u * vv]


def split(x):
    high = x.astype(jnp.bfloat16)
    return high, (x - high.astype(jnp.float32)).astype(jnp.bfloat16)


def shifted_rows(row, count, start):
    return pltpu.roll(jnp.broadcast_to(row, (count, EDGE)), start, 1, stride=1, stride_axis=0)


def iotas(rows):
    return lax.broadcasted_iota(jnp.int32, (rows, EDGE), 0), lax.broadcasted_iota(jnp.int32, (rows, EDGE), 1)


def turn(x, shift, axis):
    return pltpu.roll(x, shift % x.shape[axis], axis)


def squeeze_terms(a, bases, axis):
    padded = round_up(bases, TILE)
    gap = padded - bases
    index = lax.broadcasted_iota(jnp.int32, a.shape, axis)
    out = a
    for t in range(1, 4):
        out = jnp.where(index >= t * bases, turn(a, -t * gap, axis), out)
    return out


def pack_normal(gram, fit):
    half = fit // 2
    rows = gram.shape[0]
    sub, lane = iotas(half)
    one = lane[0:1]
    upper, lower = gram[:half], gram[half:fit]
    merged = jnp.where((lane > sub) & (lane < half), turn(lower, -half, 1), upper)
    fold = half // 2
    body = jnp.where(lane[:fold] < fit, merged[:fold], turn(merged[fold:], fit, 1))
    diag = jnp.sum(jnp.where(lane == sub + half, lower, 0.0), axis=0, keepdims=True)
    last = jnp.where(one < fit, gram[fit : fit + 1], jnp.where(one < fit + half, turn(diag, half, 1), 0.0))
    return body, last


def unpack_normal(body, last, fit):
    half = fit // 2
    sub, lane = iotas(half)
    quad = jnp.concatenate([body, turn(body, fit, 1)], axis=0)
    tall = jnp.concatenate([quad, jnp.broadcast_to(last, (TILE, EDGE))], axis=0)
    flip = jnp.transpose(tall, (1, 0))[:fit]
    flip = jnp.concatenate([flip, jnp.zeros((fit, EDGE - flip.shape[1]), jnp.float32)], axis=1)
    side = turn(flip, half, 1)
    first, second = flip[:half], flip[half:]
    diag = jnp.broadcast_to(turn(last, -fit, 1), (half, EDGE))
    top = jnp.where(lane < half, jnp.where(lane <= sub, quad, first), jnp.where(lane < fit, quad, side[:half]))
    corner = jnp.where(lane > sub, quad, jnp.where(lane == sub, diag, first))
    low = jnp.where(lane < half, second, jnp.where(lane < fit, turn(corner, half, 1), side[half:]))
    return jnp.concatenate([top, low], axis=0)


def eliminate(a, fit):
    shape = (TILE, EDGE)
    count = fit // TILE
    tiles = [a[i * TILE : (i + 1) * TILE] for i in range(count)]
    sub = lax.broadcasted_iota(jnp.int32, shape, 0)
    for i in range(count):
        order = [j % count for j in range(i, i + count)]
        cols = {j: [jnp.broadcast_to(tiles[j][:, k : k + 1], shape) for k in range(i * TILE, (i + 1) * TILE)] for j in order}
        near = list(cols[i])
        for t in range(TILE):
            inverse = pl.reciprocal(near[t][t : t + 1])

            def step(x):
                row = x[t : t + 1] * inverse
                return jnp.where(sub == t, row, x - near[t] * row)

            for w in range(t + 1, TILE):
                near[w] = step(near[w])
            tiles[i] = step(tiles[i])
        for j in order[1:]:
            terms = [cols[j][t] * tiles[i][t : t + 1] for t in range(TILE)]
            while len(terms) > 1:
                terms = [terms[q] + terms[q + 1] for q in range(0, len(terms), 2)]
            tiles[j] = tiles[j] - terms[0]
    return jnp.concatenate([jnp.broadcast_to(x[:, fit : fit + 1], shape) for x in tiles], axis=0)


def kernel(
    count,
    region_rows,
    radices,
    rounds,
    tmpl_hbm,
    exp_hbm,
    mask_hbm,
    blk_hbm,
    rowf_hbm,
    colf_hbm,
    diff,
    row_ref,
    tmpl_ref,
    exp_ref,
    mask_ref,
    blk_ref,
    rowf_ref,
    colf_ref,
    halo_send,
    halo_own,
    halo_other,
    whole,
    edge_send,
    edge_recv,
    ext_ref,
    bandw,
    bandf,
    toep_s,
    toep_f,
    vert,
    design,
    ground,
    clear,
    across_u,
    grams,
    vert_f,
    basis,
    coef_ref,
    plane,
    send,
    held,
    load_sem,
    halo_ss,
    halo_rs,
    red_ss,
    red_rs,
    hello,
):
    me = lax.axis_index("stripe")
    core = lax.axis_index("exp")
    rows, half = tmpl_ref.shape
    cols = exp_ref.shape[1]
    bases, taps = rowf_ref.shape
    fit = 3 * bases + 7
    pad_b = round_up(bases, TILE)
    ext_rows, wide = ext_ref.shape
    tall = diff.shape[0]
    half_cols = cols // 2
    blocks = half_cols // EDGE
    stamps = 2 * blocks
    tiles = cols // EDGE
    has_up = me > 0
    has_down = me < count - 1
    up_count = has_up.astype(jnp.int32)
    down_count = has_down.astype(jnp.int32)

    barrier = pltpu.get_barrier_semaphore()

    def greet(sem, stripe, exp):
        pl.semaphore_signal(sem, inc=1, device_id={"stripe": stripe, "exp": exp}, device_id_type=MESH)

    @pl.when(has_up)
    def _():
        greet(barrier, me - 1, core)

    @pl.when(has_down)
    def _():
        greet(barrier, me + 1, core)

    greet(barrier, me, 1 - core)

    loads = [
        pltpu.make_async_copy(src, dst, load_sem.at[n])
        for n, (src, dst) in enumerate(
            (
                (tmpl_hbm, tmpl_ref),
                (exp_hbm, exp_ref),
                (mask_hbm, mask_ref),
                (blk_hbm, blk_ref),
                (rowf_hbm, rowf_ref),
                (colf_hbm, colf_ref),
            )
        )
    ]
    for c in loads:
        c.start()

    ext_ref[...] = jnp.zeros_like(ext_ref)

    @pl.when(jnp.logical_not(has_up))
    def _():
        halo_own[0] = jnp.zeros_like(halo_own[0])
        halo_other[0] = jnp.zeros_like(halo_other[0])
        edge_recv[0] = jnp.zeros_like(edge_recv[0])

    @pl.when(jnp.logical_not(has_down))
    def _():
        halo_own[1] = jnp.zeros_like(halo_own[1])
        halo_other[1] = jnp.zeros_like(halo_other[1])
        edge_recv[1] = jnp.zeros_like(edge_recv[1])

    def copy(src, dst, n, stripe, exp):
        return pltpu.make_async_remote_copy(
            src_ref=src,
            dst_ref=dst,
            send_sem=halo_ss.at[n],
            recv_sem=halo_rs.at[n],
            device_id={"stripe": stripe, "exp": exp},
            device_id_type=MESH,
        )

    def halo(way):
        return copy(halo_send.at[way], halo_own.at[way], way, me + 1 - 2 * way, core)

    def edge(way):
        return copy(edge_send.at[way], edge_recv.at[way], 2 + way, me + 1 - 2 * way, core)

    def relay(way):
        return copy(halo_own.at[way], halo_other.at[way], 4 + way, me, 1 - core)

    more = REACH - TILE
    spans = half // EDGE
    for c in loads:
        c.wait()
    for way, near, far in ((0, rows - TILE, rows - REACH), (1, 0, TILE)):
        halo_send[way, :, 0:half] = tmpl_ref[near : near + TILE]
        for e in range(more):
            for m in range(spans):
                column, line = half + (e * spans + m) // TILE * EDGE, (e * spans + m) % TILE
                halo_send[way, line : line + 1, column : column + EDGE] = tmpl_ref[
                    far + e : far + e + 1, m * EDGE : (m + 1) * EDGE
                ]
    edge_send[0, 0:1, :] = exp_ref[rows - 1 : rows, :]
    edge_send[0, 1:2, :] = mask_ref[rows - 1 : rows, :].astype(jnp.float32)
    edge_send[1, 0:1, :] = exp_ref[0:1, :]
    edge_send[1, 1:2, :] = mask_ref[0:1, :].astype(jnp.float32)

    pl.semaphore_wait(barrier, 1 + up_count + down_count)

    @pl.when(has_down)
    def _():
        halo(0).start()

    @pl.when(has_up)
    def _():
        halo(1).start()

    across = copy(tmpl_ref, whole, 6, me, 1 - core)
    across.start()

    def call(n):
        reach = 1 << n

        @pl.when(me >= reach)
        def _():
            greet(hello.at[n], me - reach, core)

        @pl.when(me + reach < count)
        def _():
            greet(hello.at[n], me + reach, core)

    def listen(n):
        reach = 1 << n
        heard = (me >= reach).astype(jnp.int32) + (me + reach < count).astype(jnp.int32)
        pl.semaphore_wait(hello.at[n], heard)

    if rounds:
        call(0)

    lanes = jnp.zeros((1, EDGE - taps), jnp.float32)
    low = lax.broadcasted_iota(jnp.int32, (1, EDGE), 1) < STAMP_W
    parity = [blk_ref[0, s] % 2 == 1 for s in range(stamps)]

    def pick(x):
        parts = []
        for m in range(blocks):
            a = x[:, 2 * m * EDGE : (2 * m + 1) * EDGE]
            b = x[:, (2 * m + 1) * EDGE : (2 * m + 2) * EDGE]
            a = jnp.where(parity[2 * m], pltpu.roll(a, STAMP_W, 1), a)
            b = jnp.where(parity[2 * m + 1], b, pltpu.roll(b, STAMP_W, 1))
            parts.append(jnp.where(low, a, b))
        return jnp.concatenate(parts, axis=1)

    start = ext_rows // 2 - rows // 2 - HALF
    sub_e, lane_e = iotas(EDGE)
    sub_t = lax.broadcasted_iota(jnp.int32, (TILE, EDGE), 0)
    for b in range(bases):
        row = jnp.concatenate([rowf_ref[b : b + 1, :], lanes], axis=1)
        high = row.astype(jnp.bfloat16).astype(jnp.float32)

        def placed(x, offset):
            body = shifted_rows(x, rows + TILE, start + offset)
            above = pltpu.roll(jnp.broadcast_to(x, (TILE, EDGE)), start + offset - 1, 1)
            tail = jnp.where(sub_t == TILE - 1, above, body[rows:])
            return body[:rows], jnp.concatenate([body[:rows], tail], axis=0)

        (h0, h0f), (h1, h1f), (r0, r0f) = placed(high, 0), placed(high, ext_rows), placed(row - high, 0)
        bandw[b * rows : (b + 1) * rows, :] = jnp.concatenate([h0 + h1, r0], axis=1)
        bandf[b * tall : (b + 1) * tall, :] = jnp.concatenate([h0f + h1f, r0f], axis=1)
        row = jnp.concatenate([colf_ref[b : b + 1, :], lanes], axis=1)
        spread = shifted_rows(row, EDGE, 0)
        t_high, t_rest = split(spread[:STAMP_W])
        upper = jnp.concatenate([t_high, t_high], axis=1)
        lower = jnp.concatenate([t_rest, jnp.zeros_like(t_rest)], axis=1)
        toep_s[b] = jnp.concatenate([upper, lower], axis=0)
        inside = jnp.where(lane_e >= sub_e, spread, 0.0)
        f_high, f_rest = split(jnp.concatenate([inside, spread - inside], axis=1))
        upper = jnp.concatenate([f_high, f_high], axis=1)
        lower = jnp.concatenate([f_rest, jnp.zeros_like(f_rest)], axis=1)
        toep_f[b] = jnp.concatenate([upper, lower], axis=0)

    if rounds:
        listen(0)
    if rounds > 1:
        call(1)

    first = (me * rows).astype(jnp.float32)
    index = lax.broadcasted_iota(jnp.int32, (rows, 1), 0).astype(jnp.float32)
    v = jnp.broadcast_to(row_coords(index + first, region_rows), (rows, half_cols))
    u_all = jnp.broadcast_to(col_coords(0.0, cols, cols), (TILE, cols))
    u_sel = pick(u_all)
    u = jnp.concatenate([u_sel] * (rows // TILE), axis=0)
    good = pick(mask_ref[...].astype(jnp.float32))
    for m in range(blocks):
        clear[m] = good[:, m * EDGE : (m + 1) * EDGE]
        across_u[m] = u_sel[:, m * EDGE : (m + 1) * EDGE]
    terms = background(u, v)
    terms[0] = jnp.ones_like(u)
    terms.append(pick(exp_ref[...]))
    for k, term in enumerate(terms):
        x = term * good
        for m in range(blocks):
            ground[m, pl.ds(k, rows, stride=TILE), :] = x[:, m * EDGE : (m + 1) * EDGE]
    zero = jnp.zeros((rows, EDGE), jnp.float32)
    for b in range(bases, pad_b):
        for m in range(blocks):
            design[m, pl.ds(b, rows, stride=pad_b), :] = zero

    @pl.when(has_up)
    def _():
        halo(0).wait_recv()
        relay(0).start()

    @pl.when(has_down)
    def _():
        halo(1).wait_recv()
        relay(1).start()

    def settle(side, body, buf):
        where = pl.ds(pl.multiple_of(EDGE + side * half, EDGE), half)
        ext_ref[rows : 2 * rows, where] = body[...]
        for way, near, far in ((0, rows - TILE, rows - REACH), (1, 2 * rows, 2 * rows + TILE)):
            ext_ref[near : near + TILE, where] = buf[way, :, 0:half]
            for e in range(more):
                for m in range(spans):
                    column, line = half + (e * spans + m) // TILE * EDGE, (e * spans + m) % TILE
                    at = pl.ds(pl.multiple_of((1 + m) * EDGE + side * half, EDGE), EDGE)
                    ext_ref[far + e : far + e + 1, at] = buf[way, line : line + 1, column : column + EDGE]

    def stack(x):
        high, rest = split(x)
        gap = jnp.zeros((EDGE - 2 * ext_rows, x.shape[1]), jnp.bfloat16)
        gap2 = jnp.zeros((EDGE - ext_rows, x.shape[1]), jnp.bfloat16)
        return jnp.concatenate([high, rest, gap, high, gap2], axis=0)

    total = 3 * pad_b + TILE

    def stamp_sums(first_block, n, slot):
        span = 2 * n * EDGE
        at = pl.multiple_of(first_block * 2 * EDGE, EDGE)
        ext = turn(ext_ref[:, pl.ds(at, span + 2 * EDGE)], -(EDGE - HALF), 1)
        windows = []
        for s in range(2 * n):
            odd = blk_ref[0, 2 * first_block + s] % 2 == 1
            early = ext[:, s * EDGE : (s + 1) * EDGE]
            after = ext[:, (s + 1) * EDGE : (s + 2) * EDGE]
            late = pltpu.roll(jnp.where(low, after, early), STAMP_W, 1)
            windows.append(jnp.where(odd, late, early))
        window = jnp.concatenate(windows, axis=1)
        vert[:, :span] = jnp.dot(bandw[...].astype(jnp.bfloat16), stack(window), preferred_element_type=jnp.float32)
        for b in range(bases):
            x = vert[b * rows : (b + 1) * rows, :span]
            x = jnp.concatenate([x[:, s * EDGE : (s + 1) * EDGE] for s in range(2 * n)], axis=0)
            y = lax.dot_general(
                jnp.concatenate(split(x), axis=1), toep_s[b], LANE_DOT, preferred_element_type=jnp.float32
            )
            y = y + pltpu.roll(y, STAMP_W, 1)
            for m in range(n):
                near, far = y[2 * m * rows : (2 * m + 1) * rows], y[(2 * m + 1) * rows : (2 * m + 2) * rows]
                design[m, pl.ds(b, rows, stride=pad_b), :] = jnp.where(low, near, far) * clear[first_block + m]
        sums = [jnp.zeros((total, total), jnp.float32) for _ in range(2)]
        for pair in range(rows // 2):
            parts = []
            for r in (2 * pair, 2 * pair + 1):
                vm = v[r : r + 1, 0:EDGE]
                for m in range(n):
                    d = design[m, r * pad_b : (r + 1) * pad_b, :]
                    um = across_u[first_block + m, 0:1]
                    rest = ground[first_block + m, r * TILE : (r + 1) * TILE, :]
                    parts.append(jnp.concatenate([d, d * um, d * vm, rest], axis=0))
            x = jnp.concatenate(parts, axis=1).astype(jnp.bfloat16)
            sums[pair % 2] = sums[pair % 2] + lax.dot_general(x, x, LANE_DOT, preferred_element_type=jnp.float32)
        for h in range(2):
            grams[slot + h, :, 0:total] = sums[h]

    settle(core, tmpl_ref, halo_own)
    ahead = blocks // 2 - 1
    if ahead:
        stamp_sums(core * (blocks - ahead), ahead, 0)
    if rounds > 1:
        listen(1)
    if rounds > 2:
        call(2)
    across.wait_recv()

    @pl.when(has_up)
    def _():
        relay(0).wait_recv()

    @pl.when(has_down)
    def _():
        relay(1).wait_recv()

    settle(1 - core, whole, halo_other)
    stamp_sums((1 - core) * ahead, blocks - ahead, 2)
    @pl.when(has_down)
    def _():
        edge(0).start()

    @pl.when(has_up)
    def _():
        edge(1).start()

    acc = grams[2, :, 0:total] + grams[3, :, 0:total]
    if ahead:
        acc = acc + (grams[0, :, 0:total] + grams[1, :, 0:total])
    gram = jnp.concatenate([acc, jnp.zeros((total, EDGE - total), jnp.float32)], axis=1)
    gram = squeeze_terms(squeeze_terms(gram, bases, 0), bases, 1)
    body, last = pack_normal(gram, fit)
    for n in range(2, rounds):
        listen(n)
        if n + 1 < rounds:
            call(n + 1)

    def reduce_start(phase, base, stride, radix):
        digit = (me // stride) % radix
        copies = []
        for k in range(radix - 1, 0, -1):
            other = digit * 0
            for bit in range((radix - 1).bit_length()):
                on = (digit // (1 << bit)) % 2
                other = other + ((1 - on) if (k >> bit) & 1 else on) * (1 << bit)
            copies.append(
                pltpu.make_async_remote_copy(
                    src_ref=send.at[phase],
                    dst_ref=held.at[base + k - 1],
                    send_sem=red_ss.at[base + k - 1],
                    recv_sem=red_rs.at[base + k - 1],
                    device_id={"stripe": me + (other - digit) * stride},
                    device_id_type=MESH,
                )
            )
        for c in copies:
            c.start()
        return copies

    fold = body.shape[0]

    def put(phase, parts):
        send[phase, 0:fold] = parts[0]
        send[phase, fold : fold + 1] = parts[1]

    def tree(values):
        while len(values) > 1:
            values = [values[q] + values[q + 1] for q in range(0, len(values), 2)]
        return values[0]

    base, stride, flying = 0, 1, []
    for phase, radix in enumerate(radices):
        put(phase, (body, last))
        copies = reduce_start(phase, base, stride, radix)
        flying += copies
        if phase == 0:
            vert_f[...] = jnp.dot(
                bandf[...].astype(jnp.bfloat16), stack(turn(ext_ref[...], -(EDGE - HALF), 1)), preferred_element_type=jnp.float32
            )
            for b in range(bases):
                x = vert_f[b * tall : (b + 1) * tall, :]
                x = jnp.concatenate([x[:, m * EDGE : (m + 2) * EDGE] for m in range(tiles)], axis=0)
                y = lax.dot_general(
                    jnp.concatenate(split(x), axis=1), toep_f[b], LANE_DOT, preferred_element_type=jnp.float32
                )
                basis[b] = y[:, :EDGE] + y[:, EDGE:]
        for c in copies:
            c.wait_recv()
        body = tree([send[phase, 0:fold]] + [held[base + k, 0:fold] for k in range(radix - 1)])
        last = tree([send[phase, fold : fold + 1]] + [held[base + k, fold : fold + 1] for k in range(radix - 1)])
        base += radix - 1
        stride *= radix

    answer = eliminate(unpack_normal(body, last, fit), fit)
    coef_ref[...] = answer
    n = lax.broadcasted_iota(jnp.int32, (fit, fit), 0)
    term = (n >= bases).astype(jnp.int32) + (n >= 2 * bases).astype(jnp.int32)
    spot = jnp.where(n < 3 * bases, 3 * (n - bases * term) + term, n)
    same = spot == lax.broadcasted_iota(jnp.int32, (fit, fit), 1)
    row_ref[...] = jnp.sum(jnp.where(same, answer[:, :fit], 0.0), axis=0, keepdims=True)

    for c in (0, 1):
        @pl.when((has_up, has_down)[c])
        def _():
            edge(c).wait_recv()

    def coef(n):
        return coef_ref[pl.ds(n, TILE, stride=0), :]

    def three(x):
        return jnp.concatenate([x] * (tall // TILE), axis=0)

    place = lax.broadcasted_iota(jnp.int32, (tall, EDGE), 0)
    place = jnp.where(place == tall - 1, -1, place).astype(jnp.float32)
    v = row_coords(place + first, region_rows)
    vv = 0.5 * (3.0 * v * v - 1.0)
    for b in range(bases):
        plane[b, 0:tall] = three(coef(b)) + v * three(coef(2 * bases + b))
        plane[b, tall : tall + TILE] = coef(bases + b)
    q = [coef(3 * bases + k) for k in range(7)]
    flat = three(q[0]) + v * three(q[2]) + vv * three(q[5])
    slope = three(q[1]) + v * three(q[3]) + vv * three(q[6])
    u_all = col_coords(0.0, cols, cols)
    spare = jnp.zeros((tall - rows - 2, EDGE), jnp.float32)
    for m in range(tiles):
        at = slice(m * EDGE, (m + 1) * EDGE)
        um = jnp.broadcast_to(u_all[:, at], (TILE, EDGE))
        uu = 0.5 * (3.0 * um * um - 1.0)
        model = flat + three(um) * slope + three(q[4] * uu)
        for b in range(bases):
            factor = plane[b, 0:tall] + three(um * plane[b, tall : tall + TILE])
            model = model + factor * basis[b, m * tall : (m + 1) * tall]
        science = jnp.concatenate([exp_ref[:, at], edge_recv[1, 0:1, at], spare, edge_recv[0, 0:1, at]], axis=0)
        clean = jnp.concatenate(
            [mask_ref[:, at].astype(jnp.float32), edge_recv[1, 1:2, at], spare, edge_recv[0, 1:2, at]], axis=0
        )
        diff[:, at] = clean * (science - model)

    across.wait_send()
    for c in flying:
        c.wait_send()

    @pl.when(has_down)
    def _():
        halo(0).wait_send()
        edge(0).wait_send()
        relay(1).wait_send()

    @pl.when(has_up)
    def _():
        halo(1).wait_send()
        edge(1).wait_send()
        relay(0).wait_send()


def finish_kernel(diff_ref, coef_ref, out_ref, row_ref):
    rows, cols = out_ref.shape
    lane = lax.broadcasted_iota(jnp.int32, (rows, cols), 1)
    every = diff_ref[...]
    mid = every[:rows]
    left = jnp.where(lane == 0, 0.0, turn(mid, 1, 1))
    right = jnp.where(lane == cols - 1, 0.0, turn(mid, -1, 1))
    around = turn(every, -1, 0)[:rows] + turn(every, 1, 0)[:rows] + right + left
    out_ref[...] = 4.0 * mid - around
    row_ref[...] = coef_ref[...]


def shards(template, exposure, cosmic_mask, stamp_blocks, row_filters, col_filters):
    rows, cols = exposure.shape[1:]
    bases, taps = row_filters.shape
    fit = 3 * bases + 7
    stripes = lax.axis_size("stripe")
    half = template.shape[1]
    ext_rows = 3 * rows
    wide = cols + 2 * EDGE
    tall = round_up(rows + 2, TILE)
    pad_b = round_up(bases, TILE)
    blocks = cols // (2 * EDGE)
    tiles = cols // EDGE
    radices = []
    rest = stripes
    while rest > 1:
        radices.append(min(rest, 8))
        rest //= radices[-1]
    slots = max(1, sum(r - 1 for r in radices))
    rounds = (stripes - 2).bit_length() if stripes > 2 else 0
    packed = fit // 4 + 1
    extra = round_up((REACH - TILE) * half // EDGE, TILE) // TILE * EDGE
    f32, bf16 = jnp.float32, jnp.bfloat16
    vmem = pl.BlockSpec(memory_space=pltpu.VMEM)
    anywhere = pl.BlockSpec(memory_space=pltpu.HBM)
    operands = (template, exposure[0], cosmic_mask[0], stamp_blocks, row_filters, col_filters)
    operands = [pltpu.with_memory_space_constraint(x, pltpu.HBM) for x in operands]
    diff, coef_row = pl.pallas_call(
        functools.partial(kernel, stripes, float(rows * stripes), radices, rounds),
        out_shape=(jax.ShapeDtypeStruct((tall, cols), f32), jax.ShapeDtypeStruct((1, fit), f32)),
        in_specs=[anywhere] * 6,
        out_specs=(vmem, vmem),
        scratch_shapes=[
            pltpu.VMEM((rows, half), f32),
            pltpu.VMEM((rows, cols), f32),
            pltpu.VMEM((rows, cols), jnp.int32),
            pltpu.SMEM(stamp_blocks.shape, jnp.int32),
            pltpu.VMEM((bases, taps), f32),
            pltpu.VMEM((bases, taps), f32),
            pltpu.VMEM((2, TILE, half + extra), f32),
            pltpu.VMEM((2, TILE, half + extra), f32),
            pltpu.VMEM((2, TILE, half + extra), f32),
            pltpu.VMEM((rows, half), f32),
            pltpu.VMEM((2, 2, cols), f32),
            pltpu.VMEM((2, 2, cols), f32),
            pltpu.VMEM((ext_rows, wide), f32),
            pltpu.VMEM((bases * rows, 2 * EDGE), f32),
            pltpu.VMEM((bases * tall, 2 * EDGE), f32),
            pltpu.VMEM((bases, EDGE, 2 * EDGE), bf16),
            pltpu.VMEM((bases, 2 * EDGE, 4 * EDGE), bf16),
            pltpu.VMEM((bases * rows, cols), f32),
            pltpu.VMEM((blocks, rows * pad_b, EDGE), f32),
            pltpu.VMEM((blocks, rows * TILE, EDGE), f32),
            pltpu.VMEM((blocks, rows, EDGE), f32),
            pltpu.VMEM((blocks, TILE, EDGE), f32),
            pltpu.VMEM((4, 3 * pad_b + TILE, EDGE), f32),
            pltpu.VMEM((bases * tall, wide), f32),
            pltpu.VMEM((bases, tiles * tall, EDGE), f32),
            pltpu.VMEM((fit, EDGE), f32),
            pltpu.VMEM((bases, tall + TILE, EDGE), f32),
            pltpu.VMEM((max(1, len(radices)), packed, EDGE), f32),
            pltpu.VMEM((slots, packed, EDGE), f32),
            pltpu.SemaphoreType.DMA((6,)),
            pltpu.SemaphoreType.DMA((7,)),
            pltpu.SemaphoreType.DMA((7,)),
            pltpu.SemaphoreType.DMA((slots,)),
            pltpu.SemaphoreType.DMA((slots,)),
            pltpu.SemaphoreType.REGULAR((max(1, rounds),)),
        ],
        compiler_params=pltpu.CompilerParams(
            collective_id=0, has_side_effects=True, vmem_limit_bytes=VMEM_GRANT
        ),
        name="fused",
    )(*operands)
    filtered, coef_row = pl.pallas_call(
        finish_kernel,
        out_shape=(jax.ShapeDtypeStruct((rows, cols), f32), jax.ShapeDtypeStruct((1, fit), f32)),
        in_specs=[vmem, vmem],
        out_specs=(vmem, vmem),
        compiler_params=pltpu.CompilerParams(vmem_limit_bytes=VMEM_GRANT),
        name="finish",
    )(diff, coef_row)
    return (filtered[None], coef_row)


def solution(mesh):
    placed = (
        P(("groups", "stripe"), "exp"),
        P(("groups", "exp"), "stripe", None),
        P(("groups", "exp"), "stripe", None),
        P(("groups", "stripe"), None),
        P(),
        P(),
    )
    return jax.shard_map(
        shards,
        mesh=mesh,
        in_specs=placed,
        out_specs=(P(("groups", "exp"), "stripe", None), P(("groups", "exp"), None)),
        check_vma=False,
    )
```

```python
import functools

import jax
import jax.numpy as jnp
from jax import lax
from jax.experimental import pallas as pl
from jax.experimental.pallas import tpu as pltpu
from jax.sharding import PartitionSpec as P

HALF = 9
STAMP_W = 64
EDGE = 128
TILE = 8
BLOCK = 8
REACH = HALF + 1
VMEM_GRANT = 32 * 1024 * 1024
GRAM_EARLY = 2
MESH = pl.DeviceIdType.MESH
LANE_DOT = (((1,), (1,)), ((), ()))


def round_up(n, m):
    return -(-n // m) * m


def row_coords(index, region_rows):
    return (2.0 * index + 1.0) / region_rows - 1.0


def col_coords(first, count, col_total):
    index = lax.broadcasted_iota(jnp.int32, (1, count), 1).astype(jnp.float32) + first
    return (2.0 * index + 1.0) / col_total - 1.0


def background(u, v):
    uu = 0.5 * (3.0 * u * u - 1.0)
    vv = 0.5 * (3.0 * v * v - 1.0)
    return [None, u, v, u * v, uu, vv, u * vv]


def split(x):
    high = x.astype(jnp.bfloat16)
    return high, (x - high.astype(jnp.float32)).astype(jnp.bfloat16)


def shifted_rows(row, count, start):
    return pltpu.roll(jnp.broadcast_to(row, (count, EDGE)), start, 1, stride=1, stride_axis=0)


def iotas(rows):
    return lax.broadcasted_iota(jnp.int32, (rows, EDGE), 0), lax.broadcasted_iota(jnp.int32, (rows, EDGE), 1)


def turn(x, shift, axis):
    return pltpu.roll(x, shift % x.shape[axis], axis)


def squeeze_terms(a, bases, axis):
    padded = round_up(bases, TILE)
    gap = padded - bases
    index = lax.broadcasted_iota(jnp.int32, a.shape, axis)
    out = a
    for t in range(1, 4):
        out = jnp.where(index >= t * bases, turn(a, -t * gap, axis), out)
    return out


def pack_normal(gram, fit):
    half = fit // 2
    rows = gram.shape[0]
    sub, lane = iotas(half)
    one = lane[0:1]
    upper, lower = gram[:half], gram[half:fit]
    merged = jnp.where((lane > sub) & (lane < half), turn(lower, -half, 1), upper)
    fold = half // 2
    body = jnp.where(lane[:fold] < fit, merged[:fold], turn(merged[fold:], fit, 1))
    diag = jnp.sum(jnp.where(lane == sub + half, lower, 0.0), axis=0, keepdims=True)
    last = jnp.where(one < fit, gram[fit : fit + 1], jnp.where(one < fit + half, turn(diag, half, 1), 0.0))
    return body, last


def unpack_normal(body, last, fit):
    half = fit // 2
    sub, lane = iotas(half)
    quad = jnp.concatenate([body, turn(body, fit, 1)], axis=0)
    tall = jnp.concatenate([quad, jnp.broadcast_to(last, (TILE, EDGE))], axis=0)
    flip = jnp.transpose(tall, (1, 0))[:fit]
    flip = jnp.concatenate([flip, jnp.zeros((fit, EDGE - flip.shape[1]), jnp.float32)], axis=1)
    side = turn(flip, half, 1)
    first, second = flip[:half], flip[half:]
    diag = jnp.broadcast_to(turn(last, -fit, 1), (half, EDGE))
    top = jnp.where(lane < half, jnp.where(lane <= sub, quad, first), jnp.where(lane < fit, quad, side[:half]))
    corner = jnp.where(lane > sub, quad, jnp.where(lane == sub, diag, first))
    low = jnp.where(lane < half, second, jnp.where(lane < fit, turn(corner, half, 1), side[half:]))
    return jnp.concatenate([top, low], axis=0)


def eliminate(a, fit):
    shape = (TILE, EDGE)
    count = fit // TILE
    tiles = [a[i * TILE : (i + 1) * TILE] for i in range(count)]
    sub = lax.broadcasted_iota(jnp.int32, shape, 0)
    for i in range(count):
        order = [j % count for j in range(i, i + count)]
        cols = {j: [jnp.broadcast_to(tiles[j][:, k : k + 1], shape) for k in range(i * TILE, (i + 1) * TILE)] for j in order}
        near = list(cols[i])
        for t in range(TILE):
            inverse = pl.reciprocal(near[t][t : t + 1])

            def step(x):
                row = x[t : t + 1] * inverse
                return jnp.where(sub == t, row, x - near[t] * row)

            for w in range(t + 1, TILE):
                near[w] = step(near[w])
            tiles[i] = step(tiles[i])
        for j in order[1:]:
            terms = [cols[j][t] * tiles[i][t : t + 1] for t in range(TILE)]
            while len(terms) > 1:
                terms = [terms[q] + terms[q + 1] for q in range(0, len(terms), 2)]
            tiles[j] = tiles[j] - terms[0]
    return jnp.concatenate([jnp.broadcast_to(x[:, fit : fit + 1], shape) for x in tiles], axis=0)


def kernel(
    count,
    region_rows,
    radices,
    rounds,
    tmpl_hbm,
    exp_hbm,
    mask_hbm,
    blk_hbm,
    rowf_hbm,
    colf_hbm,
    diff,
    row_ref,
    tmpl_ref,
    exp_ref,
    mask_ref,
    blk_ref,
    rowf_ref,
    colf_ref,
    halo_send,
    halo_own,
    halo_other,
    whole,
    edge_send,
    edge_recv,
    ext_ref,
    bandw,
    bandf,
    toep_s,
    toep_f,
    vert,
    design,
    ground,
    clear,
    across_u,
    grams,
    vert_f,
    basis,
    coef_ref,
    plane,
    send,
    held,
    load_sem,
    halo_ss,
    halo_rs,
    red_ss,
    red_rs,
    hello,
):
    me = lax.axis_index("stripe")
    core = lax.axis_index("exp")
    rows, half = tmpl_ref.shape
    cols = exp_ref.shape[1]
    bases, taps = rowf_ref.shape
    fit = 3 * bases + 7
    pad_b = round_up(bases, TILE)
    ext_rows, wide = ext_ref.shape
    tall = diff.shape[0]
    half_cols = cols // 2
    blocks = half_cols // EDGE
    stamps = 2 * blocks
    tiles = cols // EDGE
    has_up = me > 0
    has_down = me < count - 1
    up_count = has_up.astype(jnp.int32)
    down_count = has_down.astype(jnp.int32)

    barrier = pltpu.get_barrier_semaphore()

    def greet(sem, stripe, exp):
        pl.semaphore_signal(sem, inc=1, device_id={"stripe": stripe, "exp": exp}, device_id_type=MESH)

    @pl.when(has_up)
    def _():
        greet(barrier, me - 1, core)

    @pl.when(has_down)
    def _():
        greet(barrier, me + 1, core)

    greet(barrier, me, 1 - core)

    loads = [
        pltpu.make_async_copy(src, dst, load_sem.at[n])
        for n, (src, dst) in enumerate(
            (
                (tmpl_hbm, tmpl_ref),
                (exp_hbm, exp_ref),
                (mask_hbm, mask_ref),
                (blk_hbm, blk_ref),
                (rowf_hbm, rowf_ref),
                (colf_hbm, colf_ref),
            )
        )
    ]
    for c in loads:
        c.start()

    ext_ref[...] = jnp.zeros_like(ext_ref)

    @pl.when(jnp.logical_not(has_up))
    def _():
        halo_own[0] = jnp.zeros_like(halo_own[0])
        halo_other[0] = jnp.zeros_like(halo_other[0])
        edge_recv[0] = jnp.zeros_like(edge_recv[0])

    @pl.when(jnp.logical_not(has_down))
    def _():
        halo_own[1] = jnp.zeros_like(halo_own[1])
        halo_other[1] = jnp.zeros_like(halo_other[1])
        edge_recv[1] = jnp.zeros_like(edge_recv[1])

    def copy(src, dst, n, stripe, exp):
        return pltpu.make_async_remote_copy(
            src_ref=src,
            dst_ref=dst,
            send_sem=halo_ss.at[n],
            recv_sem=halo_rs.at[n],
            device_id={"stripe": stripe, "exp": exp},
            device_id_type=MESH,
        )

    def halo(way):
        return copy(halo_send.at[way], halo_own.at[way], way, me + 1 - 2 * way, core)

    def edge(way):
        return copy(edge_send.at[way], edge_recv.at[way], 2 + way, me + 1 - 2 * way, core)

    def relay(way):
        return copy(halo_own.at[way], halo_other.at[way], 4 + way, me, 1 - core)

    more = REACH - TILE
    spans = half // EDGE
    for c in loads:
        c.wait()
    for way, near, far in ((0, rows - TILE, rows - REACH), (1, 0, TILE)):
        halo_send[way, :, 0:half] = tmpl_ref[near : near + TILE]
        for e in range(more):
            for m in range(spans):
                column, line = half + (e * spans + m) // TILE * EDGE, (e * spans + m) % TILE
                halo_send[way, line : line + 1, column : column + EDGE] = tmpl_ref[
                    far + e : far + e + 1, m * EDGE : (m + 1) * EDGE
                ]
    edge_send[0, 0:1, :] = exp_ref[rows - 1 : rows, :]
    edge_send[0, 1:2, :] = mask_ref[rows - 1 : rows, :].astype(jnp.float32)
    edge_send[1, 0:1, :] = exp_ref[0:1, :]
    edge_send[1, 1:2, :] = mask_ref[0:1, :].astype(jnp.float32)

    pl.semaphore_wait(barrier, 1 + up_count + down_count)

    @pl.when(has_down)
    def _():
        halo(0).start()

    @pl.when(has_up)
    def _():
        halo(1).start()

    across = copy(tmpl_ref, whole, 6, me, 1 - core)
    across.start()

    def call(n):
        reach = 1 << n

        @pl.when(me >= reach)
        def _():
            greet(hello.at[n], me - reach, core)

        @pl.when(me + reach < count)
        def _():
            greet(hello.at[n], me + reach, core)

    def listen(n):
        reach = 1 << n
        heard = (me >= reach).astype(jnp.int32) + (me + reach < count).astype(jnp.int32)
        pl.semaphore_wait(hello.at[n], heard)

    if rounds:
        call(0)

    lanes = jnp.zeros((1, EDGE - taps), jnp.float32)
    low = lax.broadcasted_iota(jnp.int32, (1, EDGE), 1) < STAMP_W
    parity = [blk_ref[0, s] % 2 == 1 for s in range(stamps)]

    def pick(x):
        parts = []
        for m in range(blocks):
            a = x[:, 2 * m * EDGE : (2 * m + 1) * EDGE]
            b = x[:, (2 * m + 1) * EDGE : (2 * m + 2) * EDGE]
            a = jnp.where(parity[2 * m], pltpu.roll(a, STAMP_W, 1), a)
            b = jnp.where(parity[2 * m + 1], b, pltpu.roll(b, STAMP_W, 1))
            parts.append(jnp.where(low, a, b))
        return jnp.concatenate(parts, axis=1)

    start = ext_rows // 2 - rows // 2 - HALF
    sub_e, lane_e = iotas(EDGE)
    sub_t = lax.broadcasted_iota(jnp.int32, (TILE, EDGE), 0)
    for b in range(bases):
        row = jnp.concatenate([rowf_ref[b : b + 1, :], lanes], axis=1)
        high = row.astype(jnp.bfloat16).astype(jnp.float32)

        def placed(x, offset):
            body = shifted_rows(x, rows + TILE, start + offset)
            above = pltpu.roll(jnp.broadcast_to(x, (TILE, EDGE)), start + offset - 1, 1)
            tail = jnp.where(sub_t == TILE - 1, above, body[rows:])
            return body[:rows], jnp.concatenate([body[:rows], tail], axis=0)

        (h0, h0f), (h1, h1f), (r0, r0f) = placed(high, 0), placed(high, ext_rows), placed(row - high, 0)
        bandw[b * rows : (b + 1) * rows, :] = jnp.concatenate([h0 + h1, r0], axis=1)
        bandf[b * tall : (b + 1) * tall, :] = jnp.concatenate([h0f + h1f, r0f], axis=1)
        row = jnp.concatenate([colf_ref[b : b + 1, :], lanes], axis=1)
        spread = shifted_rows(row, EDGE, 0)
        t_high, t_rest = split(spread[:STAMP_W])
        upper = jnp.concatenate([t_high, t_high], axis=1)
        lower = jnp.concatenate([t_rest, jnp.zeros_like(t_rest)], axis=1)
        toep_s[b] = jnp.concatenate([upper, lower], axis=0)
        inside = jnp.where(lane_e >= sub_e, spread, 0.0)
        f_high, f_rest = split(jnp.concatenate([inside, spread - inside], axis=1))
        upper = jnp.concatenate([f_high, f_high], axis=1)
        lower = jnp.concatenate([f_rest, jnp.zeros_like(f_rest)], axis=1)
        toep_f[b] = jnp.concatenate([upper, lower], axis=0)

    if rounds:
        listen(0)
    if rounds > 1:
        call(1)

    first = (me * rows).astype(jnp.float32)
    index = lax.broadcasted_iota(jnp.int32, (rows, 1), 0).astype(jnp.float32)
    v = jnp.broadcast_to(row_coords(index + first, region_rows), (rows, half_cols))
    u_all = jnp.broadcast_to(col_coords(0.0, cols, cols), (TILE, cols))
    u_sel = pick(u_all)
    u = jnp.concatenate([u_sel] * (rows // TILE), axis=0)
    good = pick(mask_ref[...].astype(jnp.float32))
    for m in range(blocks):
        clear[m] = good[:, m * EDGE : (m + 1) * EDGE]
        across_u[m] = u_sel[:, m * EDGE : (m + 1) * EDGE]
    terms = background(u, v)
    terms[0] = jnp.ones_like(u)
    terms.append(pick(exp_ref[...]))
    for k, term in enumerate(terms):
        x = term * good
        for m in range(blocks):
            ground[m, pl.ds(k, rows, stride=TILE), :] = x[:, m * EDGE : (m + 1) * EDGE]
    zero = jnp.zeros((rows, EDGE), jnp.float32)
    for b in range(bases, pad_b):
        for m in range(blocks):
            design[m, pl.ds(b, rows, stride=pad_b), :] = zero

    @pl.when(has_up)
    def _():
        halo(0).wait_recv()
        relay(0).start()

    @pl.when(has_down)
    def _():
        halo(1).wait_recv()
        relay(1).start()

    def settle(side, body, buf):
        where = pl.ds(pl.multiple_of(EDGE + side * half, EDGE), half)
        ext_ref[rows : 2 * rows, where] = body[...]
        for way, near, far in ((0, rows - TILE, rows - REACH), (1, 2 * rows, 2 * rows + TILE)):
            ext_ref[near : near + TILE, where] = buf[way, :, 0:half]
            for e in range(more):
                for m in range(spans):
                    column, line = half + (e * spans + m) // TILE * EDGE, (e * spans + m) % TILE
                    at = pl.ds(pl.multiple_of((1 + m) * EDGE + side * half, EDGE), EDGE)
                    ext_ref[far + e : far + e + 1, at] = buf[way, line : line + 1, column : column + EDGE]

    def stack(x):
        high, rest = split(x)
        gap = jnp.zeros((EDGE - 2 * ext_rows, x.shape[1]), jnp.bfloat16)
        gap2 = jnp.zeros((EDGE - ext_rows, x.shape[1]), jnp.bfloat16)
        return jnp.concatenate([high, rest, gap, high, gap2], axis=0)

    total = 3 * pad_b + TILE

    def stamp_design(first_block, n, place):
        span = 2 * n * EDGE
        at = pl.multiple_of(first_block * 2 * EDGE, EDGE)
        ext = turn(ext_ref[:, pl.ds(at, span + 2 * EDGE)], -(EDGE - HALF), 1)
        windows = []
        for s in range(2 * n):
            odd = blk_ref[0, 2 * first_block + s] % 2 == 1
            early = ext[:, s * EDGE : (s + 1) * EDGE]
            after = ext[:, (s + 1) * EDGE : (s + 2) * EDGE]
            late = pltpu.roll(jnp.where(low, after, early), STAMP_W, 1)
            windows.append(jnp.where(odd, late, early))
        window = jnp.concatenate(windows, axis=1)
        vert[:, :span] = jnp.dot(bandw[...].astype(jnp.bfloat16), stack(window), preferred_element_type=jnp.float32)
        for b in range(bases):
            x = vert[b * rows : (b + 1) * rows, :span]
            x = jnp.concatenate([x[:, s * EDGE : (s + 1) * EDGE] for s in range(2 * n)], axis=0)
            y = lax.dot_general(
                jnp.concatenate(split(x), axis=1), toep_s[b], LANE_DOT, preferred_element_type=jnp.float32
            )
            for m in range(n):
                near, far = y[2 * m * rows : (2 * m + 1) * rows], y[(2 * m + 1) * rows : (2 * m + 2) * rows]
                picked = jnp.where(low, near, far) + pltpu.roll(jnp.where(low, far, near), STAMP_W, 1)
                design[place + m, pl.ds(b, rows, stride=pad_b), :] = picked * clear[first_block + m]

    def stamp_gram(first_block, n, place, pairs, slot):
        sums = [jnp.zeros((total, total), jnp.float32) for _ in range(2)]
        for pair in pairs:
            parts = []
            for r in (2 * pair, 2 * pair + 1):
                vm = v[r : r + 1, 0:EDGE]
                for m in range(n):
                    d = design[place + m, r * pad_b : (r + 1) * pad_b, :]
                    um = across_u[first_block + m, 0:1]
                    rest = ground[first_block + m, r * TILE : (r + 1) * TILE, :]
                    parts.append(jnp.concatenate([d, d * um, d * vm, rest], axis=0))
            x = jnp.concatenate(parts, axis=1).astype(jnp.bfloat16)
            sums[pair % 2] = sums[pair % 2] + lax.dot_general(x, x, LANE_DOT, preferred_element_type=jnp.float32)
        for h in range(2):
            grams[slot + h, :, 0:total] = sums[h]

    settle(core, tmpl_ref, halo_own)
    ahead = blocks // 2 - 1
    pairs = range(rows // 2)
    near_block, far_block = core * (blocks - ahead), (1 - core) * ahead
    if ahead:
        stamp_design(near_block, ahead, 0)
        stamp_gram(near_block, ahead, 0, pairs[:GRAM_EARLY], 0)
    if rounds > 1:
        listen(1)
    if rounds > 2:
        call(2)
    across.wait_recv()

    @pl.when(has_up)
    def _():
        relay(0).wait_recv()

    @pl.when(has_down)
    def _():
        relay(1).wait_recv()

    settle(1 - core, whole, halo_other)
    if ahead:
        stamp_gram(near_block, ahead, 0, pairs[GRAM_EARLY:], 2)
    stamp_design(far_block, blocks - ahead, ahead)
    stamp_gram(far_block, blocks - ahead, ahead, pairs, 4)
    @pl.when(has_down)
    def _():
        edge(0).start()

    @pl.when(has_up)
    def _():
        edge(1).start()

    acc = grams[4, :, 0:total] + grams[5, :, 0:total]
    if ahead:
        acc = acc + ((grams[0, :, 0:total] + grams[1, :, 0:total]) + (grams[2, :, 0:total] + grams[3, :, 0:total]))
    gram = jnp.concatenate([acc, jnp.zeros((total, EDGE - total), jnp.float32)], axis=1)
    gram = squeeze_terms(squeeze_terms(gram, bases, 0), bases, 1)
    body, last = pack_normal(gram, fit)
    for n in range(2, rounds):
        listen(n)
        if n + 1 < rounds:
            call(n + 1)

    def reduce_start(phase, base, stride, radix):
        digit = (me // stride) % radix
        copies = []
        for k in range(radix - 1, 0, -1):
            other = digit * 0
            for bit in range((radix - 1).bit_length()):
                on = (digit // (1 << bit)) % 2
                other = other + ((1 - on) if (k >> bit) & 1 else on) * (1 << bit)
            copies.append(
                pltpu.make_async_remote_copy(
                    src_ref=send.at[phase],
                    dst_ref=held.at[base + k - 1],
                    send_sem=red_ss.at[base + k - 1],
                    recv_sem=red_rs.at[base + k - 1],
                    device_id={"stripe": me + (other - digit) * stride},
                    device_id_type=MESH,
                )
            )
        for c in copies:
            c.start()
        return copies

    fold = body.shape[0]

    def put(phase, parts):
        send[phase, 0:fold] = parts[0]
        send[phase, fold : fold + 1] = parts[1]

    def tree(values):
        while len(values) > 1:
            values = [values[q] + values[q + 1] for q in range(0, len(values), 2)]
        return values[0]

    base, stride, flying = 0, 1, []
    for phase, radix in enumerate(radices):
        put(phase, (body, last))
        copies = reduce_start(phase, base, stride, radix)
        flying += copies
        if phase == 0:
            vert_f[...] = jnp.dot(
                bandf[...].astype(jnp.bfloat16), stack(turn(ext_ref[...], -(EDGE - HALF), 1)), preferred_element_type=jnp.float32
            )
            for b in range(bases):
                x = vert_f[b * tall : (b + 1) * tall, :]
                x = jnp.concatenate([x[:, m * EDGE : (m + 2) * EDGE] for m in range(tiles)], axis=0)
                y = lax.dot_general(
                    jnp.concatenate(split(x), axis=1), toep_f[b], LANE_DOT, preferred_element_type=jnp.float32
                )
                basis[b] = y[:, :EDGE] + y[:, EDGE:]
        for c in copies:
            c.wait_recv()
        body = tree([send[phase, 0:fold]] + [held[base + k, 0:fold] for k in range(radix - 1)])
        last = tree([send[phase, fold : fold + 1]] + [held[base + k, fold : fold + 1] for k in range(radix - 1)])
        base += radix - 1
        stride *= radix

    answer = eliminate(unpack_normal(body, last, fit), fit)
    coef_ref[...] = answer
    n = lax.broadcasted_iota(jnp.int32, (fit, fit), 0)
    term = (n >= bases).astype(jnp.int32) + (n >= 2 * bases).astype(jnp.int32)
    spot = jnp.where(n < 3 * bases, 3 * (n - bases * term) + term, n)
    same = spot == lax.broadcasted_iota(jnp.int32, (fit, fit), 1)
    row_ref[...] = jnp.sum(jnp.where(same, answer[:, :fit], 0.0), axis=0, keepdims=True)

    for c in (0, 1):
        @pl.when((has_up, has_down)[c])
        def _():
            edge(c).wait_recv()

    def coef(n):
        return coef_ref[pl.ds(n, TILE, stride=0), :]

    def three(x):
        return jnp.concatenate([x] * (tall // TILE), axis=0)

    place = lax.broadcasted_iota(jnp.int32, (tall, EDGE), 0)
    place = jnp.where(place == tall - 1, -1, place).astype(jnp.float32)
    v = row_coords(place + first, region_rows)
    vv = 0.5 * (3.0 * v * v - 1.0)
    for b in range(bases):
        plane[b, 0:tall] = three(coef(b)) + v * three(coef(2 * bases + b))
        plane[b, tall : tall + TILE] = coef(bases + b)
    q = [coef(3 * bases + k) for k in range(7)]
    flat = three(q[0]) + v * three(q[2]) + vv * three(q[5])
    slope = three(q[1]) + v * three(q[3]) + vv * three(q[6])
    u_all = col_coords(0.0, cols, cols)
    spare = jnp.zeros((tall - rows - 2, EDGE), jnp.float32)
    for m in range(tiles):
        at = slice(m * EDGE, (m + 1) * EDGE)
        um = jnp.broadcast_to(u_all[:, at], (TILE, EDGE))
        uu = 0.5 * (3.0 * um * um - 1.0)
        model = flat + three(um) * slope + three(q[4] * uu)
        for b in range(bases):
            factor = plane[b, 0:tall] + three(um * plane[b, tall : tall + TILE])
            model = model + factor * basis[b, m * tall : (m + 1) * tall]
        science = jnp.concatenate([exp_ref[:, at], edge_recv[1, 0:1, at], spare, edge_recv[0, 0:1, at]], axis=0)
        clean = jnp.concatenate(
            [mask_ref[:, at].astype(jnp.float32), edge_recv[1, 1:2, at], spare, edge_recv[0, 1:2, at]], axis=0
        )
        diff[:, at] = clean * (science - model)

    across.wait_send()
    for c in flying:
        c.wait_send()

    @pl.when(has_down)
    def _():
        halo(0).wait_send()
        edge(0).wait_send()
        relay(1).wait_send()

    @pl.when(has_up)
    def _():
        halo(1).wait_send()
        edge(1).wait_send()
        relay(0).wait_send()


def finish_kernel(diff_ref, coef_ref, out_ref, row_ref):
    rows, cols = out_ref.shape
    lane = lax.broadcasted_iota(jnp.int32, (rows, cols), 1)
    every = diff_ref[...]
    mid = every[:rows]
    left = jnp.where(lane == 0, 0.0, turn(mid, 1, 1))
    right = jnp.where(lane == cols - 1, 0.0, turn(mid, -1, 1))
    around = turn(every, -1, 0)[:rows] + turn(every, 1, 0)[:rows] + right + left
    out_ref[...] = 4.0 * mid - around
    row_ref[...] = coef_ref[...]


def shards(template, exposure, cosmic_mask, stamp_blocks, row_filters, col_filters):
    rows, cols = exposure.shape[1:]
    bases, taps = row_filters.shape
    fit = 3 * bases + 7
    stripes = lax.axis_size("stripe")
    half = template.shape[1]
    ext_rows = 3 * rows
    wide = cols + 2 * EDGE
    tall = round_up(rows + 2, TILE)
    pad_b = round_up(bases, TILE)
    blocks = cols // (2 * EDGE)
    tiles = cols // EDGE
    radices = []
    rest = stripes
    while rest > 1:
        radices.append(min(rest, 8))
        rest //= radices[-1]
    slots = max(1, sum(r - 1 for r in radices))
    rounds = (stripes - 2).bit_length() if stripes > 2 else 0
    packed = fit // 4 + 1
    extra = round_up((REACH - TILE) * half // EDGE, TILE) // TILE * EDGE
    f32, bf16 = jnp.float32, jnp.bfloat16
    vmem = pl.BlockSpec(memory_space=pltpu.VMEM)
    anywhere = pl.BlockSpec(memory_space=pltpu.HBM)
    operands = (template, exposure[0], cosmic_mask[0], stamp_blocks, row_filters, col_filters)
    operands = [pltpu.with_memory_space_constraint(x, pltpu.HBM) for x in operands]
    diff, coef_row = pl.pallas_call(
        functools.partial(kernel, stripes, float(rows * stripes), radices, rounds),
        out_shape=(jax.ShapeDtypeStruct((tall, cols), f32), jax.ShapeDtypeStruct((1, fit), f32)),
        in_specs=[anywhere] * 6,
        out_specs=(vmem, vmem),
        scratch_shapes=[
            pltpu.VMEM((rows, half), f32),
            pltpu.VMEM((rows, cols), f32),
            pltpu.VMEM((rows, cols), jnp.int32),
            pltpu.SMEM(stamp_blocks.shape, jnp.int32),
            pltpu.VMEM((bases, taps), f32),
            pltpu.VMEM((bases, taps), f32),
            pltpu.VMEM((2, TILE, half + extra), f32),
            pltpu.VMEM((2, TILE, half + extra), f32),
            pltpu.VMEM((2, TILE, half + extra), f32),
            pltpu.VMEM((rows, half), f32),
            pltpu.VMEM((2, 2, cols), f32),
            pltpu.VMEM((2, 2, cols), f32),
            pltpu.VMEM((ext_rows, wide), f32),
            pltpu.VMEM((bases * rows, 2 * EDGE), f32),
            pltpu.VMEM((bases * tall, 2 * EDGE), f32),
            pltpu.VMEM((bases, EDGE, 2 * EDGE), bf16),
            pltpu.VMEM((bases, 2 * EDGE, 4 * EDGE), bf16),
            pltpu.VMEM((bases * rows, cols), f32),
            pltpu.VMEM((blocks, rows * pad_b, EDGE), f32),
            pltpu.VMEM((blocks, rows * TILE, EDGE), f32),
            pltpu.VMEM((blocks, rows, EDGE), f32),
            pltpu.VMEM((blocks, TILE, EDGE), f32),
            pltpu.VMEM((6, 3 * pad_b + TILE, EDGE), f32),
            pltpu.VMEM((bases * tall, wide), f32),
            pltpu.VMEM((bases, tiles * tall, EDGE), f32),
            pltpu.VMEM((fit, EDGE), f32),
            pltpu.VMEM((bases, tall + TILE, EDGE), f32),
            pltpu.VMEM((max(1, len(radices)), packed, EDGE), f32),
            pltpu.VMEM((slots, packed, EDGE), f32),
            pltpu.SemaphoreType.DMA((6,)),
            pltpu.SemaphoreType.DMA((7,)),
            pltpu.SemaphoreType.DMA((7,)),
            pltpu.SemaphoreType.DMA((slots,)),
            pltpu.SemaphoreType.DMA((slots,)),
            pltpu.SemaphoreType.REGULAR((max(1, rounds),)),
        ],
        compiler_params=pltpu.CompilerParams(
            collective_id=0, has_side_effects=True, vmem_limit_bytes=VMEM_GRANT
        ),
        name="fused",
    )(*operands)
    filtered, coef_row = pl.pallas_call(
        finish_kernel,
        out_shape=(jax.ShapeDtypeStruct((rows, cols), f32), jax.ShapeDtypeStruct((1, fit), f32)),
        in_specs=[vmem, vmem],
        out_specs=(vmem, vmem),
        compiler_params=pltpu.CompilerParams(vmem_limit_bytes=VMEM_GRANT),
        name="finish",
    )(diff, coef_row)
    return (filtered[None], coef_row)


def solution(mesh):
    placed = (
        P(("groups", "stripe"), "exp"),
        P(("groups", "exp"), "stripe", None),
        P(("groups", "exp"), "stripe", None),
        P(("groups", "stripe"), None),
        P(),
        P(),
    )
    return jax.shard_map(
        shards,
        mesh=mesh,
        in_specs=placed,
        out_specs=(P(("groups", "exp"), "stripe", None), P(("groups", "exp"), None)),
        check_vma=False,
    )
```

```python
import functools

import jax
import jax.numpy as jnp
from jax import lax
from jax.experimental import pallas as pl
from jax.experimental.pallas import tpu as pltpu
from jax.sharding import PartitionSpec as P

HALF = 9
STAMP_W = 64
EDGE = 128
TILE = 8
BLOCK = 8
REACH = HALF + 1
VMEM_GRANT = 32 * 1024 * 1024
GRAM_EARLY = 2
MESH = pl.DeviceIdType.MESH
LANE_DOT = (((1,), (1,)), ((), ()))


def round_up(n, m):
    return -(-n // m) * m


def row_coords(index, region_rows):
    return (2.0 * index + 1.0) / region_rows - 1.0


def col_coords(first, count, col_total):
    index = lax.broadcasted_iota(jnp.int32, (1, count), 1).astype(jnp.float32) + first
    return (2.0 * index + 1.0) / col_total - 1.0


def background(u, v):
    uu = 0.5 * (3.0 * u * u - 1.0)
    vv = 0.5 * (3.0 * v * v - 1.0)
    return [None, u, v, u * v, uu, vv, u * vv]


def split(x):
    high = x.astype(jnp.bfloat16)
    return high, (x - high.astype(jnp.float32)).astype(jnp.bfloat16)


def shifted_rows(row, count, start):
    return pltpu.roll(jnp.broadcast_to(row, (count, EDGE)), start, 1, stride=1, stride_axis=0)


def iotas(rows):
    return lax.broadcasted_iota(jnp.int32, (rows, EDGE), 0), lax.broadcasted_iota(jnp.int32, (rows, EDGE), 1)


def turn(x, shift, axis):
    return pltpu.roll(x, shift % x.shape[axis], axis)


def squeeze_terms(a, bases, axis):
    padded = round_up(bases, TILE)
    gap = padded - bases
    index = lax.broadcasted_iota(jnp.int32, a.shape, axis)
    out = a
    for t in range(1, 4):
        out = jnp.where(index >= t * bases, turn(a, -t * gap, axis), out)
    return out


def pack_normal(gram, fit):
    half = fit // 2
    rows = gram.shape[0]
    sub, lane = iotas(half)
    one = lane[0:1]
    upper, lower = gram[:half], gram[half:fit]
    merged = jnp.where((lane > sub) & (lane < half), turn(lower, -half, 1), upper)
    fold = half // 2
    body = jnp.where(lane[:fold] < fit, merged[:fold], turn(merged[fold:], fit, 1))
    diag = jnp.sum(jnp.where(lane == sub + half, lower, 0.0), axis=0, keepdims=True)
    last = jnp.where(one < fit, gram[fit : fit + 1], jnp.where(one < fit + half, turn(diag, half, 1), 0.0))
    return body, last


def unpack_normal(body, last, fit):
    half = fit // 2
    sub, lane = iotas(half)
    quad = jnp.concatenate([body, turn(body, fit, 1)], axis=0)
    tall = jnp.concatenate([quad, jnp.broadcast_to(last, (TILE, EDGE))], axis=0)
    flip = jnp.transpose(tall, (1, 0))[:fit]
    flip = jnp.concatenate([flip, jnp.zeros((fit, EDGE - flip.shape[1]), jnp.float32)], axis=1)
    side = turn(flip, half, 1)
    first, second = flip[:half], flip[half:]
    diag = jnp.broadcast_to(turn(last, -fit, 1), (half, EDGE))
    top = jnp.where(lane < half, jnp.where(lane <= sub, quad, first), jnp.where(lane < fit, quad, side[:half]))
    corner = jnp.where(lane > sub, quad, jnp.where(lane == sub, diag, first))
    low = jnp.where(lane < half, second, jnp.where(lane < fit, turn(corner, half, 1), side[half:]))
    return jnp.concatenate([top, low], axis=0)


def eliminate(a, fit):
    shape = (TILE, EDGE)
    count = fit // TILE
    tiles = [a[i * TILE : (i + 1) * TILE] for i in range(count)]
    sub = lax.broadcasted_iota(jnp.int32, shape, 0)
    for i in range(count):
        order = [j % count for j in range(i, i + count)]
        cols = {j: [jnp.broadcast_to(tiles[j][:, k : k + 1], shape) for k in range(i * TILE, (i + 1) * TILE)] for j in order}
        near = list(cols[i])
        for t in range(TILE):
            inverse = pl.reciprocal(near[t][t : t + 1])

            def step(x):
                row = x[t : t + 1] * inverse
                return jnp.where(sub == t, row, x - near[t] * row)

            for w in range(t + 1, TILE):
                near[w] = step(near[w])
            tiles[i] = step(tiles[i])
        for j in order[1:]:
            terms = [cols[j][t] * tiles[i][t : t + 1] for t in range(TILE)]
            while len(terms) > 1:
                terms = [terms[q] + terms[q + 1] for q in range(0, len(terms), 2)]
            tiles[j] = tiles[j] - terms[0]
    return jnp.concatenate([jnp.broadcast_to(x[:, fit : fit + 1], shape) for x in tiles], axis=0)


def kernel(
    count,
    region_rows,
    radices,
    rounds,
    tmpl_hbm,
    exp_hbm,
    mask_hbm,
    blk_hbm,
    rowf_hbm,
    colf_hbm,
    diff,
    row_ref,
    tmpl_ref,
    exp_ref,
    mask_ref,
    blk_ref,
    rowf_ref,
    colf_ref,
    halo_send,
    halo_own,
    halo_other,
    whole,
    edge_send,
    edge_recv,
    ext_ref,
    bandw,
    bandf,
    toep_s,
    toep_f,
    vert,
    design,
    ground,
    clear,
    across_u,
    grams,
    vert_f,
    basis,
    coef_ref,
    plane,
    clean_ref,
    send,
    held,
    load_sem,
    halo_ss,
    halo_rs,
    red_ss,
    red_rs,
    hello,
):
    me = lax.axis_index("stripe")
    core = lax.axis_index("exp")
    rows, half = tmpl_ref.shape
    cols = exp_ref.shape[1]
    bases, taps = rowf_ref.shape
    fit = 3 * bases + 7
    pad_b = round_up(bases, TILE)
    ext_rows, wide = ext_ref.shape
    tall = diff.shape[0]
    half_cols = cols // 2
    blocks = half_cols // EDGE
    stamps = 2 * blocks
    tiles = cols // EDGE
    has_up = me > 0
    has_down = me < count - 1
    up_count = has_up.astype(jnp.int32)
    down_count = has_down.astype(jnp.int32)

    barrier = pltpu.get_barrier_semaphore()

    def greet(sem, stripe, exp):
        pl.semaphore_signal(sem, inc=1, device_id={"stripe": stripe, "exp": exp}, device_id_type=MESH)

    @pl.when(has_up)
    def _():
        greet(barrier, me - 1, core)

    @pl.when(has_down)
    def _():
        greet(barrier, me + 1, core)

    greet(barrier, me, 1 - core)

    loads = [
        pltpu.make_async_copy(src, dst, load_sem.at[n])
        for n, (src, dst) in enumerate(
            (
                (tmpl_hbm, tmpl_ref),
                (exp_hbm, exp_ref),
                (mask_hbm, mask_ref),
                (blk_hbm, blk_ref),
                (rowf_hbm, rowf_ref),
                (colf_hbm, colf_ref),
            )
        )
    ]
    for c in loads:
        c.start()

    ext_ref[...] = jnp.zeros_like(ext_ref)

    @pl.when(jnp.logical_not(has_up))
    def _():
        halo_own[0] = jnp.zeros_like(halo_own[0])
        halo_other[0] = jnp.zeros_like(halo_other[0])
        edge_recv[0] = jnp.zeros_like(edge_recv[0])

    @pl.when(jnp.logical_not(has_down))
    def _():
        halo_own[1] = jnp.zeros_like(halo_own[1])
        halo_other[1] = jnp.zeros_like(halo_other[1])
        edge_recv[1] = jnp.zeros_like(edge_recv[1])

    def copy(src, dst, n, stripe, exp):
        return pltpu.make_async_remote_copy(
            src_ref=src,
            dst_ref=dst,
            send_sem=halo_ss.at[n],
            recv_sem=halo_rs.at[n],
            device_id={"stripe": stripe, "exp": exp},
            device_id_type=MESH,
        )

    def halo(way):
        return copy(halo_send.at[way], halo_own.at[way], way, me + 1 - 2 * way, core)

    def edge(way):
        return copy(edge_send.at[way], edge_recv.at[way], 2 + way, me + 1 - 2 * way, core)

    def relay(way):
        return copy(halo_own.at[way], halo_other.at[way], 4 + way, me, 1 - core)

    more = REACH - TILE
    spans = half // EDGE
    for c in loads:
        c.wait()
    for way, near, far in ((0, rows - TILE, rows - REACH), (1, 0, TILE)):
        halo_send[way, :, 0:half] = tmpl_ref[near : near + TILE]
        for e in range(more):
            for m in range(spans):
                column, line = half + (e * spans + m) // TILE * EDGE, (e * spans + m) % TILE
                halo_send[way, line : line + 1, column : column + EDGE] = tmpl_ref[
                    far + e : far + e + 1, m * EDGE : (m + 1) * EDGE
                ]
    edge_send[0, 0:1, :] = exp_ref[rows - 1 : rows, :]
    edge_send[0, 1:2, :] = mask_ref[rows - 1 : rows, :].astype(jnp.float32)
    edge_send[1, 0:1, :] = exp_ref[0:1, :]
    edge_send[1, 1:2, :] = mask_ref[0:1, :].astype(jnp.float32)

    pl.semaphore_wait(barrier, 1 + up_count + down_count)

    @pl.when(has_down)
    def _():
        halo(0).start()

    @pl.when(has_up)
    def _():
        halo(1).start()

    across = copy(tmpl_ref, whole, 6, me, 1 - core)
    across.start()

    def call(n):
        reach = 1 << n

        @pl.when(me >= reach)
        def _():
            greet(hello.at[n], me - reach, core)

        @pl.when(me + reach < count)
        def _():
            greet(hello.at[n], me + reach, core)

    def listen(n):
        reach = 1 << n
        heard = (me >= reach).astype(jnp.int32) + (me + reach < count).astype(jnp.int32)
        pl.semaphore_wait(hello.at[n], heard)

    if rounds:
        call(0)

    lanes = jnp.zeros((1, EDGE - taps), jnp.float32)
    low = lax.broadcasted_iota(jnp.int32, (1, EDGE), 1) < STAMP_W
    parity = [blk_ref[0, s] % 2 == 1 for s in range(stamps)]

    def pick(x):
        parts = []
        for m in range(blocks):
            a = x[:, 2 * m * EDGE : (2 * m + 1) * EDGE]
            b = x[:, (2 * m + 1) * EDGE : (2 * m + 2) * EDGE]
            a = jnp.where(parity[2 * m], pltpu.roll(a, STAMP_W, 1), a)
            b = jnp.where(parity[2 * m + 1], b, pltpu.roll(b, STAMP_W, 1))
            parts.append(jnp.where(low, a, b))
        return jnp.concatenate(parts, axis=1)

    start = ext_rows // 2 - rows // 2 - HALF
    sub_e, lane_e = iotas(EDGE)
    sub_t = lax.broadcasted_iota(jnp.int32, (TILE, EDGE), 0)
    for b in range(bases):
        row = jnp.concatenate([rowf_ref[b : b + 1, :], lanes], axis=1)
        high = row.astype(jnp.bfloat16).astype(jnp.float32)

        def placed(x, offset):
            body = shifted_rows(x, rows + TILE, start + offset)
            above = pltpu.roll(jnp.broadcast_to(x, (TILE, EDGE)), start + offset - 1, 1)
            tail = jnp.where(sub_t == TILE - 1, above, body[rows:])
            return body[:rows], jnp.concatenate([body[:rows], tail], axis=0)

        (h0, h0f), (h1, h1f), (r0, r0f) = placed(high, 0), placed(high, ext_rows), placed(row - high, 0)
        bandw[b * rows : (b + 1) * rows, :] = jnp.concatenate([h0 + h1, r0], axis=1)
        bandf[b * tall : (b + 1) * tall, :] = jnp.concatenate([h0f + h1f, r0f], axis=1)
        row = jnp.concatenate([colf_ref[b : b + 1, :], lanes], axis=1)
        spread = shifted_rows(row, EDGE, 0)
        t_high, t_rest = split(spread[:STAMP_W])
        upper = jnp.concatenate([t_high, t_high], axis=1)
        lower = jnp.concatenate([t_rest, jnp.zeros_like(t_rest)], axis=1)
        toep_s[b] = jnp.concatenate([upper, lower], axis=0)
        inside = jnp.where(lane_e >= sub_e, spread, 0.0)
        f_high, f_rest = split(jnp.concatenate([inside, spread - inside], axis=1))
        upper = jnp.concatenate([f_high, f_high], axis=1)
        lower = jnp.concatenate([f_rest, jnp.zeros_like(f_rest)], axis=1)
        toep_f[b] = jnp.concatenate([upper, lower], axis=0)

    if rounds:
        listen(0)
    if rounds > 1:
        call(1)

    first = (me * rows).astype(jnp.float32)
    index = lax.broadcasted_iota(jnp.int32, (rows, 1), 0).astype(jnp.float32)
    v = jnp.broadcast_to(row_coords(index + first, region_rows), (rows, half_cols))
    u_all = jnp.broadcast_to(col_coords(0.0, cols, cols), (TILE, cols))
    u_sel = pick(u_all)
    u = jnp.concatenate([u_sel] * (rows // TILE), axis=0)
    good = pick(mask_ref[...].astype(jnp.float32))
    for m in range(blocks):
        clear[m] = good[:, m * EDGE : (m + 1) * EDGE]
        across_u[m] = u_sel[:, m * EDGE : (m + 1) * EDGE]
    terms = background(u, v)
    terms[0] = jnp.ones_like(u)
    terms.append(pick(exp_ref[...]))
    for k, term in enumerate(terms):
        x = term * good
        for m in range(blocks):
            ground[m, pl.ds(k, rows, stride=TILE), :] = x[:, m * EDGE : (m + 1) * EDGE]
    zero = jnp.zeros((rows, EDGE), jnp.float32)
    for b in range(bases, pad_b):
        for m in range(blocks):
            design[m, pl.ds(b, rows, stride=pad_b), :] = zero

    @pl.when(has_up)
    def _():
        halo(0).wait_recv()
        relay(0).start()

    @pl.when(has_down)
    def _():
        halo(1).wait_recv()
        relay(1).start()

    def settle(side, body, buf):
        where = pl.ds(pl.multiple_of(EDGE + side * half, EDGE), half)
        ext_ref[rows : 2 * rows, where] = body[...]
        for way, near, far in ((0, rows - TILE, rows - REACH), (1, 2 * rows, 2 * rows + TILE)):
            ext_ref[near : near + TILE, where] = buf[way, :, 0:half]
            for e in range(more):
                for m in range(spans):
                    column, line = half + (e * spans + m) // TILE * EDGE, (e * spans + m) % TILE
                    at = pl.ds(pl.multiple_of((1 + m) * EDGE + side * half, EDGE), EDGE)
                    ext_ref[far + e : far + e + 1, at] = buf[way, line : line + 1, column : column + EDGE]

    def stack(x):
        high, rest = split(x)
        gap = jnp.zeros((EDGE - 2 * ext_rows, x.shape[1]), jnp.bfloat16)
        gap2 = jnp.zeros((EDGE - ext_rows, x.shape[1]), jnp.bfloat16)
        return jnp.concatenate([high, rest, gap, high, gap2], axis=0)

    total = 3 * pad_b + TILE

    def stamp_design(first_block, n, place):
        span = 2 * n * EDGE
        at = pl.multiple_of(first_block * 2 * EDGE, EDGE)
        ext = turn(ext_ref[:, pl.ds(at, span + 2 * EDGE)], -(EDGE - HALF), 1)
        windows = []
        for s in range(2 * n):
            odd = blk_ref[0, 2 * first_block + s] % 2 == 1
            early = ext[:, s * EDGE : (s + 1) * EDGE]
            after = ext[:, (s + 1) * EDGE : (s + 2) * EDGE]
            late = pltpu.roll(jnp.where(low, after, early), STAMP_W, 1)
            windows.append(jnp.where(odd, late, early))
        window = jnp.concatenate(windows, axis=1)
        vert[:, :span] = jnp.dot(bandw[...].astype(jnp.bfloat16), stack(window), preferred_element_type=jnp.float32)
        for b in range(bases):
            x = vert[b * rows : (b + 1) * rows, :span]
            x = jnp.concatenate([x[:, s * EDGE : (s + 1) * EDGE] for s in range(2 * n)], axis=0)
            y = lax.dot_general(
                jnp.concatenate(split(x), axis=1), toep_s[b], LANE_DOT, preferred_element_type=jnp.float32
            )
            for m in range(n):
                near, far = y[2 * m * rows : (2 * m + 1) * rows], y[(2 * m + 1) * rows : (2 * m + 2) * rows]
                picked = jnp.where(low, near, far) + pltpu.roll(jnp.where(low, far, near), STAMP_W, 1)
                design[place + m, pl.ds(b, rows, stride=pad_b), :] = picked * clear[first_block + m]

    def stamp_gram(first_block, n, place, pairs, slot):
        sums = [jnp.zeros((total, total), jnp.float32) for _ in range(2)]
        for pair in pairs:
            parts = []
            for r in (2 * pair, 2 * pair + 1):
                vm = v[r : r + 1, 0:EDGE]
                for m in range(n):
                    d = design[place + m, r * pad_b : (r + 1) * pad_b, :]
                    um = across_u[first_block + m, 0:1]
                    rest = ground[first_block + m, r * TILE : (r + 1) * TILE, :]
                    parts.append(jnp.concatenate([d, d * um, d * vm, rest], axis=0))
            x = jnp.concatenate(parts, axis=1).astype(jnp.bfloat16)
            sums[pair % 2] = sums[pair % 2] + lax.dot_general(x, x, LANE_DOT, preferred_element_type=jnp.float32)
        for h in range(2):
            grams[slot + h, :, 0:total] = sums[h]

    settle(core, tmpl_ref, halo_own)
    ahead = blocks // 2 - 1
    pairs = range(rows // 2)
    near_block, far_block = core * (blocks - ahead), (1 - core) * ahead
    if ahead:
        stamp_design(near_block, ahead, 0)
        stamp_gram(near_block, ahead, 0, pairs[:GRAM_EARLY], 0)
    if rounds > 1:
        listen(1)
    if rounds > 2:
        call(2)
    across.wait_recv()

    @pl.when(has_up)
    def _():
        relay(0).wait_recv()

    @pl.when(has_down)
    def _():
        relay(1).wait_recv()

    settle(1 - core, whole, halo_other)
    if ahead:
        stamp_gram(near_block, ahead, 0, pairs[GRAM_EARLY:], 2)
    stamp_design(far_block, blocks - ahead, ahead)
    stamp_gram(far_block, blocks - ahead, ahead, pairs, 4)
    @pl.when(has_down)
    def _():
        edge(0).start()

    @pl.when(has_up)
    def _():
        edge(1).start()

    acc = grams[4, :, 0:total] + grams[5, :, 0:total]
    if ahead:
        acc = acc + ((grams[0, :, 0:total] + grams[1, :, 0:total]) + (grams[2, :, 0:total] + grams[3, :, 0:total]))
    gram = jnp.concatenate([acc, jnp.zeros((total, EDGE - total), jnp.float32)], axis=1)
    gram = squeeze_terms(squeeze_terms(gram, bases, 0), bases, 1)
    body, last = pack_normal(gram, fit)
    for n in range(2, rounds):
        listen(n)
        if n + 1 < rounds:
            call(n + 1)

    def reduce_start(phase, base, stride, radix):
        digit = (me // stride) % radix
        copies = []
        for k in range(radix - 1, 0, -1):
            other = digit * 0
            for bit in range((radix - 1).bit_length()):
                on = (digit // (1 << bit)) % 2
                other = other + ((1 - on) if (k >> bit) & 1 else on) * (1 << bit)
            copies.append(
                pltpu.make_async_remote_copy(
                    src_ref=send.at[phase],
                    dst_ref=held.at[base + k - 1],
                    send_sem=red_ss.at[base + k - 1],
                    recv_sem=red_rs.at[base + k - 1],
                    device_id={"stripe": me + (other - digit) * stride},
                    device_id_type=MESH,
                )
            )
        for c in copies:
            c.start()
        return copies

    fold = body.shape[0]

    def put(phase, parts):
        send[phase, 0:fold] = parts[0]
        send[phase, fold : fold + 1] = parts[1]

    def tree(values):
        while len(values) > 1:
            values = [values[q] + values[q + 1] for q in range(0, len(values), 2)]
        return values[0]

    def prepare():
        for c in (0, 1):

            @pl.when((has_up, has_down)[c])
            def _():
                edge(c).wait_recv()

        spare = jnp.zeros((tall - rows - 2, EDGE), jnp.float32)
        for m in range(tiles):
            at = slice(m * EDGE, (m + 1) * EDGE)
            science = jnp.concatenate([exp_ref[:, at], edge_recv[1, 0:1, at], spare, edge_recv[0, 0:1, at]], axis=0)
            clean = jnp.concatenate(
                [mask_ref[:, at].astype(jnp.float32), edge_recv[1, 1:2, at], spare, edge_recv[0, 1:2, at]], axis=0
            )
            clean_ref[:, at] = clean
            diff[:, at] = clean * science

    base, stride, flying = 0, 1, []
    if not radices:
        prepare()
    for phase, radix in enumerate(radices):
        put(phase, (body, last))
        copies = reduce_start(phase, base, stride, radix)
        flying += copies
        if phase == 0:
            vert_f[...] = jnp.dot(
                bandf[...].astype(jnp.bfloat16), stack(turn(ext_ref[...], -(EDGE - HALF), 1)), preferred_element_type=jnp.float32
            )
            for b in range(bases):
                x = vert_f[b * tall : (b + 1) * tall, :]
                x = jnp.concatenate([x[:, m * EDGE : (m + 2) * EDGE] for m in range(tiles)], axis=0)
                y = lax.dot_general(
                    jnp.concatenate(split(x), axis=1), toep_f[b], LANE_DOT, preferred_element_type=jnp.float32
                )
                basis[b] = y[:, :EDGE] + y[:, EDGE:]
            prepare()
        for c in copies:
            c.wait_recv()
        body = tree([send[phase, 0:fold]] + [held[base + k, 0:fold] for k in range(radix - 1)])
        last = tree([send[phase, fold : fold + 1]] + [held[base + k, fold : fold + 1] for k in range(radix - 1)])
        base += radix - 1
        stride *= radix

    answer = eliminate(unpack_normal(body, last, fit), fit)
    coef_ref[...] = answer
    n = lax.broadcasted_iota(jnp.int32, (fit, fit), 0)
    term = (n >= bases).astype(jnp.int32) + (n >= 2 * bases).astype(jnp.int32)
    spot = jnp.where(n < 3 * bases, 3 * (n - bases * term) + term, n)
    same = spot == lax.broadcasted_iota(jnp.int32, (fit, fit), 1)
    row_ref[...] = jnp.sum(jnp.where(same, answer[:, :fit], 0.0), axis=0, keepdims=True)

    def coef(n):
        return coef_ref[pl.ds(n, TILE, stride=0), :]

    def three(x):
        return jnp.concatenate([x] * (tall // TILE), axis=0)

    place = lax.broadcasted_iota(jnp.int32, (tall, EDGE), 0)
    place = jnp.where(place == tall - 1, -1, place).astype(jnp.float32)
    v = row_coords(place + first, region_rows)
    vv = 0.5 * (3.0 * v * v - 1.0)
    for b in range(bases):
        plane[b, 0:tall] = three(coef(b)) + v * three(coef(2 * bases + b))
        plane[b, tall : tall + TILE] = coef(bases + b)
    q = [coef(3 * bases + k) for k in range(7)]
    flat = three(q[0]) + v * three(q[2]) + vv * three(q[5])
    slope = three(q[1]) + v * three(q[3]) + vv * three(q[6])
    u_all = col_coords(0.0, cols, cols)
    for m in range(tiles):
        at = slice(m * EDGE, (m + 1) * EDGE)
        um = jnp.broadcast_to(u_all[:, at], (TILE, EDGE))
        uu = 0.5 * (3.0 * um * um - 1.0)
        model = flat + three(um) * slope + three(q[4] * uu)
        for b in range(bases):
            factor = plane[b, 0:tall] + three(um * plane[b, tall : tall + TILE])
            model = model + factor * basis[b, m * tall : (m + 1) * tall]
        diff[:, at] = diff[:, at] - clean_ref[:, at] * model

    across.wait_send()
    for c in flying:
        c.wait_send()

    @pl.when(has_down)
    def _():
        halo(0).wait_send()
        edge(0).wait_send()
        relay(1).wait_send()

    @pl.when(has_up)
    def _():
        halo(1).wait_send()
        edge(1).wait_send()
        relay(0).wait_send()


def finish_kernel(diff_ref, coef_ref, out_ref, row_ref):
    rows, cols = out_ref.shape
    lane = lax.broadcasted_iota(jnp.int32, (rows, cols), 1)
    every = diff_ref[...]
    mid = every[:rows]
    left = jnp.where(lane == 0, 0.0, turn(mid, 1, 1))
    right = jnp.where(lane == cols - 1, 0.0, turn(mid, -1, 1))
    around = turn(every, -1, 0)[:rows] + turn(every, 1, 0)[:rows] + right + left
    out_ref[...] = 4.0 * mid - around
    row_ref[...] = coef_ref[...]


def shards(template, exposure, cosmic_mask, stamp_blocks, row_filters, col_filters):
    rows, cols = exposure.shape[1:]
    bases, taps = row_filters.shape
    fit = 3 * bases + 7
    stripes = lax.axis_size("stripe")
    half = template.shape[1]
    ext_rows = 3 * rows
    wide = cols + 2 * EDGE
    tall = round_up(rows + 2, TILE)
    pad_b = round_up(bases, TILE)
    blocks = cols // (2 * EDGE)
    tiles = cols // EDGE
    radices = []
    rest = stripes
    while rest > 1:
        radices.append(min(rest, 8))
        rest //= radices[-1]
    slots = max(1, sum(r - 1 for r in radices))
    rounds = (stripes - 2).bit_length() if stripes > 2 else 0
    packed = fit // 4 + 1
    extra = round_up((REACH - TILE) * half // EDGE, TILE) // TILE * EDGE
    f32, bf16 = jnp.float32, jnp.bfloat16
    vmem = pl.BlockSpec(memory_space=pltpu.VMEM)
    anywhere = pl.BlockSpec(memory_space=pltpu.HBM)
    operands = (template, exposure[0], cosmic_mask[0], stamp_blocks, row_filters, col_filters)
    operands = [pltpu.with_memory_space_constraint(x, pltpu.HBM) for x in operands]
    diff, coef_row = pl.pallas_call(
        functools.partial(kernel, stripes, float(rows * stripes), radices, rounds),
        out_shape=(jax.ShapeDtypeStruct((tall, cols), f32), jax.ShapeDtypeStruct((1, fit), f32)),
        in_specs=[anywhere] * 6,
        out_specs=(vmem, vmem),
        scratch_shapes=[
            pltpu.VMEM((rows, half), f32),
            pltpu.VMEM((rows, cols), f32),
            pltpu.VMEM((rows, cols), jnp.int32),
            pltpu.SMEM(stamp_blocks.shape, jnp.int32),
            pltpu.VMEM((bases, taps), f32),
            pltpu.VMEM((bases, taps), f32),
            pltpu.VMEM((2, TILE, half + extra), f32),
            pltpu.VMEM((2, TILE, half + extra), f32),
            pltpu.VMEM((2, TILE, half + extra), f32),
            pltpu.VMEM((rows, half), f32),
            pltpu.VMEM((2, 2, cols), f32),
            pltpu.VMEM((2, 2, cols), f32),
            pltpu.VMEM((ext_rows, wide), f32),
            pltpu.VMEM((bases * rows, 2 * EDGE), f32),
            pltpu.VMEM((bases * tall, 2 * EDGE), f32),
            pltpu.VMEM((bases, EDGE, 2 * EDGE), bf16),
            pltpu.VMEM((bases, 2 * EDGE, 4 * EDGE), bf16),
            pltpu.VMEM((bases * rows, cols), f32),
            pltpu.VMEM((blocks, rows * pad_b, EDGE), f32),
            pltpu.VMEM((blocks, rows * TILE, EDGE), f32),
            pltpu.VMEM((blocks, rows, EDGE), f32),
            pltpu.VMEM((blocks, TILE, EDGE), f32),
            pltpu.VMEM((6, 3 * pad_b + TILE, EDGE), f32),
            pltpu.VMEM((bases * tall, wide), f32),
            pltpu.VMEM((bases, tiles * tall, EDGE), f32),
            pltpu.VMEM((fit, EDGE), f32),
            pltpu.VMEM((bases, tall + TILE, EDGE), f32),
            pltpu.VMEM((tall, cols), f32),
            pltpu.VMEM((max(1, len(radices)), packed, EDGE), f32),
            pltpu.VMEM((slots, packed, EDGE), f32),
            pltpu.SemaphoreType.DMA((6,)),
            pltpu.SemaphoreType.DMA((7,)),
            pltpu.SemaphoreType.DMA((7,)),
            pltpu.SemaphoreType.DMA((slots,)),
            pltpu.SemaphoreType.DMA((slots,)),
            pltpu.SemaphoreType.REGULAR((max(1, rounds),)),
        ],
        compiler_params=pltpu.CompilerParams(
            collective_id=0, has_side_effects=True, vmem_limit_bytes=VMEM_GRANT
        ),
        name="fused",
    )(*operands)
    filtered, coef_row = pl.pallas_call(
        finish_kernel,
        out_shape=(jax.ShapeDtypeStruct((rows, cols), f32), jax.ShapeDtypeStruct((1, fit), f32)),
        in_specs=[vmem, vmem],
        out_specs=(vmem, vmem),
        compiler_params=pltpu.CompilerParams(vmem_limit_bytes=VMEM_GRANT),
        name="finish",
    )(diff, coef_row)
    return (filtered[None], coef_row)


def solution(mesh):
    placed = (
        P(("groups", "stripe"), "exp"),
        P(("groups", "exp"), "stripe", None),
        P(("groups", "exp"), "stripe", None),
        P(("groups", "stripe"), None),
        P(),
        P(),
    )
    return jax.shard_map(
        shards,
        mesh=mesh,
        in_specs=placed,
        out_specs=(P(("groups", "exp"), "stripe", None), P(("groups", "exp"), None)),
        check_vma=False,
    )
```

```python
import functools

import jax
import jax.numpy as jnp
from jax import lax
from jax.experimental import pallas as pl
from jax.experimental.pallas import tpu as pltpu
from jax.sharding import PartitionSpec as P

HALF = 9
STAMP_W = 64
EDGE = 128
TILE = 8
BLOCK = 8
REACH = HALF + 1
VMEM_GRANT = 32 * 1024 * 1024
GRAM_EARLY = 3
MESH = pl.DeviceIdType.MESH
LANE_DOT = (((1,), (1,)), ((), ()))


def round_up(n, m):
    return -(-n // m) * m


def row_coords(index, region_rows):
    return (2.0 * index + 1.0) / region_rows - 1.0


def col_coords(first, count, col_total):
    index = lax.broadcasted_iota(jnp.int32, (1, count), 1).astype(jnp.float32) + first
    return (2.0 * index + 1.0) / col_total - 1.0


def background(u, v):
    uu = 0.5 * (3.0 * u * u - 1.0)
    vv = 0.5 * (3.0 * v * v - 1.0)
    return [None, u, v, u * v, uu, vv, u * vv]


def split(x):
    high = x.astype(jnp.bfloat16)
    return high, (x - high.astype(jnp.float32)).astype(jnp.bfloat16)


def shifted_rows(row, count, start):
    return pltpu.roll(jnp.broadcast_to(row, (count, EDGE)), start, 1, stride=1, stride_axis=0)


def iotas(rows):
    return lax.broadcasted_iota(jnp.int32, (rows, EDGE), 0), lax.broadcasted_iota(jnp.int32, (rows, EDGE), 1)


def turn(x, shift, axis):
    return pltpu.roll(x, shift % x.shape[axis], axis)


def squeeze_terms(a, bases, axis):
    padded = round_up(bases, TILE)
    gap = padded - bases
    index = lax.broadcasted_iota(jnp.int32, a.shape, axis)
    out = a
    for t in range(1, 4):
        out = jnp.where(index >= t * bases, turn(a, -t * gap, axis), out)
    return out


def pack_normal(gram, fit):
    half = fit // 2
    rows = gram.shape[0]
    sub, lane = iotas(half)
    one = lane[0:1]
    upper, lower = gram[:half], gram[half:fit]
    merged = jnp.where((lane > sub) & (lane < half), turn(lower, -half, 1), upper)
    fold = half // 2
    body = jnp.where(lane[:fold] < fit, merged[:fold], turn(merged[fold:], fit, 1))
    diag = jnp.sum(jnp.where(lane == sub + half, lower, 0.0), axis=0, keepdims=True)
    last = jnp.where(one < fit, gram[fit : fit + 1], jnp.where(one < fit + half, turn(diag, half, 1), 0.0))
    return body, last


def unpack_normal(body, last, fit):
    half = fit // 2
    sub, lane = iotas(half)
    quad = jnp.concatenate([body, turn(body, fit, 1)], axis=0)
    tall = jnp.concatenate([quad, jnp.broadcast_to(last, (TILE, EDGE))], axis=0)
    flip = jnp.transpose(tall, (1, 0))[:fit]
    flip = jnp.concatenate([flip, jnp.zeros((fit, EDGE - flip.shape[1]), jnp.float32)], axis=1)
    side = turn(flip, half, 1)
    first, second = flip[:half], flip[half:]
    diag = jnp.broadcast_to(turn(last, -fit, 1), (half, EDGE))
    top = jnp.where(lane < half, jnp.where(lane <= sub, quad, first), jnp.where(lane < fit, quad, side[:half]))
    corner = jnp.where(lane > sub, quad, jnp.where(lane == sub, diag, first))
    low = jnp.where(lane < half, second, jnp.where(lane < fit, turn(corner, half, 1), side[half:]))
    return jnp.concatenate([top, low], axis=0)


def eliminate(a, fit):
    shape = (TILE, EDGE)
    count = fit // TILE
    tiles = [a[i * TILE : (i + 1) * TILE] for i in range(count)]
    sub = lax.broadcasted_iota(jnp.int32, shape, 0)
    for i in range(count):
        order = [j % count for j in range(i, i + count)]
        cols = {j: [jnp.broadcast_to(tiles[j][:, k : k + 1], shape) for k in range(i * TILE, (i + 1) * TILE)] for j in order}
        near = list(cols[i])
        for t in range(TILE):
            inverse = pl.reciprocal(near[t][t : t + 1])

            def step(x):
                row = x[t : t + 1] * inverse
                return jnp.where(sub == t, row, x - near[t] * row)

            for w in range(t + 1, TILE):
                near[w] = step(near[w])
            tiles[i] = step(tiles[i])
        for j in order[1:]:
            terms = [cols[j][t] * tiles[i][t : t + 1] for t in range(TILE)]
            while len(terms) > 1:
                terms = [terms[q] + terms[q + 1] for q in range(0, len(terms), 2)]
            tiles[j] = tiles[j] - terms[0]
    return jnp.concatenate([jnp.broadcast_to(x[:, fit : fit + 1], shape) for x in tiles], axis=0)


def kernel(
    count,
    region_rows,
    radices,
    rounds,
    tmpl_hbm,
    exp_hbm,
    mask_hbm,
    blk_hbm,
    rowf_hbm,
    colf_hbm,
    diff,
    row_ref,
    tmpl_ref,
    exp_ref,
    mask_ref,
    blk_ref,
    rowf_ref,
    colf_ref,
    halo_send,
    halo_own,
    halo_other,
    whole,
    edge_send,
    edge_recv,
    ext_ref,
    bandw,
    bandf,
    toep_s,
    toep_f,
    vert,
    design,
    ground,
    clear,
    across_u,
    grams,
    vert_f,
    basis,
    coef_ref,
    plane,
    clean_ref,
    send,
    held,
    load_sem,
    halo_ss,
    halo_rs,
    red_ss,
    red_rs,
    hello,
):
    me = lax.axis_index("stripe")
    core = lax.axis_index("exp")
    rows, half = tmpl_ref.shape
    cols = exp_ref.shape[1]
    bases, taps = rowf_ref.shape
    fit = 3 * bases + 7
    pad_b = round_up(bases, TILE)
    ext_rows, wide = ext_ref.shape
    tall = diff.shape[0]
    half_cols = cols // 2
    blocks = half_cols // EDGE
    stamps = 2 * blocks
    tiles = cols // EDGE
    has_up = me > 0
    has_down = me < count - 1
    up_count = has_up.astype(jnp.int32)
    down_count = has_down.astype(jnp.int32)

    barrier = pltpu.get_barrier_semaphore()

    def greet(sem, stripe, exp):
        pl.semaphore_signal(sem, inc=1, device_id={"stripe": stripe, "exp": exp}, device_id_type=MESH)

    @pl.when(has_up)
    def _():
        greet(barrier, me - 1, core)

    @pl.when(has_down)
    def _():
        greet(barrier, me + 1, core)

    greet(barrier, me, 1 - core)

    loads = [
        pltpu.make_async_copy(src, dst, load_sem.at[n])
        for n, (src, dst) in enumerate(
            (
                (tmpl_hbm, tmpl_ref),
                (exp_hbm, exp_ref),
                (mask_hbm, mask_ref),
                (blk_hbm, blk_ref),
                (rowf_hbm, rowf_ref),
                (colf_hbm, colf_ref),
            )
        )
    ]
    for c in loads:
        c.start()

    ext_ref[...] = jnp.zeros_like(ext_ref)

    @pl.when(jnp.logical_not(has_up))
    def _():
        halo_own[0] = jnp.zeros_like(halo_own[0])
        halo_other[0] = jnp.zeros_like(halo_other[0])
        edge_recv[0] = jnp.zeros_like(edge_recv[0])

    @pl.when(jnp.logical_not(has_down))
    def _():
        halo_own[1] = jnp.zeros_like(halo_own[1])
        halo_other[1] = jnp.zeros_like(halo_other[1])
        edge_recv[1] = jnp.zeros_like(edge_recv[1])

    def copy(src, dst, n, stripe, exp):
        return pltpu.make_async_remote_copy(
            src_ref=src,
            dst_ref=dst,
            send_sem=halo_ss.at[n],
            recv_sem=halo_rs.at[n],
            device_id={"stripe": stripe, "exp": exp},
            device_id_type=MESH,
        )

    def halo(way):
        return copy(halo_send.at[way], halo_own.at[way], way, me + 1 - 2 * way, core)

    def edge(way):
        return copy(edge_send.at[way], edge_recv.at[way], 2 + way, me + 1 - 2 * way, core)

    def relay(way):
        return copy(halo_own.at[way], halo_other.at[way], 4 + way, me, 1 - core)

    more = REACH - TILE
    spans = half // EDGE
    for c in loads:
        c.wait()
    for way, near, far in ((0, rows - TILE, rows - REACH), (1, 0, TILE)):
        halo_send[way, :, 0:half] = tmpl_ref[near : near + TILE]
        for e in range(more):
            for m in range(spans):
                column, line = half + (e * spans + m) // TILE * EDGE, (e * spans + m) % TILE
                halo_send[way, line : line + 1, column : column + EDGE] = tmpl_ref[
                    far + e : far + e + 1, m * EDGE : (m + 1) * EDGE
                ]
    edge_send[0, 0:1, :] = exp_ref[rows - 1 : rows, :]
    edge_send[0, 1:2, :] = mask_ref[rows - 1 : rows, :].astype(jnp.float32)
    edge_send[1, 0:1, :] = exp_ref[0:1, :]
    edge_send[1, 1:2, :] = mask_ref[0:1, :].astype(jnp.float32)

    pl.semaphore_wait(barrier, 1 + up_count + down_count)

    @pl.when(has_down)
    def _():
        halo(0).start()

    @pl.when(has_up)
    def _():
        halo(1).start()

    across = copy(tmpl_ref, whole, 6, me, 1 - core)
    across.start()

    def call(n):
        reach = 1 << n

        @pl.when(me >= reach)
        def _():
            greet(hello.at[n], me - reach, core)

        @pl.when(me + reach < count)
        def _():
            greet(hello.at[n], me + reach, core)

    def listen(n):
        reach = 1 << n
        heard = (me >= reach).astype(jnp.int32) + (me + reach < count).astype(jnp.int32)
        pl.semaphore_wait(hello.at[n], heard)

    if rounds:
        call(0)

    lanes = jnp.zeros((1, EDGE - taps), jnp.float32)
    low = lax.broadcasted_iota(jnp.int32, (1, EDGE), 1) < STAMP_W
    parity = [blk_ref[0, s] % 2 == 1 for s in range(stamps)]

    def pick(x):
        parts = []
        for m in range(blocks):
            a = x[:, 2 * m * EDGE : (2 * m + 1) * EDGE]
            b = x[:, (2 * m + 1) * EDGE : (2 * m + 2) * EDGE]
            a = jnp.where(parity[2 * m], pltpu.roll(a, STAMP_W, 1), a)
            b = jnp.where(parity[2 * m + 1], b, pltpu.roll(b, STAMP_W, 1))
            parts.append(jnp.where(low, a, b))
        return jnp.concatenate(parts, axis=1)

    start = ext_rows // 2 - rows // 2 - HALF
    sub_e, lane_e = iotas(EDGE)
    sub_t = lax.broadcasted_iota(jnp.int32, (TILE, EDGE), 0)
    for b in range(bases):
        row = jnp.concatenate([rowf_ref[b : b + 1, :], lanes], axis=1)
        high = row.astype(jnp.bfloat16).astype(jnp.float32)

        def placed(x, offset):
            body = shifted_rows(x, rows + TILE, start + offset)
            above = pltpu.roll(jnp.broadcast_to(x, (TILE, EDGE)), start + offset - 1, 1)
            tail = jnp.where(sub_t == TILE - 1, above, body[rows:])
            return body[:rows], jnp.concatenate([body[:rows], tail], axis=0)

        (h0, h0f), (h1, h1f), (r0, r0f) = placed(high, 0), placed(high, ext_rows), placed(row - high, 0)
        bandw[b * rows : (b + 1) * rows, :] = jnp.concatenate([h0 + h1, r0], axis=1)
        bandf[b * tall : (b + 1) * tall, :] = jnp.concatenate([h0f + h1f, r0f], axis=1)
        row = jnp.concatenate([colf_ref[b : b + 1, :], lanes], axis=1)
        spread = shifted_rows(row, EDGE, 0)
        t_high, t_rest = split(spread[:STAMP_W])
        upper = jnp.concatenate([t_high, t_high], axis=1)
        lower = jnp.concatenate([t_rest, jnp.zeros_like(t_rest)], axis=1)
        toep_s[b] = jnp.concatenate([upper, lower], axis=0)
        inside = jnp.where(lane_e >= sub_e, spread, 0.0)
        f_high, f_rest = split(jnp.concatenate([inside, spread - inside], axis=1))
        upper = jnp.concatenate([f_high, f_high], axis=1)
        lower = jnp.concatenate([f_rest, jnp.zeros_like(f_rest)], axis=1)
        toep_f[b] = jnp.concatenate([upper, lower], axis=0)

    if rounds:
        listen(0)
    if rounds > 1:
        call(1)

    first = (me * rows).astype(jnp.float32)
    index = lax.broadcasted_iota(jnp.int32, (rows, 1), 0).astype(jnp.float32)
    v = jnp.broadcast_to(row_coords(index + first, region_rows), (rows, half_cols))
    u_all = jnp.broadcast_to(col_coords(0.0, cols, cols), (TILE, cols))
    u_sel = pick(u_all)
    u = jnp.concatenate([u_sel] * (rows // TILE), axis=0)
    good = pick(mask_ref[...].astype(jnp.float32))
    for m in range(blocks):
        clear[m] = good[:, m * EDGE : (m + 1) * EDGE]
        across_u[m] = u_sel[:, m * EDGE : (m + 1) * EDGE]
    terms = background(u, v)
    terms[0] = jnp.ones_like(u)
    terms.append(pick(exp_ref[...]))
    for k, term in enumerate(terms):
        x = term * good
        for m in range(blocks):
            ground[m, pl.ds(k, rows, stride=TILE), :] = x[:, m * EDGE : (m + 1) * EDGE]
    zero = jnp.zeros((rows, EDGE), jnp.float32)
    for b in range(bases, pad_b):
        for m in range(blocks):
            design[m, pl.ds(b, rows, stride=pad_b), :] = zero

    @pl.when(has_up)
    def _():
        halo(0).wait_recv()
        relay(0).start()

    @pl.when(has_down)
    def _():
        halo(1).wait_recv()
        relay(1).start()

    def settle(side, body, buf):
        where = pl.ds(pl.multiple_of(EDGE + side * half, EDGE), half)
        ext_ref[rows : 2 * rows, where] = body[...]
        for way, near, far in ((0, rows - TILE, rows - REACH), (1, 2 * rows, 2 * rows + TILE)):
            ext_ref[near : near + TILE, where] = buf[way, :, 0:half]
            for e in range(more):
                for m in range(spans):
                    column, line = half + (e * spans + m) // TILE * EDGE, (e * spans + m) % TILE
                    at = pl.ds(pl.multiple_of((1 + m) * EDGE + side * half, EDGE), EDGE)
                    ext_ref[far + e : far + e + 1, at] = buf[way, line : line + 1, column : column + EDGE]

    def stack(x):
        high, rest = split(x)
        gap = jnp.zeros((EDGE - 2 * ext_rows, x.shape[1]), jnp.bfloat16)
        gap2 = jnp.zeros((EDGE - ext_rows, x.shape[1]), jnp.bfloat16)
        return jnp.concatenate([high, rest, gap, high, gap2], axis=0)

    total = 3 * pad_b + TILE

    def stamp_design(first_block, n, place):
        span = 2 * n * EDGE
        at = pl.multiple_of(first_block * 2 * EDGE, EDGE)
        ext = turn(ext_ref[:, pl.ds(at, span + 2 * EDGE)], -(EDGE - HALF), 1)
        windows = []
        for s in range(2 * n):
            odd = blk_ref[0, 2 * first_block + s] % 2 == 1
            early = ext[:, s * EDGE : (s + 1) * EDGE]
            after = ext[:, (s + 1) * EDGE : (s + 2) * EDGE]
            late = pltpu.roll(jnp.where(low, after, early), STAMP_W, 1)
            windows.append(jnp.where(odd, late, early))
        window = jnp.concatenate(windows, axis=1)
        vert[:, :span] = jnp.dot(bandw[...].astype(jnp.bfloat16), stack(window), preferred_element_type=jnp.float32)
        for b in range(bases):
            x = vert[b * rows : (b + 1) * rows, :span]
            x = jnp.concatenate([x[:, s * EDGE : (s + 1) * EDGE] for s in range(2 * n)], axis=0)
            y = lax.dot_general(
                jnp.concatenate(split(x), axis=1), toep_s[b], LANE_DOT, preferred_element_type=jnp.float32
            )
            for m in range(n):
                near, far = y[2 * m * rows : (2 * m + 1) * rows], y[(2 * m + 1) * rows : (2 * m + 2) * rows]
                picked = jnp.where(low, near, far) + pltpu.roll(jnp.where(low, far, near), STAMP_W, 1)
                design[place + m, pl.ds(b, rows, stride=pad_b), :] = picked * clear[first_block + m]

    def stamp_gram(first_block, n, place, pairs, slot):
        sums = [jnp.zeros((total, total), jnp.float32) for _ in range(2)]
        for pair in pairs:
            parts = []
            for r in (2 * pair, 2 * pair + 1):
                vm = v[r : r + 1, 0:EDGE]
                for m in range(n):
                    d = design[place + m, r * pad_b : (r + 1) * pad_b, :]
                    um = across_u[first_block + m, 0:1]
                    rest = ground[first_block + m, r * TILE : (r + 1) * TILE, :]
                    parts.append(jnp.concatenate([d, d * um, d * vm, rest], axis=0))
            x = jnp.concatenate(parts, axis=1).astype(jnp.bfloat16)
            sums[pair % 2] = sums[pair % 2] + lax.dot_general(x, x, LANE_DOT, preferred_element_type=jnp.float32)
        for h in range(2):
            grams[slot + h, :, 0:total] = sums[h]

    settle(core, tmpl_ref, halo_own)
    ahead = blocks // 2 - 1
    pairs = range(rows // 2)
    near_block, far_block = core * (blocks - ahead), (1 - core) * ahead
    if ahead:
        stamp_design(near_block, ahead, 0)
        stamp_gram(near_block, ahead, 0, pairs[:GRAM_EARLY], 0)
    if rounds > 1:
        listen(1)
    if rounds > 2:
        call(2)
    across.wait_recv()

    @pl.when(has_up)
    def _():
        relay(0).wait_recv()

    @pl.when(has_down)
    def _():
        relay(1).wait_recv()

    settle(1 - core, whole, halo_other)
    if ahead:
        stamp_gram(near_block, ahead, 0, pairs[GRAM_EARLY:], 2)
    stamp_design(far_block, blocks - ahead, ahead)
    stamp_gram(far_block, blocks - ahead, ahead, pairs, 4)
    @pl.when(has_down)
    def _():
        edge(0).start()

    @pl.when(has_up)
    def _():
        edge(1).start()

    acc = grams[4, :, 0:total] + grams[5, :, 0:total]
    if ahead:
        acc = acc + ((grams[0, :, 0:total] + grams[1, :, 0:total]) + (grams[2, :, 0:total] + grams[3, :, 0:total]))
    gram = jnp.concatenate([acc, jnp.zeros((total, EDGE - total), jnp.float32)], axis=1)
    gram = squeeze_terms(squeeze_terms(gram, bases, 0), bases, 1)
    body, last = pack_normal(gram, fit)
    for n in range(2, rounds):
        listen(n)
        if n + 1 < rounds:
            call(n + 1)

    def reduce_start(phase, base, stride, radix):
        digit = (me // stride) % radix
        copies = []
        for k in range(radix - 1, 0, -1):
            other = digit * 0
            for bit in range((radix - 1).bit_length()):
                on = (digit // (1 << bit)) % 2
                other = other + ((1 - on) if (k >> bit) & 1 else on) * (1 << bit)
            copies.append(
                pltpu.make_async_remote_copy(
                    src_ref=send.at[phase],
                    dst_ref=held.at[base + k - 1],
                    send_sem=red_ss.at[base + k - 1],
                    recv_sem=red_rs.at[base + k - 1],
                    device_id={"stripe": me + (other - digit) * stride},
                    device_id_type=MESH,
                )
            )
        for c in copies:
            c.start()
        return copies

    fold = body.shape[0]

    def put(phase, parts):
        send[phase, 0:fold] = parts[0]
        send[phase, fold : fold + 1] = parts[1]

    def tree(values):
        while len(values) > 1:
            values = [values[q] + values[q + 1] for q in range(0, len(values), 2)]
        return values[0]

    def prepare():
        for c in (0, 1):

            @pl.when((has_up, has_down)[c])
            def _():
                edge(c).wait_recv()

        spare = jnp.zeros((tall - rows - 2, EDGE), jnp.float32)
        for m in range(tiles):
            at = slice(m * EDGE, (m + 1) * EDGE)
            science = jnp.concatenate([exp_ref[:, at], edge_recv[1, 0:1, at], spare, edge_recv[0, 0:1, at]], axis=0)
            clean = jnp.concatenate(
                [mask_ref[:, at].astype(jnp.float32), edge_recv[1, 1:2, at], spare, edge_recv[0, 1:2, at]], axis=0
            )
            clean_ref[:, at] = clean
            diff[:, at] = clean * science

    base, stride, flying = 0, 1, []
    if not radices:
        prepare()
    for phase, radix in enumerate(radices):
        put(phase, (body, last))
        copies = reduce_start(phase, base, stride, radix)
        flying += copies
        if phase == 0:
            vert_f[...] = jnp.dot(
                bandf[...].astype(jnp.bfloat16), stack(turn(ext_ref[...], -(EDGE - HALF), 1)), preferred_element_type=jnp.float32
            )
            for b in range(bases):
                x = vert_f[b * tall : (b + 1) * tall, :]
                x = jnp.concatenate([x[:, m * EDGE : (m + 2) * EDGE] for m in range(tiles)], axis=0)
                y = lax.dot_general(
                    jnp.concatenate(split(x), axis=1), toep_f[b], LANE_DOT, preferred_element_type=jnp.float32
                )
                basis[b] = y[:, :EDGE] + y[:, EDGE:]
            prepare()
        for c in copies:
            c.wait_recv()
        body = tree([send[phase, 0:fold]] + [held[base + k, 0:fold] for k in range(radix - 1)])
        last = tree([send[phase, fold : fold + 1]] + [held[base + k, fold : fold + 1] for k in range(radix - 1)])
        base += radix - 1
        stride *= radix

    answer = eliminate(unpack_normal(body, last, fit), fit)
    coef_ref[...] = answer
    n = lax.broadcasted_iota(jnp.int32, (fit, fit), 0)
    term = (n >= bases).astype(jnp.int32) + (n >= 2 * bases).astype(jnp.int32)
    spot = jnp.where(n < 3 * bases, 3 * (n - bases * term) + term, n)
    same = spot == lax.broadcasted_iota(jnp.int32, (fit, fit), 1)
    row_ref[...] = jnp.sum(jnp.where(same, answer[:, :fit], 0.0), axis=0, keepdims=True)

    def coef(n):
        return coef_ref[pl.ds(n, TILE, stride=0), :]

    def three(x):
        return jnp.concatenate([x] * (tall // TILE), axis=0)

    place = lax.broadcasted_iota(jnp.int32, (tall, EDGE), 0)
    place = jnp.where(place == tall - 1, -1, place).astype(jnp.float32)
    v = row_coords(place + first, region_rows)
    vv = 0.5 * (3.0 * v * v - 1.0)
    for b in range(bases):
        plane[b, 0:tall] = three(coef(b)) + v * three(coef(2 * bases + b))
        plane[b, tall : tall + TILE] = coef(bases + b)
    q = [coef(3 * bases + k) for k in range(7)]
    flat = three(q[0]) + v * three(q[2]) + vv * three(q[5])
    slope = three(q[1]) + v * three(q[3]) + vv * three(q[6])
    u_all = col_coords(0.0, cols, cols)
    for m in range(tiles):
        at = slice(m * EDGE, (m + 1) * EDGE)
        um = jnp.broadcast_to(u_all[:, at], (TILE, EDGE))
        uu = 0.5 * (3.0 * um * um - 1.0)
        model = flat + three(um) * slope + three(q[4] * uu)
        for b in range(bases):
            factor = plane[b, 0:tall] + three(um * plane[b, tall : tall + TILE])
            model = model + factor * basis[b, m * tall : (m + 1) * tall]
        diff[:, at] = diff[:, at] - clean_ref[:, at] * model

    across.wait_send()
    for c in flying:
        c.wait_send()

    @pl.when(has_down)
    def _():
        halo(0).wait_send()
        edge(0).wait_send()
        relay(1).wait_send()

    @pl.when(has_up)
    def _():
        halo(1).wait_send()
        edge(1).wait_send()
        relay(0).wait_send()


def finish_kernel(diff_ref, coef_ref, out_ref, row_ref):
    rows, cols = out_ref.shape
    lane = lax.broadcasted_iota(jnp.int32, (rows, cols), 1)
    every = diff_ref[...]
    mid = every[:rows]
    left = jnp.where(lane == 0, 0.0, turn(mid, 1, 1))
    right = jnp.where(lane == cols - 1, 0.0, turn(mid, -1, 1))
    around = turn(every, -1, 0)[:rows] + turn(every, 1, 0)[:rows] + right + left
    out_ref[...] = 4.0 * mid - around
    row_ref[...] = coef_ref[...]


def shards(template, exposure, cosmic_mask, stamp_blocks, row_filters, col_filters):
    rows, cols = exposure.shape[1:]
    bases, taps = row_filters.shape
    fit = 3 * bases + 7
    stripes = lax.axis_size("stripe")
    half = template.shape[1]
    ext_rows = 3 * rows
    wide = cols + 2 * EDGE
    tall = round_up(rows + 2, TILE)
    pad_b = round_up(bases, TILE)
    blocks = cols // (2 * EDGE)
    tiles = cols // EDGE
    radices = []
    rest = stripes
    while rest > 1:
        radices.append(min(rest, 8))
        rest //= radices[-1]
    slots = max(1, sum(r - 1 for r in radices))
    rounds = (stripes - 2).bit_length() if stripes > 2 else 0
    packed = fit // 4 + 1
    extra = round_up((REACH - TILE) * half // EDGE, TILE) // TILE * EDGE
    f32, bf16 = jnp.float32, jnp.bfloat16
    vmem = pl.BlockSpec(memory_space=pltpu.VMEM)
    anywhere = pl.BlockSpec(memory_space=pltpu.HBM)
    operands = (template, exposure[0], cosmic_mask[0], stamp_blocks, row_filters, col_filters)
    operands = [pltpu.with_memory_space_constraint(x, pltpu.HBM) for x in operands]
    diff, coef_row = pl.pallas_call(
        functools.partial(kernel, stripes, float(rows * stripes), radices, rounds),
        out_shape=(jax.ShapeDtypeStruct((tall, cols), f32), jax.ShapeDtypeStruct((1, fit), f32)),
        in_specs=[anywhere] * 6,
        out_specs=(vmem, vmem),
        scratch_shapes=[
            pltpu.VMEM((rows, half), f32),
            pltpu.VMEM((rows, cols), f32),
            pltpu.VMEM((rows, cols), jnp.int32),
            pltpu.SMEM(stamp_blocks.shape, jnp.int32),
            pltpu.VMEM((bases, taps), f32),
            pltpu.VMEM((bases, taps), f32),
            pltpu.VMEM((2, TILE, half + extra), f32),
            pltpu.VMEM((2, TILE, half + extra), f32),
            pltpu.VMEM((2, TILE, half + extra), f32),
            pltpu.VMEM((rows, half), f32),
            pltpu.VMEM((2, 2, cols), f32),
            pltpu.VMEM((2, 2, cols), f32),
            pltpu.VMEM((ext_rows, wide), f32),
            pltpu.VMEM((bases * rows, 2 * EDGE), f32),
            pltpu.VMEM((bases * tall, 2 * EDGE), f32),
            pltpu.VMEM((bases, EDGE, 2 * EDGE), bf16),
            pltpu.VMEM((bases, 2 * EDGE, 4 * EDGE), bf16),
            pltpu.VMEM((bases * rows, cols), f32),
            pltpu.VMEM((blocks, rows * pad_b, EDGE), f32),
            pltpu.VMEM((blocks, rows * TILE, EDGE), f32),
            pltpu.VMEM((blocks, rows, EDGE), f32),
            pltpu.VMEM((blocks, TILE, EDGE), f32),
            pltpu.VMEM((6, 3 * pad_b + TILE, EDGE), f32),
            pltpu.VMEM((bases * tall, wide), f32),
            pltpu.VMEM((bases, tiles * tall, EDGE), f32),
            pltpu.VMEM((fit, EDGE), f32),
            pltpu.VMEM((bases, tall + TILE, EDGE), f32),
            pltpu.VMEM((tall, cols), f32),
            pltpu.VMEM((max(1, len(radices)), packed, EDGE), f32),
            pltpu.VMEM((slots, packed, EDGE), f32),
            pltpu.SemaphoreType.DMA((6,)),
            pltpu.SemaphoreType.DMA((7,)),
            pltpu.SemaphoreType.DMA((7,)),
            pltpu.SemaphoreType.DMA((slots,)),
            pltpu.SemaphoreType.DMA((slots,)),
            pltpu.SemaphoreType.REGULAR((max(1, rounds),)),
        ],
        compiler_params=pltpu.CompilerParams(
            collective_id=0, has_side_effects=True, vmem_limit_bytes=VMEM_GRANT
        ),
        name="fused",
    )(*operands)
    filtered, coef_row = pl.pallas_call(
        finish_kernel,
        out_shape=(jax.ShapeDtypeStruct((rows, cols), f32), jax.ShapeDtypeStruct((1, fit), f32)),
        in_specs=[vmem, vmem],
        out_specs=(vmem, vmem),
        compiler_params=pltpu.CompilerParams(vmem_limit_bytes=VMEM_GRANT),
        name="finish",
    )(diff, coef_row)
    return (filtered[None], coef_row)


def solution(mesh):
    placed = (
        P(("groups", "stripe"), "exp"),
        P(("groups", "exp"), "stripe", None),
        P(("groups", "exp"), "stripe", None),
        P(("groups", "stripe"), None),
        P(),
        P(),
    )
    return jax.shard_map(
        shards,
        mesh=mesh,
        in_specs=placed,
        out_specs=(P(("groups", "exp"), "stripe", None), P(("groups", "exp"), None)),
        check_vma=False,
    )
```
